256 devices in a mesh: gx: 32 (over x, y, core), gy: 8 (over z).
Axes of the slice: x: 4, y: 4, z: 8, core: 2. Of those that a mesh axis runs over, the one named last changes fastest.
Arguments:
- factor: bfloat16 [64, 256, 128, 256], P(None, 'gx', 'gy'), may hold values from -200 to 200
- offset: int32 [1], replicated, may hold values from 0 to 32
- diagonal: float32 [256, 128, 256], P('gx', 'gy'), may hold values from 0.25 to 16
- actuators: bfloat16 [8, 256, 128, 256], P(None, 'gx', 'gy'), may hold values from -200 to 200
- sensors: bfloat16 [8, 256, 128, 256], P(None, 'gx', 'gy'), may hold values from -200 to 200
Outputs:
- rotated: bfloat16 [32, 256, 128, 256], P(None, 'gx', 'gy')
- residual_factor: bfloat16 [32, 256, 128, 256], P(None, 'gx', 'gy')
- riccati: float32 [32, 32], replicated
- gram_first: float32 [32, 32], replicated
The draws below stay inside these ranges and needn't reach their ends.
All inputs are finite; a program needn't handle non-finite values.
Results may differ from the reference program's by a relative error of at most 0.0034.
Values may be sent and summed in bfloat16 or wider, within the bound.
A program may use at most 128 MiB of HBM per device.

```python
import math
import jax
import jax.numpy as jnp
from jax import lax

WINDOW = 32
RANK = 64
ACTUATORS = 8
SENSORS = 8
CX = 8
NZ = 256
KLEIN = 3
SMITH = 4
NX = 256
NY = 128


def grid_axes():
    x_coord = (jnp.arange(NX, dtype=jnp.float32) + 0.5) / NX
    y_coord = (jnp.arange(NY, dtype=jnp.float32) + 0.5) / NY
    z_coord = (jnp.arange(NZ, dtype=jnp.float32) + 0.5) / NZ
    return (x_coord[:, None, None], y_coord[None, :, None], z_coord[None, None, :])


def ramp_field():
    x_ramp = jnp.arange(NX, dtype=jnp.float32) / max(NX - 1, 1)
    y_ramp = jnp.arange(NY, dtype=jnp.float32) / max(NY - 1, 1)
    return jnp.exp(0.5 * math.log(3.0) * (x_ramp[:, None, None] + y_ramp[None, :, None]))


def envelopes(key, how_many):
    x_coord, y_coord, z_coord = grid_axes()
    frequency = jax.random.randint(jax.random.fold_in(key, 1), (how_many, 3), 1, 4).astype(jnp.float32)
    phases = jax.random.uniform(jax.random.fold_in(key, 2), (how_many, 3), jnp.float32, 0.0, 2.0 * math.pi)
    amplitude = jax.random.uniform(jax.random.fold_in(key, 3), (how_many, 1, 1, 1), jnp.float32, 0.3, 0.6)
    waves = jnp.sin(2.0 * math.pi * frequency[:, 0, None, None, None] * x_coord[None] + phases[:, 0, None, None, None])
    waves = waves + jnp.sin(2.0 * math.pi * frequency[:, 1, None, None, None] * y_coord[None] + phases[:, 1, None, None, None])
    waves = waves + jnp.sin(2.0 * math.pi * frequency[:, 2, None, None, None] * z_coord[None] + phases[:, 2, None, None, None])
    return jnp.exp(amplitude * waves)


def rough_field(key, shape):
    return jnp.clip(jax.random.normal(key, shape, jnp.float32), -5.0, 5.0)


def shared_field(key):
    base_field = rough_field(jax.random.fold_in(key, 21), (NX, NY, NZ))
    return base_field


def detail_field(key):
    return rough_field(jax.random.fold_in(key, 22), (NX, NY, NZ))


def draw_factor(key, part):
    field_values = shared_field(key)
    detail_values = detail_field(key)
    envelope = envelopes(jax.random.fold_in(key, 31), RANK)
    detail_envelope = envelopes(jax.random.fold_in(key, 34), RANK)
    noise_field = rough_field(jax.random.fold_in(key, 32), (RANK, NX, NY, NZ))
    scales = jnp.exp(jax.random.uniform(jax.random.fold_in(key, 33), (RANK, 1, 1, 1), jnp.float32, 0.0, math.log(10.0)))
    inner_value = envelope * field_values[None] + 0.002 * detail_envelope * detail_values[None] + 0.0008 * noise_field
    factor_value = 0.2 * scales * ramp_field()[None] * inner_value
    return factor_value.astype(jnp.bfloat16)


def input_fields(key, how_many, fold_base):
    field_values = shared_field(key)
    detail_values = detail_field(key)
    envelope = envelopes(jax.random.fold_in(key, fold_base), how_many)
    detail_envelope = envelopes(jax.random.fold_in(key, fold_base + 2), how_many)
    noise_field = rough_field(jax.random.fold_in(key, fold_base + 1), (how_many, NX, NY, NZ))
    smooth_part = envelope * field_values[None] + detail_envelope * detail_values[None]
    return (ramp_field()[None] * smooth_part + 0.5 * noise_field).astype(jnp.bfloat16)


def draw_actuators(key, part):
    return input_fields(key, ACTUATORS, 41)


def draw_sensors(key, part):
    return input_fields(key, SENSORS, 51)


def shard_levels(own_key, dims, pieces, low, high):
    gain = 1.0
    for axis_at, parts in pieces:
        heights = jax.random.uniform(jax.random.fold_in(jax.random.fold_in(own_key, 6), axis_at), (parts,), jnp.float32, low / len(pieces), high / len(pieces))
        gain = gain * jnp.repeat(jnp.exp(heights), dims[axis_at] // parts).reshape((-1,) + (1,) * (len(dims) - 1 - axis_at))
    return gain


def setup_inputs(seed: int = 0) -> dict:
    arg_keys = jax.random.split(jax.random.key(seed), 6)
    return {
        "factor": draw_factor(jax.random.fold_in(arg_keys[5], 71), 0),
        "offset": jax.random.randint(arg_keys[1], (1,), 0, RANK - WINDOW + 1).astype(jnp.int32),
        "diagonal": jnp.clip(jnp.exp(math.log(16.0) - 4.158883 * jax.random.uniform(arg_keys[2], (NX, NY, NZ), jnp.float32) ** shard_levels(arg_keys[2], (NX, NY, NZ), ((0, 32), (1, 8)), -0.2, 0.2)), 0.25, 16.0),
        "actuators": draw_actuators(jax.random.fold_in(arg_keys[5], 71), 0),
        "sensors": draw_sensors(jax.random.fold_in(arg_keys[5], 71), 0),
    }


highest = lax.Precision.HIGHEST
cayley_shift = 1.0

def product(left, right):
    return jnp.dot(left.astype(jnp.float32), right.astype(jnp.float32), precision=highest, preferred_element_type=jnp.float32)

def lower_inverse(gram_matrix):
    lower_factor = jnp.linalg.cholesky(gram_matrix)
    identity = jnp.eye(gram_matrix.shape[0], dtype=jnp.float32)
    return lax.linalg.triangular_solve(lower_factor, identity, left_side=True, lower=True)

def general_inverse(matrix):
    normal_matrix = product(matrix.T, matrix)
    lower_factor = jnp.linalg.cholesky(normal_matrix)
    forward = lax.linalg.triangular_solve(lower_factor, matrix.T, left_side=True, lower=True)
    return lax.linalg.triangular_solve(lower_factor, forward, left_side=True, lower=True, transpose_a=True)

def lyapunov(closed, forcing):
    identity = jnp.eye(closed.shape[0], dtype=jnp.float32)
    inverse_shift = general_inverse(closed.T - cayley_shift * identity)
    cayley = product(inverse_shift, closed.T + cayley_shift * identity)
    accumulated = 2.0 * cayley_shift * product(product(inverse_shift, forcing), inverse_shift.T)
    for doubling in range(SMITH):
        accumulated = accumulated + product(product(cayley, accumulated), cayley.T)
        cayley = product(cayley, cayley)
    return 0.5 * (accumulated + accumulated.T)

def riccati_solve(projected, drive_part, sense_part):
    gain_matrix = product(drive_part, drive_part.T)
    weight_matrix = product(sense_part, sense_part.T)
    solution = jnp.zeros_like(projected)
    for iteration in range(KLEIN):
        closed = projected - product(gain_matrix, solution)
        forcing = weight_matrix + product(product(solution, gain_matrix), solution)
        solution = lyapunov(closed, forcing)
    return solution

def stencil(extended, coefficient):
    centre = extended[:, 1:-1, 1:-1, :]
    zero_plane = jnp.zeros(centre.shape[:-1] + (1,), centre.dtype)
    beside = extended[:, 2:, 1:-1, :] + extended[:, :-2, 1:-1, :]
    beside = beside + extended[:, 1:-1, 2:, :] + extended[:, 1:-1, :-2, :]
    beside = beside + jnp.concatenate([centre[..., 1:], zero_plane], axis=-1)
    beside = beside + jnp.concatenate([zero_plane, centre[..., :-1]], axis=-1)
    return beside - (6.0 + coefficient) * centre

def pairwise_total(gram_stack):
    while gram_stack.shape[0] > 1:
        length = gram_stack.shape[0]
        paired = length - length % 2
        summed = gram_stack[0:paired:2] + gram_stack[1:paired:2]
        gram_stack = jnp.concatenate([summed, gram_stack[paired:]], axis=0)
    return gram_stack[0]

def reference(factor, offset, diagonal, actuators, sensors):
    cell_weight = 1.0 / (NX * NY * NZ)
    window = lax.dynamic_slice_in_dim(factor, offset[0].astype(jnp.int32), WINDOW, 0)

    def row_gram(row_index):
        plane_rows = lax.dynamic_slice_in_dim(window, row_index.astype(jnp.int32), 1, 1).reshape(WINDOW, -1)
        return jnp.dot(plane_rows.astype(jnp.float32), plane_rows.T.astype(jnp.float32), preferred_element_type=jnp.float32)
    gram_stack = lax.map(row_gram, jnp.arange(NX, dtype=jnp.int32))
    gram_first = pairwise_total(gram_stack) * cell_weight
    inverse_first = lower_inverse(gram_first)
    window_pad = jnp.pad(window, ((0, 0), (1, 1), (0, 0), (0, 0)))
    blocks = jnp.arange(NX // CX, dtype=jnp.int32)

    def take_slab(block_index):
        return lax.dynamic_slice_in_dim(window_pad, (block_index * CX).astype(jnp.int32), CX + 2, 1).astype(jnp.float32)

    def gram_step(totals, block_index):
        inner = take_slab(block_index)[:, 1:-1].reshape(WINDOW, -1)
        first_rows = product(inverse_first, inner)
        return (totals + product(first_rows, first_rows.T), None)
    gram_second = lax.scan(gram_step, jnp.zeros((WINDOW, WINDOW), jnp.float32), blocks)[0] * cell_weight
    inverse_second = lower_inverse(gram_second)

    def block_fields(block_index):
        slab_rows = take_slab(block_index).reshape(WINDOW, -1)
        basis_slab = product(inverse_second, product(inverse_first, slab_rows)).reshape(WINDOW, CX + 2, NY, NZ)
        extended = jnp.pad(basis_slab, ((0, 0), (0, 0), (1, 1), (0, 0)))
        coefficient = lax.dynamic_slice_in_dim(diagonal, (block_index * CX).astype(jnp.int32), CX, 0)
        image_rows = stencil(extended, coefficient).reshape(WINDOW, -1)
        basis_rows = basis_slab[:, 1:-1].reshape(WINDOW, -1)
        return (basis_rows, image_rows)

    def project_step(totals, block_index):
        basis_rows, image_rows = block_fields(block_index)
        start_cell = (block_index * CX).astype(jnp.int32)
        drive_slab = lax.dynamic_slice_in_dim(actuators, start_cell, CX, 1).reshape(ACTUATORS, -1).astype(jnp.float32)
        sense_slab = lax.dynamic_slice_in_dim(sensors, start_cell, CX, 1).reshape(SENSORS, -1).astype(jnp.float32)
        return ((totals[0] + product(basis_rows, image_rows.T), totals[1] + product(basis_rows, drive_slab.T), totals[2] + product(basis_rows, sense_slab.T)), None)
    initial = (jnp.zeros((WINDOW, WINDOW), jnp.float32), jnp.zeros((WINDOW, ACTUATORS), jnp.float32), jnp.zeros((WINDOW, SENSORS), jnp.float32))
    totals = lax.scan(project_step, initial, blocks)[0]
    raw_projected = totals[0] * cell_weight
    projected = 0.5 * (raw_projected + raw_projected.T)
    drive_part = totals[1] * cell_weight
    sense_part = totals[2] * cell_weight
    solution = riccati_solve(projected, drive_part, sense_part)

    def output_step(block_index):
        basis_rows, image_rows = block_fields(block_index)
        rotated_rows = product(solution, basis_rows).astype(jnp.bfloat16)
        remainder = product(solution, image_rows - product(projected, basis_rows)).astype(jnp.bfloat16)
        return (rotated_rows.reshape(WINDOW, CX, NY, NZ), remainder.reshape(WINDOW, CX, NY, NZ))
    rotated_blocks, remainder_blocks = lax.map(output_step, blocks)
    rotated = jnp.transpose(rotated_blocks, (1, 0, 2, 3, 4)).reshape(WINDOW, NX, NY, NZ)
    residual_factor = jnp.transpose(remainder_blocks, (1, 0, 2, 3, 4)).reshape(WINDOW, NX, NY, NZ)
    return (rotated, residual_factor, solution, gram_first)
```

```python
import functools
import jax
import jax.numpy as jnp
from jax import lax
from jax.experimental import pallas as pl
from jax.experimental.pallas import tpu as pltpu
from jax.sharding import PartitionSpec as P

WINDOW = 32
KLEIN = 3
SMITH = 4
CONTROLS = 8
NX_LOC, NY_LOC, NZ = 8, 16, 256
CELLS = 256 * 128 * 256
MESH = pl.DeviceIdType.MESH
f32, bf16 = jnp.float32, jnp.bfloat16
HIGHEST = lax.Precision.HIGHEST


def dot(left, right, dims=((1,), (0,))):
    return lax.dot_general(left, right, (dims, ((), ())), precision=HIGHEST, preferred_element_type=f32)


def bdot(left, right, dims=((1,), (0,))):
    return lax.dot_general(left, right, (dims, ((), ())), preferred_element_type=f32)


def pieces(value, count):
    out = []
    rest = value
    for at in range(count):
        piece = rest.astype(bf16)
        out.append(piece)
        if at < count - 1:
            rest = rest - piece.astype(f32)
    return out


def peer_groups():
    gx = lax.axis_index("gx")
    z = lax.axis_index("gy")
    xy = gx // 2
    core = gx % 2
    return (
        (2, core, lambda d: (xy * 2 + (core + d) % 2, z)),
        (16, xy, lambda d: (((xy + d) % 16) * 2 + core, z)),
        (8, z, lambda d: (gx, (z + d) % 8)),
    )


def stats_kernel(w_hbm, diag_ref, as_ref, tot_ref, aw_hbm, wext, awbuf, acc, buf0, buf1, buf2,
                 in_sem, hs_sem, hr_sem, s_sem, r_sem, out_sem):
    gx = lax.axis_index("gx")
    gz = lax.axis_index("gy")
    bufs = (buf0, buf1, buf2)
    load = pltpu.make_async_copy(w_hbm, wext.at[pl.ds(1, NX_LOC), pl.ds(1, NY_LOC)], in_sem)
    load.start()
    barrier = pltpu.get_barrier_semaphore()
    right, left = ((gx + 1) % 32, gz), ((gx + 31) % 32, gz)
    up, down = (gx, (gz + 1) % 8), (gx, (gz + 7) % 8)
    count = 0
    for n, me, dev in peer_groups():
        for d in range(1, n):
            pl.semaphore_signal(barrier, inc=1, device_id=dev(d), device_id_type=MESH)
            count += 1
    for target in (right, left):
        pl.semaphore_signal(barrier, inc=1, device_id=target, device_id_type=MESH)
        count += 1
    load.wait()
    pl.semaphore_wait(barrier, count)
    inner_y = pl.ds(1, NY_LOC)
    inner_x = pl.ds(1, NX_LOC)
    moves = (
        (wext.at[NX_LOC, inner_y], wext.at[0, inner_y], right),
        (wext.at[1, inner_y], wext.at[NX_LOC + 1, inner_y], left),
        (wext.at[inner_x, NY_LOC], wext.at[inner_x, 0], up),
        (wext.at[inner_x, 1], wext.at[inner_x, NY_LOC + 1], down),
    )
    copies = []
    for at, (source, target, who) in enumerate(moves):
        copy = pltpu.make_async_remote_copy(source, target, hs_sem.at[at], hr_sem.at[at], device_id=who, device_id_type=MESH)
        copy.start()
        copies.append(copy)
    for copy in copies:
        copy.wait()

    @pl.when(gx == 0)
    def _():
        wext[0] = jnp.zeros_like(wext[0])

    @pl.when(gx == 31)
    def _():
        wext[NX_LOC + 1] = jnp.zeros_like(wext[0])

    @pl.when(gz == 0)
    def _():
        wext[:, 0] = jnp.zeros_like(wext[:, 0])

    @pl.when(gz == 7)
    def _():
        wext[:, NY_LOC + 1] = jnp.zeros_like(wext[:, 0])

    lane = lax.broadcasted_iota(jnp.int32, (WINDOW, NZ), 1)

    def line(at, total):
        x = at // NY_LOC
        y = at % NY_LOC
        w16 = wext[x + 1, y + 1]
        w = w16.astype(f32)
        beside = wext[x + 2, y + 1].astype(f32) + wext[x, y + 1].astype(f32)
        beside = beside + wext[x + 1, y + 2].astype(f32) + wext[x + 1, y].astype(f32)
        beside = beside + jnp.where(lane == NZ - 1, 0.0, pltpu.roll(w, NZ - 1, 1))
        beside = beside + jnp.where(lane == 0, 0.0, pltpu.roll(w, 1, 1))
        image = beside - (6.0 + diag_ref[x, pl.ds(y, 1), :]) * w
        parts = jnp.concatenate(pieces(image, 3), axis=0)
        awbuf[x, y] = parts
        stack = jnp.concatenate([w16, parts, as_ref[x, y]], axis=0)
        return total + bdot(stack, w16, ((1,), (1,)))

    def plane(x, total):
        return total + lax.fori_loop(0, NY_LOC, lambda y, t: line(x * NY_LOC + y, t), jnp.zeros((144, WINDOW), f32))

    total = lax.fori_loop(0, NX_LOC, plane, jnp.zeros((144, WINDOW), f32)) * (1.0 / CELLS)
    write = pltpu.make_async_copy(awbuf, aw_hbm, out_sem)
    write.start()
    gram = total[0:32]
    cross = (total[32:64] + (total[64:96] + total[96:128]))
    io = total[128:144]
    current = jnp.concatenate([
        jnp.concatenate([gram[8 * q:8 * q + 8] for q in range(4)], axis=1),
        jnp.concatenate([cross[8 * q:8 * q + 8] for q in range(4)], axis=1),
        jnp.concatenate([io[0:8], io[8:16], jnp.zeros((8, 64), f32)], axis=1),
    ], axis=0)
    for at, (n, me, dev) in enumerate(peer_groups()):
        buf = bufs[at]
        buf[me] = current
        for d in range(1, n):
            pltpu.make_async_remote_copy(buf.at[me], buf.at[me], s_sem.at[at], r_sem.at[at], device_id=dev(d), device_id_type=MESH).start()
        span = buf.at[pl.ds(0, n - 1)]
        pltpu.make_async_copy(span, span, r_sem.at[at]).wait()
        parts = [buf[j] for j in range(n)]
        while len(parts) > 1:
            parts = [parts[i] + parts[i + 1] for i in range(0, len(parts), 2)]
        current = parts[0]
    tot_ref[...] = current
    for at, (n, me, dev) in enumerate(peer_groups()):
        span = bufs[at].at[pl.ds(0, n - 1)]
        pltpu.make_async_copy(span, span, s_sem.at[at]).wait()
    write.wait()


def stats(w_t, diagonal, as_t):
    return pl.pallas_call(
        stats_kernel,
        out_shape=(jax.ShapeDtypeStruct((24, 128), f32), jax.ShapeDtypeStruct((NX_LOC, NY_LOC, 96, NZ), bf16)),
        in_specs=[pl.BlockSpec(memory_space=pl.ANY), pl.BlockSpec(memory_space=pltpu.VMEM), pl.BlockSpec(memory_space=pltpu.VMEM)],
        out_specs=(pl.BlockSpec(memory_space=pltpu.VMEM), pl.BlockSpec(memory_space=pl.ANY)),
        scratch_shapes=[
            pltpu.VMEM((NX_LOC + 2, NY_LOC + 2, WINDOW, NZ), bf16),
            pltpu.VMEM((NX_LOC, NY_LOC, 96, NZ), bf16),
            pltpu.VMEM((144, WINDOW), f32),
            pltpu.VMEM((2, 24, 128), f32), pltpu.VMEM((16, 24, 128), f32), pltpu.VMEM((8, 24, 128), f32),
            pltpu.SemaphoreType.DMA, pltpu.SemaphoreType.DMA((4,)), pltpu.SemaphoreType.DMA((4,)),
            pltpu.SemaphoreType.DMA((3,)), pltpu.SemaphoreType.DMA((3,)), pltpu.SemaphoreType.DMA,
        ],
        compiler_params=pltpu.CompilerParams(collective_id=0, has_side_effects=True, vmem_limit_bytes=40 << 20),
        name="stats_all_reduce",
    )(w_t, diagonal, as_t)


def eliminate(table, count):
    row_at = lax.broadcasted_iota(jnp.int32, table.shape, 0)
    for k in range(count):
        pivot_row = table[k:k + 1, :]
        factor = table[:, k:k + 1] * (1.0 / pivot_row[:, k:k + 1])
        table = jnp.where(row_at > k, table - factor * pivot_row, table)
    return table


def jordan(table, count):
    row_at = lax.broadcasted_iota(jnp.int32, table.shape, 0)
    for k in range(count):
        scaled = table[k:k + 1, :] * (1.0 / table[k:k + 1, k:k + 1])
        table = jnp.where(row_at == k, scaled, table - table[:, k:k + 1] * scaled)
    return table


def cholesky_rows(table):
    done = eliminate(table, WINDOW)
    row_at = lax.broadcasted_iota(jnp.int32, (WINDOW, WINDOW), 0)
    col_at = lax.broadcasted_iota(jnp.int32, (WINDOW, WINDOW), 1)
    pivots = jnp.sum(jnp.where(row_at == col_at, done[:, :WINDOW], 0.0), axis=1, keepdims=True)
    return done * (1.0 / jnp.sqrt(pivots))


def eye(n):
    return (lax.broadcasted_iota(jnp.int32, (n, n), 0) == lax.broadcasted_iota(jnp.int32, (n, n), 1)).astype(f32)


def small_algebra(totals):
    gram = jnp.concatenate([totals[0:8, 32 * q:32 * q + 32] for q in range(4)], axis=0)
    cross = jnp.concatenate([totals[8:16, 32 * q:32 * q + 32] for q in range(4)], axis=0)
    io_rows = jnp.concatenate([totals[16:24, 0:32], totals[16:24, 32:64]], axis=0)
    ident = eye(WINDOW)
    inverse_first = cholesky_rows(jnp.concatenate([gram, ident, jnp.zeros((WINDOW, 64), f32)], axis=1))[:, 32:64]
    both = dot(inverse_first, jnp.concatenate([gram, cross], axis=1))
    both = dot(jnp.concatenate([both[:, :32], both[:, 32:]], axis=0), inverse_first, ((1,), (1,)))
    gram_second, cross_first = both[:32], both[32:]
    io_first = dot(inverse_first, io_rows, ((1,), (1,)))
    second = cholesky_rows(jnp.concatenate([gram_second, ident, cross_first, io_first, jnp.zeros((WINDOW, 16), f32)], axis=1))
    inverse_second = second[:, 32:64]
    raw = dot(second[:, 64:96], inverse_second, ((1,), (1,)))
    projected = 0.5 * (raw + raw.T)
    drive = second[:, 96:104]
    sense = second[:, 104:112]
    transform = dot(inverse_second, inverse_first)
    shifted = jordan(jnp.concatenate([ident - projected, ident, jnp.zeros((WINDOW, 64), f32)], axis=1), WINDOW)
    inv_n = shifted[:, 32:64]
    inv_n_t = inv_n.T
    drive_t, sense_t = drive.T, sense.T
    hd_t = dot(drive_t, inv_n_t)
    riccati = None
    for iteration in range(KLEIN):
        if riccati is None:
            einv_t = -inv_n_t
            rows = sense_t
        else:
            q_t = dot(drive_t, riccati)
            hq_t = dot(q_t, inv_n_t)
            small = eye(CONTROLS) + dot(hd_t, q_t, ((1,), (1,)))
            small_t = small.T
            normal = dot(small_t, small)
            table = jnp.concatenate([normal, small_t, jnp.zeros((CONTROLS, 112), f32)], axis=1)
            small_inv = jordan(table, CONTROLS)[:, 8:16]
            middle = dot(small_inv, hd_t)
            einv_t = dot(middle, hq_t, ((0,), (0,))) - inv_n_t
            rows = jnp.concatenate([sense_t, q_t], axis=0)
        cayley_t = ident + 2.0 * einv_t
        chain = dot(rows, einv_t)
        for doubling in range(SMITH):
            chain = jnp.concatenate([chain, dot(chain, cayley_t)], axis=0)
            if doubling < SMITH - 1:
                cayley_t = dot(cayley_t, cayley_t)
        riccati = 2.0 * dot(chain, chain, ((0,), (0,)))
    rotate = dot(riccati, transform)
    remain = dot(dot(riccati, projected), transform)
    return rotate, remain, riccati, gram


def output_kernel(tot_ref, w_ref, aw_ref, rot_ref, res_ref, ric_ref, gram_ref, coef, tmp):
    @pl.when(pl.program_id(0) == 0)
    def _():
        rotate, remain, riccati, gram = small_algebra(tot_ref[...])
        ric_ref[...] = riccati
        gram_ref[...] = gram
        r0, r1, r2 = pieces(rotate, 3)
        m0, m1, m2 = pieces(-remain, 3)
        zero = jnp.zeros((WINDOW, 192), bf16)
        top = jnp.concatenate([r0, r1, r2, zero], axis=1)
        low = jnp.concatenate([m0, m1, m2, r0, r0, r0, r1, r1, r2], axis=1)
        coef[0:32, 0:288] = top
        coef[32:64, 0:288] = low

    def line(y, carry):
        w = w_ref[0, y]
        parts = aw_ref[0, y]
        hi, mid = parts[0:32], parts[32:64]
        data = jnp.concatenate([w, w, w, parts, hi, mid, hi], axis=0)
        tmp[y] = bdot(coef[:, 0:288], data)
        return carry

    lax.fori_loop(0, NY_LOC, line, 0)
    rot_ref[:, 0] = jnp.swapaxes(tmp[:, 0:32, :], 0, 1).astype(bf16)
    res_ref[:, 0] = jnp.swapaxes(tmp[:, 32:64, :], 0, 1).astype(bf16)


def outputs(totals, w_t, aw):
    field = (WINDOW, NX_LOC, NY_LOC, NZ)
    whole = lambda *shape: pl.BlockSpec(shape, lambda x: (0,) * len(shape))
    return pl.pallas_call(
        output_kernel,
        grid=(NX_LOC,),
        out_shape=(jax.ShapeDtypeStruct(field, bf16), jax.ShapeDtypeStruct(field, bf16),
                   jax.ShapeDtypeStruct((WINDOW, WINDOW), f32), jax.ShapeDtypeStruct((WINDOW, WINDOW), f32)),
        in_specs=[whole(24, 128),
                  pl.BlockSpec((1, NY_LOC, WINDOW, NZ), lambda x: (x, 0, 0, 0)),
                  pl.BlockSpec((1, NY_LOC, 96, NZ), lambda x: (x, 0, 0, 0))],
        out_specs=(pl.BlockSpec((WINDOW, 1, NY_LOC, NZ), lambda x: (0, x, 0, 0)),
                   pl.BlockSpec((WINDOW, 1, NY_LOC, NZ), lambda x: (0, x, 0, 0)),
                   whole(WINDOW, WINDOW), whole(WINDOW, WINDOW)),
        scratch_shapes=[pltpu.VMEM((64, 384), bf16), pltpu.VMEM((NY_LOC, 64, NZ), f32)],
        compiler_params=pltpu.CompilerParams(vmem_limit_bytes=40 << 20),
        name="algebra_outputs",
    )(totals, w_t, aw)


def local(factor, offset, diagonal, actuators, sensors):
    window = lax.dynamic_slice_in_dim(factor, offset[0], WINDOW, 0)
    w_t = jnp.transpose(window, (1, 2, 0, 3))
    as_t = jnp.transpose(jnp.concatenate([actuators, sensors], axis=0), (1, 2, 0, 3))
    totals, aw = stats(w_t, diagonal, as_t)
    rotated, residual, riccati, gram = outputs(totals, w_t, aw)
    return rotated, residual, riccati, gram


def solution(mesh):
    return jax.shard_map(
        local,
        mesh=mesh,
        in_specs=(P(None, "gx", "gy", None), P(), P("gx", "gy", None), P(None, "gx", "gy", None), P(None, "gx", "gy", None)),
        out_specs=(P(None, "gx", "gy", None), P(None, "gx", "gy", None), P(), P()),
        check_vma=False,
    )
```

```python
import functools
import jax
import jax.numpy as jnp
from jax import lax
from jax.experimental import pallas as pl
from jax.experimental.pallas import tpu as pltpu
from jax.sharding import PartitionSpec as P

WINDOW = 32
KLEIN = 3
SMITH = 4
CONTROLS = 8
NX_LOC, NY_LOC, NZ = 8, 16, 256
CELLS = 256 * 128 * 256
MESH = pl.DeviceIdType.MESH
f32, bf16 = jnp.float32, jnp.bfloat16
HIGHEST = lax.Precision.HIGHEST


def dot(left, right, dims=((1,), (0,))):
    return lax.dot_general(left, right, (dims, ((), ())), precision=HIGHEST, preferred_element_type=f32)


def bdot(left, right, dims=((1,), (0,))):
    return lax.dot_general(left, right, (dims, ((), ())), preferred_element_type=f32)


def pieces(value, count):
    out = []
    rest = value
    for at in range(count):
        piece = rest.astype(bf16)
        out.append(piece)
        if at < count - 1:
            rest = rest - piece.astype(f32)
    return out


def peer_groups():
    gx = lax.axis_index("gx")
    z = lax.axis_index("gy")
    xy = gx // 2
    core = gx % 2
    return (
        (2, core, lambda d: (xy * 2 + (core + d) % 2, z)),
        (16, xy, lambda d: (((xy + d) % 16) * 2 + core, z)),
        (8, z, lambda d: (gx, (z + d) % 8)),
    )


def tree_sum(parts):
    while len(parts) > 1:
        parts = [parts[i] + parts[i + 1] for i in range(0, len(parts) - 1, 2)] + parts[len(parts) - len(parts) % 2:]
    return parts[0]


class Reduction:
    def __init__(self, bufs, s_sem, r_sem):
        self.bufs, self.s_sem, self.r_sem = bufs, s_sem, r_sem
        self.groups = peer_groups()

    def send(self, at, value):
        n, me, dev = self.groups[at]
        buf = self.bufs[at]
        buf[me] = value
        for d in range(1, n):
            pltpu.make_async_remote_copy(buf.at[me], buf.at[me], self.s_sem.at[at], self.r_sem.at[at],
                                         device_id=dev(d), device_id_type=MESH).start()

    def receive(self, at):
        n = self.groups[at][0]
        buf = self.bufs[at]
        span = buf.at[pl.ds(0, n - 1)]
        pltpu.make_async_copy(span, span, self.r_sem.at[at]).wait()
        return tree_sum([buf[j] for j in range(n)])

    def finish(self):
        for at, (n, me, dev) in enumerate(self.groups):
            span = self.bufs[at].at[pl.ds(0, n - 1)]
            pltpu.make_async_copy(span, span, self.s_sem.at[at]).wait()


def fold(rows):
    return jnp.concatenate([rows[8 * q:8 * q + 8] for q in range(4)], axis=1)


def unfold(block):
    return jnp.concatenate([block[:, 32 * q:32 * q + 32] for q in range(4)], axis=0)


def stats_kernel(off_ref, fac_hbm, diag_ref, act_hbm, sen_hbm, small_ref, w_hbm, aw_hbm,
                 fac, io, wext, io_t, awbuf, g0, g1, g2, s0, s1, s2,
                 in_sem, hs_sem, hr_sem, gs_sem, gr_sem, ss_sem, sr_sem, out_sem):
    gx = lax.axis_index("gx")
    gz = lax.axis_index("gy")
    loads = [pltpu.make_async_copy(fac_hbm, fac, in_sem.at[0]),
             pltpu.make_async_copy(act_hbm, io.at[pl.ds(0, CONTROLS)], in_sem.at[1]),
             pltpu.make_async_copy(sen_hbm, io.at[pl.ds(CONTROLS, CONTROLS)], in_sem.at[2])]
    for load in loads:
        load.start()
    barrier = pltpu.get_barrier_semaphore()
    right, left = ((gx + 1) % 32, gz), ((gx + 31) % 32, gz)
    up, down = (gx, (gz + 1) % 8), (gx, (gz + 7) % 8)
    count = 0
    for n, me, dev in peer_groups():
        for d in range(1, n):
            pl.semaphore_signal(barrier, inc=1, device_id=dev(d), device_id_type=MESH)
            count += 1
    for target in (right, left):
        pl.semaphore_signal(barrier, inc=1, device_id=target, device_id_type=MESH)
        count += 1
    start = off_ref[0]
    loads[0].wait()

    def turn(x, total):
        plane = fac[pl.ds(start, WINDOW), x].astype(f32)
        wext[x + 1, pl.ds(1, NY_LOC)] = jnp.swapaxes(plane, 0, 1).astype(bf16)
        part = jnp.zeros((WINDOW, WINDOW), f32)
        for y in range(NY_LOC):
            rows = wext[x + 1, y + 1]
            part = part + bdot(rows, rows, ((1,), (1,)))
        return total + part

    gram_local = lax.fori_loop(0, NX_LOC, turn, jnp.zeros((WINDOW, WINDOW), f32)) * (1.0 / CELLS)
    pl.semaphore_wait(barrier, count)
    inner_y = pl.ds(1, NY_LOC)
    inner_x = pl.ds(1, NX_LOC)
    moves = (
        (wext.at[NX_LOC, inner_y], wext.at[0, inner_y], right),
        (wext.at[1, inner_y], wext.at[NX_LOC + 1, inner_y], left),
        (wext.at[inner_x, NY_LOC], wext.at[inner_x, 0], up),
        (wext.at[inner_x, 1], wext.at[inner_x, NY_LOC + 1], down),
    )
    copies = []
    for at, (source, target, who) in enumerate(moves):
        copy = pltpu.make_async_remote_copy(source, target, hs_sem.at[at], hr_sem.at[at], device_id=who, device_id_type=MESH)
        copy.start()
        copies.append(copy)
    gram_sum = Reduction((g0, g1, g2), gs_sem, gr_sem)
    cross_sum = Reduction((s0, s1, s2), ss_sem, sr_sem)
    gram_sum.send(0, fold(gram_local))
    w_write = pltpu.make_async_copy(wext.at[inner_x, inner_y], w_hbm, out_sem.at[0])
    w_write.start()
    loads[1].wait()
    loads[2].wait()

    def turn_io(x, carry):
        io_t[x] = jnp.swapaxes(io[:, x].astype(f32), 0, 1).astype(bf16)
        return carry

    lax.fori_loop(0, NX_LOC, turn_io, 0)
    gram_sum.send(1, gram_sum.receive(0))

    lane = lax.broadcasted_iota(jnp.int32, (WINDOW, NZ), 1)

    def line(x, y):
        w16 = wext[x + 1, y + 1]
        w = w16.astype(f32)
        beside = wext[x + 2, y + 1].astype(f32) + wext[x, y + 1].astype(f32)
        beside = beside + wext[x + 1, y + 2].astype(f32) + wext[x + 1, y].astype(f32)
        beside = beside + jnp.where(lane == NZ - 1, 0.0, pltpu.roll(w, NZ - 1, 1))
        beside = beside + jnp.where(lane == 0, 0.0, pltpu.roll(w, 1, 1))
        image = beside - (6.0 + diag_ref[x, y:y + 1, :]) * w
        parts = jnp.concatenate(pieces(image, 3), axis=0)
        awbuf[x, y] = parts
        return bdot(jnp.concatenate([parts, io_t[x, y]], axis=0), w16, ((1,), (1,)))

    def lines(ys):
        def body(x, total):
            part = jnp.zeros((112, WINDOW), f32)
            for y in ys:
                part = part + line(x, y)
            return total + part
        return body

    total = lax.fori_loop(1, NX_LOC - 1, lines(range(1, NY_LOC - 1)), jnp.zeros((112, WINDOW), f32))
    for copy in copies:
        copy.wait()
    w_write.wait()

    @pl.when(gx == 0)
    def _():
        wext[0] = jnp.zeros_like(wext[0])

    @pl.when(gx == 31)
    def _():
        wext[NX_LOC + 1] = jnp.zeros_like(wext[0])

    @pl.when(gz == 0)
    def _():
        wext[:, 0] = jnp.zeros_like(wext[:, 0])

    @pl.when(gz == 7)
    def _():
        wext[:, NY_LOC + 1] = jnp.zeros_like(wext[:, 0])

    def edge(step, total):
        return lines((0, NY_LOC - 1))(2 * step + 2, lines((0, NY_LOC - 1))(2 * step + 1, total))

    total = lax.fori_loop(0, (NX_LOC - 2) // 2, edge, total)
    total = lax.fori_loop(0, 2, lambda at, t: lines(range(NY_LOC))(at * (NX_LOC - 1), t), total)
    total = total * (1.0 / CELLS)
    cross = total[0:32] + (total[32:64] + total[64:96])
    io_sum = jnp.concatenate([total[96:104], total[104:112], jnp.zeros((8, 64), f32)], axis=1)
    cross_sum.send(0, jnp.concatenate([fold(cross), io_sum], axis=0))
    aw_write = pltpu.make_async_copy(awbuf, aw_hbm, out_sem.at[1])
    aw_write.start()
    gram_sum.send(2, gram_sum.receive(1))
    cross_sum.send(1, cross_sum.receive(0))
    gram = unfold(gram_sum.receive(2))
    ident = eye(WINDOW)
    table = jnp.concatenate([gram, ident, jnp.zeros((WINDOW, 64), f32)], axis=1)
    table = eliminate(table, 0, 16)
    cross_sum.send(2, cross_sum.receive(1))
    inverse_first = unit_pivots(eliminate(table, 16, WINDOW))[:, 32:64]
    gram_second = dot(dot(inverse_first, gram), inverse_first, ((1,), (1,)))
    table = jnp.concatenate([gram_second, ident, jnp.zeros((WINDOW, 64), f32)], axis=1)
    inverse_second = unit_pivots(eliminate(table, 0, WINDOW))[:, 32:64]
    transform = dot(inverse_second, inverse_first)
    received = cross_sum.receive(2)
    cross = unfold(received[0:8])
    io_rows = jnp.concatenate([received[8:16, 0:32], received[8:16, 32:64]], axis=0)
    raw = dot(dot(transform, cross), transform, ((1,), (1,)))
    io_basis = dot(transform, io_rows, ((1,), (1,)))
    small_ref[0:32] = jnp.concatenate([raw, transform, io_basis, jnp.zeros((WINDOW, 48), f32)], axis=1)
    small_ref[32:64] = jnp.concatenate([gram, jnp.zeros((WINDOW, 96), f32)], axis=1)
    gram_sum.finish()
    cross_sum.finish()
    aw_write.wait()


def stats(offset, factor, diagonal, actuators, sensors):
    vmem, anywhere = pl.BlockSpec(memory_space=pltpu.VMEM), pl.BlockSpec(memory_space=pl.ANY)
    dma = pltpu.SemaphoreType.DMA
    return pl.pallas_call(
        stats_kernel,
        out_shape=(jax.ShapeDtypeStruct((64, 128), f32),
                   jax.ShapeDtypeStruct((NX_LOC, NY_LOC, WINDOW, NZ), bf16),
                   jax.ShapeDtypeStruct((NX_LOC, NY_LOC, 96, NZ), bf16)),
        in_specs=[pl.BlockSpec(memory_space=pltpu.SMEM), anywhere, vmem, anywhere, anywhere],
        out_specs=(vmem, anywhere, anywhere),
        scratch_shapes=[
            pltpu.VMEM((64, NX_LOC, NY_LOC, NZ), bf16),
            pltpu.VMEM((2 * CONTROLS, NX_LOC, NY_LOC, NZ), bf16),
            pltpu.VMEM((NX_LOC + 2, NY_LOC + 2, WINDOW, NZ), bf16),
            pltpu.VMEM((NX_LOC, NY_LOC, 2 * CONTROLS, NZ), bf16),
            pltpu.VMEM((NX_LOC, NY_LOC, 96, NZ), bf16),
            pltpu.VMEM((2, 8, 128), f32), pltpu.VMEM((16, 8, 128), f32), pltpu.VMEM((8, 8, 128), f32),
            pltpu.VMEM((2, 16, 128), f32), pltpu.VMEM((16, 16, 128), f32), pltpu.VMEM((8, 16, 128), f32),
            dma((3,)), dma((4,)), dma((4,)), dma((3,)), dma((3,)), dma((3,)), dma((3,)), dma((2,)),
        ],
        compiler_params=pltpu.CompilerParams(collective_id=0, has_side_effects=True, vmem_limit_bytes=40 << 20),
        name="stats_all_reduce",
    )(offset, factor, diagonal, actuators, sensors)


def eliminate(table, first, last):
    row_at = lax.broadcasted_iota(jnp.int32, table.shape, 0)
    for k in range(first, last):
        pivot_row = table[k:k + 1, :]
        factor = table[:, k:k + 1] * (1.0 / pivot_row[:, k:k + 1])
        table = jnp.where(row_at > k, table - factor * pivot_row, table)
    return table


def jordan(table, count):
    row_at = lax.broadcasted_iota(jnp.int32, table.shape, 0)
    for k in range(count):
        scaled = table[k:k + 1, :] * (1.0 / table[k:k + 1, k:k + 1])
        table = jnp.where(row_at == k, scaled, table - table[:, k:k + 1] * scaled)
    return table


def unit_pivots(done):
    row_at = lax.broadcasted_iota(jnp.int32, (WINDOW, WINDOW), 0)
    col_at = lax.broadcasted_iota(jnp.int32, (WINDOW, WINDOW), 1)
    pivots = jnp.sum(jnp.where(row_at == col_at, done[:, :WINDOW], 0.0), axis=1, keepdims=True)
    return done * (1.0 / jnp.sqrt(pivots))


def eye(n):
    return (lax.broadcasted_iota(jnp.int32, (n, n), 0) == lax.broadcasted_iota(jnp.int32, (n, n), 1)).astype(f32)


def small_algebra(small):
    ident = eye(WINDOW)
    raw = small[0:32, 0:32]
    transform = small[0:32, 32:64]
    projected = 0.5 * (raw + raw.T)
    drive = small[0:32, 64:72]
    sense = small[0:32, 72:80]
    gram = small[32:64, 0:32]
    shifted = jordan(jnp.concatenate([ident - projected, ident, jnp.zeros((WINDOW, 64), f32)], axis=1), WINDOW)
    inv_n = shifted[:, 32:64]
    inv_n_t = inv_n.T
    drive_t, sense_t = drive.T, sense.T
    hd_t = dot(drive_t, inv_n_t)
    riccati = None
    for iteration in range(KLEIN):
        if riccati is None:
            einv_t = -inv_n_t
            rows = sense_t
        else:
            q_t = dot(drive_t, riccati)
            hq_t = dot(q_t, inv_n_t)
            small = eye(CONTROLS) + dot(hd_t, q_t, ((1,), (1,)))
            small_t = small.T
            normal = dot(small_t, small)
            table = jnp.concatenate([normal, small_t, jnp.zeros((CONTROLS, 112), f32)], axis=1)
            small_inv = jordan(table, CONTROLS)[:, 8:16]
            middle = dot(small_inv, hd_t)
            einv_t = dot(middle, hq_t, ((0,), (0,))) - inv_n_t
            rows = jnp.concatenate([sense_t, q_t], axis=0)
        cayley_t = ident + 2.0 * einv_t
        chain = dot(rows, einv_t)
        for doubling in range(SMITH):
            chain = jnp.concatenate([chain, dot(chain, cayley_t)], axis=0)
            if doubling < SMITH - 1:
                cayley_t = dot(cayley_t, cayley_t)
        riccati = 2.0 * dot(chain, chain, ((0,), (0,)))
    rotate = dot(riccati, transform)
    remain = dot(dot(riccati, projected), transform)
    return rotate, remain, riccati, gram


def output_kernel(tot_ref, w_ref, aw_ref, rot_ref, res_ref, ric_ref, gram_ref, coef, tmp):
    @pl.when(pl.program_id(0) == 0)
    def _():
        rotate, remain, riccati, gram = small_algebra(tot_ref[...])
        ric_ref[...] = riccati
        gram_ref[...] = gram
        r0, r1, r2 = pieces(rotate, 3)
        m0, m1, m2 = pieces(-remain, 3)
        zero = jnp.zeros((WINDOW, WINDOW), bf16)
        cat = lambda *blocks: jnp.concatenate(blocks, axis=1)
        coef[...] = jnp.concatenate([
            cat(r0, zero, zero, zero), cat(m0, r0, r0, r0),
            cat(r1, zero, zero, zero), cat(m1, r1, r1, zero),
            cat(r2, zero, zero, zero), cat(m2, r2, zero, zero)], axis=0)

    for y in range(NY_LOC):
        data = jnp.concatenate([w_ref[0, y], aw_ref[0, y]], axis=0)
        out = bdot(coef[...], data)
        tmp[y] = out[0:64] + (out[64:128] + out[128:192])
    rot_ref[:, 0] = jnp.swapaxes(tmp[:, 0:32, :], 0, 1).astype(bf16)
    res_ref[:, 0] = jnp.swapaxes(tmp[:, 32:64, :], 0, 1).astype(bf16)


def outputs(totals, w_t, aw):
    field = (WINDOW, NX_LOC, NY_LOC, NZ)
    whole = lambda *shape: pl.BlockSpec(shape, lambda x: (0,) * len(shape))
    return pl.pallas_call(
        output_kernel,
        grid=(NX_LOC,),
        out_shape=(jax.ShapeDtypeStruct(field, bf16), jax.ShapeDtypeStruct(field, bf16),
                   jax.ShapeDtypeStruct((WINDOW, WINDOW), f32), jax.ShapeDtypeStruct((WINDOW, WINDOW), f32)),
        in_specs=[whole(64, 128),
                  pl.BlockSpec((1, NY_LOC, WINDOW, NZ), lambda x: (x, 0, 0, 0)),
                  pl.BlockSpec((1, NY_LOC, 96, NZ), lambda x: (x, 0, 0, 0))],
        out_specs=(pl.BlockSpec((WINDOW, 1, NY_LOC, NZ), lambda x: (0, x, 0, 0)),
                   pl.BlockSpec((WINDOW, 1, NY_LOC, NZ), lambda x: (0, x, 0, 0)),
                   whole(WINDOW, WINDOW), whole(WINDOW, WINDOW)),
        scratch_shapes=[pltpu.VMEM((192, 128), bf16), pltpu.VMEM((NY_LOC, 64, NZ), f32)],
        compiler_params=pltpu.CompilerParams(vmem_limit_bytes=40 << 20),
        name="algebra_outputs",
    )(totals, w_t, aw)


def local(factor, offset, diagonal, actuators, sensors):
    small, w_t, aw = stats(offset, factor, diagonal, actuators, sensors)
    return outputs(small, w_t, aw)


def solution(mesh):
    return jax.shard_map(
        local,
        mesh=mesh,
        in_specs=(P(None, "gx", "gy", None), P(), P("gx", "gy", None), P(None, "gx", "gy", None), P(None, "gx", "gy", None)),
        out_specs=(P(None, "gx", "gy", None), P(None, "gx", "gy", None), P(), P()),
        check_vma=False,
    )
```

```python
import functools
import jax
import jax.numpy as jnp
from jax import lax
from jax.experimental import pallas as pl
from jax.experimental.pallas import tpu as pltpu
from jax.sharding import PartitionSpec as P

WINDOW = 32
KLEIN = 3
SMITH = 4
CONTROLS = 8
NX_LOC, NY_LOC, NZ = 8, 16, 256
CELLS = 256 * 128 * 256
MESH = pl.DeviceIdType.MESH
f32, bf16 = jnp.float32, jnp.bfloat16
HIGHEST = lax.Precision.HIGHEST


def dot(left, right, dims=((1,), (0,))):
    return lax.dot_general(left, right, (dims, ((), ())), precision=HIGHEST, preferred_element_type=f32)


def bdot(left, right, dims=((1,), (0,))):
    return lax.dot_general(left, right, (dims, ((), ())), preferred_element_type=f32)


def dot3(left, right, dims=((1,), (0,))):
    left_hi, left_lo = pieces(left, 2)
    right_hi, right_lo = pieces(right, 2)
    return bdot(left_hi, right_hi, dims) + (bdot(left_hi, right_lo, dims) + bdot(left_lo, right_hi, dims))


def pieces(value, count):
    out = []
    rest = value
    for at in range(count):
        piece = rest.astype(bf16)
        out.append(piece)
        if at < count - 1:
            rest = rest - piece.astype(f32)
    return out


def peer_groups():
    gx = lax.axis_index("gx")
    z = lax.axis_index("gy")
    xy = gx // 2
    core = gx % 2
    return (
        (2, core, lambda d: (xy * 2 + (core + d) % 2, z)),
        (16, xy, lambda d: (((xy + d) % 16) * 2 + core, z)),
        (8, z, lambda d: (gx, (z + d) % 8)),
    )


def tree_sum(parts):
    while len(parts) > 1:
        parts = [parts[i] + parts[i + 1] for i in range(0, len(parts) - 1, 2)] + parts[len(parts) - len(parts) % 2:]
    return parts[0]


class Reduction:
    def __init__(self, bufs, s_sem, r_sem):
        self.bufs, self.s_sem, self.r_sem = bufs, s_sem, r_sem
        self.groups = peer_groups()

    def send(self, at, value):
        n, me, dev = self.groups[at]
        buf = self.bufs[at]
        buf[me] = value
        for d in range(1, n):
            pltpu.make_async_remote_copy(buf.at[me], buf.at[me], self.s_sem.at[at], self.r_sem.at[at],
                                         device_id=dev(d), device_id_type=MESH).start()

    def receive(self, at):
        n = self.groups[at][0]
        buf = self.bufs[at]
        span = buf.at[pl.ds(0, n - 1)]
        pltpu.make_async_copy(span, span, self.r_sem.at[at]).wait()
        return tree_sum([buf[j] for j in range(n)])

    def finish(self):
        for at, (n, me, dev) in enumerate(self.groups):
            span = self.bufs[at].at[pl.ds(0, n - 1)]
            pltpu.make_async_copy(span, span, self.s_sem.at[at]).wait()


def fold(rows):
    return jnp.concatenate([rows[8 * q:8 * q + 8] for q in range(4)], axis=1)


def unfold(block):
    return jnp.concatenate([block[:, 32 * q:32 * q + 32] for q in range(4)], axis=0)


def stats_kernel(off_ref, fac_hbm, diag_hbm, act_hbm, sen_hbm, small_ref, w_hbm, aw_hbm,
                 fac, diag_ref, io, wext, io_t, awbuf, g0, g1, g2, s0, s1, s2,
                 in_sem, hs_sem, hr_sem, gs_sem, gr_sem, ss_sem, sr_sem, out_sem):
    gx = lax.axis_index("gx")
    gz = lax.axis_index("gy")
    loads = [pltpu.make_async_copy(fac_hbm, fac, in_sem.at[0]),
             pltpu.make_async_copy(act_hbm, io.at[pl.ds(0, CONTROLS)], in_sem.at[1]),
             pltpu.make_async_copy(sen_hbm, io.at[pl.ds(CONTROLS, CONTROLS)], in_sem.at[2]),
             pltpu.make_async_copy(diag_hbm, diag_ref, in_sem.at[3])]
    for load in loads:
        load.start()
    barrier = pltpu.get_barrier_semaphore()
    right, left = ((gx + 1) % 32, gz), ((gx + 31) % 32, gz)
    up, down = (gx, (gz + 1) % 8), (gx, (gz + 7) % 8)
    count = 0
    for n, me, dev in peer_groups():
        for d in range(1, n):
            pl.semaphore_signal(barrier, inc=1, device_id=dev(d), device_id_type=MESH)
            count += 1
    for target in (right, left):
        pl.semaphore_signal(barrier, inc=1, device_id=target, device_id_type=MESH)
        count += 1
    start = off_ref[0]
    loads[0].wait()

    def turn(x, carry):
        plane = fac[pl.ds(start, WINDOW), x].astype(f32)
        wext[x + 1, pl.ds(1, NY_LOC)] = jnp.swapaxes(plane, 0, 1).astype(bf16)
        return carry

    lax.fori_loop(0, NX_LOC, turn, 0)
    pl.semaphore_wait(barrier, count)
    inner_y = pl.ds(1, NY_LOC)
    inner_x = pl.ds(1, NX_LOC)
    moves = (
        (wext.at[NX_LOC, inner_y], wext.at[0, inner_y], right),
        (wext.at[1, inner_y], wext.at[NX_LOC + 1, inner_y], left),
        (wext.at[inner_x, NY_LOC], wext.at[inner_x, 0], up),
        (wext.at[inner_x, 1], wext.at[inner_x, NY_LOC + 1], down),
    )
    copies = []
    for at, (source, target, who) in enumerate(moves):
        copy = pltpu.make_async_remote_copy(source, target, hs_sem.at[at], hr_sem.at[at], device_id=who, device_id_type=MESH)
        copy.start()
        copies.append(copy)

    def gram_plane(x, total):
        part = jnp.zeros((WINDOW, WINDOW), f32)
        for y in range(NY_LOC):
            rows = wext[x + 1, y + 1]
            part = part + bdot(rows, rows, ((1,), (1,)))
        return total + part

    gram_local = lax.fori_loop(0, NX_LOC, gram_plane, jnp.zeros((WINDOW, WINDOW), f32)) * (1.0 / CELLS)
    gram_sum = Reduction((g0, g1, g2), gs_sem, gr_sem)
    cross_sum = Reduction((s0, s1, s2), ss_sem, sr_sem)
    gram_sum.send(0, fold(gram_local))
    w_write = pltpu.make_async_copy(wext.at[inner_x, inner_y], w_hbm, out_sem.at[0])
    w_write.start()
    for load in loads[1:]:
        load.wait()

    def turn_io(x, carry):
        io_t[x] = jnp.swapaxes(io[:, x].astype(f32), 0, 1).astype(bf16)
        return carry

    lax.fori_loop(0, NX_LOC, turn_io, 0)
    gram_sum.send(1, gram_sum.receive(0))

    lane = lax.broadcasted_iota(jnp.int32, (WINDOW, NZ), 1)

    def line(x, y):
        w16 = wext[x + 1, y + 1]
        w = w16.astype(f32)
        beside = wext[x + 2, y + 1].astype(f32) + wext[x, y + 1].astype(f32)
        beside = beside + wext[x + 1, y + 2].astype(f32) + wext[x + 1, y].astype(f32)
        beside = beside + jnp.where(lane == NZ - 1, 0.0, pltpu.roll(w, NZ - 1, 1))
        beside = beside + jnp.where(lane == 0, 0.0, pltpu.roll(w, 1, 1))
        image = beside - (6.0 + diag_ref[x, y:y + 1, :]) * w
        parts = jnp.concatenate(pieces(image, 3), axis=0)
        awbuf[x, y] = parts
        return bdot(jnp.concatenate([parts, io_t[x, y]], axis=0), w16, ((1,), (1,)))

    def lines(ys):
        def body(x, total):
            part = jnp.zeros((112, WINDOW), f32)
            for y in ys:
                part = part + line(x, y)
            return total + part
        return body

    total = lax.fori_loop(1, NX_LOC - 1, lines(range(1, NY_LOC - 1)), jnp.zeros((112, WINDOW), f32))
    for copy in copies:
        copy.wait()
    w_write.wait()

    @pl.when(gx == 0)
    def _():
        wext[0] = jnp.zeros_like(wext[0])

    @pl.when(gx == 31)
    def _():
        wext[NX_LOC + 1] = jnp.zeros_like(wext[0])

    @pl.when(gz == 0)
    def _():
        wext[:, 0] = jnp.zeros_like(wext[:, 0])

    @pl.when(gz == 7)
    def _():
        wext[:, NY_LOC + 1] = jnp.zeros_like(wext[:, 0])

    def edge(step, total):
        return lines((0, NY_LOC - 1))(2 * step + 2, lines((0, NY_LOC - 1))(2 * step + 1, total))

    total = lax.fori_loop(0, (NX_LOC - 2) // 2, edge, total)
    total = lax.fori_loop(0, 2, lambda at, t: lines(range(NY_LOC))(at * (NX_LOC - 1), t), total)
    total = total * (1.0 / CELLS)
    cross = total[0:32] + (total[32:64] + total[64:96])
    io_sum = jnp.concatenate([total[96:104], total[104:112], jnp.zeros((8, 64), f32)], axis=1)
    cross_sum.send(0, jnp.concatenate([fold(cross), io_sum], axis=0))
    aw_write = pltpu.make_async_copy(awbuf, aw_hbm, out_sem.at[1])
    aw_write.start()
    gram_sum.send(2, gram_sum.receive(1))
    cross_sum.send(1, cross_sum.receive(0))
    cross_sum.send(2, cross_sum.receive(1))
    gram = unfold(gram_sum.receive(2))
    ident = eye(WINDOW)
    table = jnp.concatenate([gram, ident, jnp.zeros((WINDOW, 64), f32)], axis=1)
    inverse_first = unit_pivots(sweep(table, WINDOW, False))[:, 32:64]
    gram_second = dot(dot(inverse_first, gram), inverse_first, ((1,), (1,)))
    table = jnp.concatenate([gram_second, ident, jnp.zeros((WINDOW, 64), f32)], axis=1)
    inverse_second = unit_pivots(sweep(table, WINDOW, False))[:, 32:64]
    transform = dot(inverse_second, inverse_first)
    received = cross_sum.receive(2)
    cross = unfold(received[0:8])
    io_rows = jnp.concatenate([received[8:16, 0:32], received[8:16, 32:64]], axis=0)
    raw = dot(dot(transform, cross), transform, ((1,), (1,)))
    io_basis = dot(transform, io_rows, ((1,), (1,)))
    small_ref[0:32] = jnp.concatenate([raw, transform, io_basis, jnp.zeros((WINDOW, 48), f32)], axis=1)
    small_ref[32:64] = jnp.concatenate([gram, jnp.zeros((WINDOW, 96), f32)], axis=1)
    gram_sum.finish()
    cross_sum.finish()
    aw_write.wait()


def stats(offset, factor, diagonal, actuators, sensors):
    vmem, anywhere = pl.BlockSpec(memory_space=pltpu.VMEM), pl.BlockSpec(memory_space=pltpu.HBM)
    dma = pltpu.SemaphoreType.DMA
    return pl.pallas_call(
        stats_kernel,
        out_shape=(jax.ShapeDtypeStruct((64, 128), f32),
                   jax.ShapeDtypeStruct((NX_LOC, NY_LOC, WINDOW, NZ), bf16),
                   jax.ShapeDtypeStruct((NX_LOC, NY_LOC, 96, NZ), bf16)),
        in_specs=[pl.BlockSpec(memory_space=pltpu.SMEM), anywhere, anywhere, anywhere, anywhere],
        out_specs=(vmem, anywhere, anywhere),
        scratch_shapes=[
            pltpu.VMEM((64, NX_LOC, NY_LOC, NZ), bf16),
            pltpu.VMEM((NX_LOC, NY_LOC, NZ), f32),
            pltpu.VMEM((2 * CONTROLS, NX_LOC, NY_LOC, NZ), bf16),
            pltpu.VMEM((NX_LOC + 2, NY_LOC + 2, WINDOW, NZ), bf16),
            pltpu.VMEM((NX_LOC, NY_LOC, 2 * CONTROLS, NZ), bf16),
            pltpu.VMEM((NX_LOC, NY_LOC, 96, NZ), bf16),
            pltpu.VMEM((2, 8, 128), f32), pltpu.VMEM((16, 8, 128), f32), pltpu.VMEM((8, 8, 128), f32),
            pltpu.VMEM((2, 16, 128), f32), pltpu.VMEM((16, 16, 128), f32), pltpu.VMEM((8, 16, 128), f32),
            dma((4,)), dma((4,)), dma((4,)), dma((3,)), dma((3,)), dma((3,)), dma((3,)), dma((2,)),
        ],
        compiler_params=pltpu.CompilerParams(collective_id=0, has_side_effects=True, vmem_limit_bytes=60 << 20),
        name="stats_all_reduce",
    )(offset, factor, diagonal, actuators, sensors)


def sweep(table, count, upward):
    row_at = lax.broadcasted_iota(jnp.int32, table.shape, 0)
    for start in range(0, count, 8):
        columns = [jnp.broadcast_to(table[:, k:k + 1], table.shape) for k in range(start, start + 8)]
        for at in range(0, 8, 2):
            k = start + at
            col0, col1 = columns[at], columns[at + 1]
            a, b, c, d = col0[k:k + 1], col1[k:k + 1], col0[k + 1:k + 2], col1[k + 1:k + 2]
            inverse = 1.0 / (a * d - b * c)

            def step(value):
                row0, row1 = value[k:k + 1], value[k + 1:k + 2]
                scaled0 = (row0 * d - row1 * b) * inverse
                scaled1 = (row1 * a - row0 * c) * inverse
                other = value - (col0 * scaled0 + col1 * scaled1)
                if upward:
                    return jnp.where(row_at == k, scaled0, jnp.where(row_at == k + 1, scaled1, other))
                inner = row1 - row0 * (c / a)
                return jnp.where(row_at > k + 1, other, jnp.where(row_at == k + 1, inner, value))

            table = step(table)
            for later in range(at + 2, 8):
                columns[later] = step(columns[later])
    return table


def unit_pivots(done):
    row_at = lax.broadcasted_iota(jnp.int32, (WINDOW, WINDOW), 0)
    col_at = lax.broadcasted_iota(jnp.int32, (WINDOW, WINDOW), 1)
    pivots = jnp.sum(jnp.where(row_at == col_at, done[:, :WINDOW], 0.0), axis=1, keepdims=True)
    return done * (1.0 / jnp.sqrt(pivots))


def eye(n):
    return (lax.broadcasted_iota(jnp.int32, (n, n), 0) == lax.broadcasted_iota(jnp.int32, (n, n), 1)).astype(f32)


def small_algebra(small):
    ident = eye(WINDOW)
    raw = small[0:32, 0:32]
    transform = small[0:32, 32:64]
    projected = 0.5 * (raw + raw.T)
    drive = small[0:32, 64:72]
    sense = small[0:32, 72:80]
    gram = small[32:64, 0:32]
    shifted = sweep(jnp.concatenate([ident - projected, ident, jnp.zeros((WINDOW, 64), f32)], axis=1), WINDOW, True)
    inv_n = shifted[:, 32:64]
    drive_t, sense_t = drive.T, sense.T
    hd = dot3(inv_n, drive)
    hd_t = hd.T
    chain = None
    for iteration in range(KLEIN):
        if chain is None:
            einv_t = -inv_n
            rows = sense_t
        else:
            q_t = 2.0 * dot3(dot3(drive_t, chain, ((1,), (1,))), chain)
            hq_t = dot3(q_t, inv_n)
            small = eye(CONTROLS) + dot3(hd_t, q_t, ((1,), (1,)))
            normal = dot3(small, small, ((1,), (1,)))
            table = jnp.concatenate([normal, dot3(small, hq_t), jnp.zeros((CONTROLS, 88), f32)], axis=1)
            solved = sweep(table, CONTROLS, True)[:, CONTROLS:CONTROLS + WINDOW]
            einv_t = dot3(hd, solved) - inv_n
            rows = jnp.concatenate([sense_t, q_t], axis=0)
        cayley_t = ident + 2.0 * einv_t
        chain = dot3(rows, einv_t)
        for doubling in range(SMITH):
            chain = jnp.concatenate([chain, dot3(chain, cayley_t)], axis=0)
            if doubling < SMITH - 1:
                cayley_t = dot3(cayley_t, cayley_t)
    riccati = 2.0 * dot3(chain, chain, ((0,), (0,)))
    rotate = dot(riccati, transform)
    remain = dot(dot(riccati, projected), transform)
    return rotate, remain, riccati, gram


def output_kernel(small_ref, w_hbm, aw_hbm, rot_hbm, res_hbm, ric_ref, gram_ref,
                  wbuf, awbuf, rot, res, coef, tmp, in_sem, out_sem):
    loads = [pltpu.make_async_copy(w_hbm, wbuf, in_sem.at[0]), pltpu.make_async_copy(aw_hbm, awbuf, in_sem.at[1])]
    for load in loads:
        load.start()
    rotate, remain, riccati, gram = small_algebra(small_ref[...])
    ric_ref[...] = riccati
    gram_ref[...] = gram
    r0, r1, r2 = pieces(rotate, 3)
    m0, m1, m2 = pieces(-remain, 3)
    zero = jnp.zeros((WINDOW, WINDOW), bf16)
    cat = lambda *blocks: jnp.concatenate(blocks, axis=1)
    coef[...] = jnp.concatenate([
        cat(r0, zero, zero, zero), cat(m0, r0, r0, r0),
        cat(r1, zero, zero, zero), cat(m1, r1, r1, zero),
        cat(r2, zero, zero, zero), cat(m2, r2, zero, zero)], axis=0)
    for load in loads:
        load.wait()

    def plane(x, carry):
        for y in range(NY_LOC):
            data = jnp.concatenate([wbuf[x, y], awbuf[x, y]], axis=0)
            out = bdot(coef[...], data)
            tmp[y] = out[0:64] + (out[64:128] + out[128:192])
        rot[x] = jnp.swapaxes(tmp[:, 0:32, :], 0, 1).astype(bf16)
        res[x] = jnp.swapaxes(tmp[:, 32:64, :], 0, 1).astype(bf16)
        pltpu.make_async_copy(rot.at[x], rot_hbm.at[:, x], out_sem.at[0]).start()
        pltpu.make_async_copy(res.at[x], res_hbm.at[:, x], out_sem.at[1]).start()
        return carry

    lax.fori_loop(0, NX_LOC, plane, 0)
    pltpu.make_async_copy(rot, rot, out_sem.at[0]).wait()
    pltpu.make_async_copy(res, res, out_sem.at[1]).wait()


def outputs(small, w_t, aw):
    field = (WINDOW, NX_LOC, NY_LOC, NZ)
    vmem, hbm = pl.BlockSpec(memory_space=pltpu.VMEM), pl.BlockSpec(memory_space=pltpu.HBM)
    return pl.pallas_call(
        output_kernel,
        out_shape=(jax.ShapeDtypeStruct(field, bf16), jax.ShapeDtypeStruct(field, bf16),
                   jax.ShapeDtypeStruct((WINDOW, WINDOW), f32), jax.ShapeDtypeStruct((WINDOW, WINDOW), f32)),
        in_specs=[vmem, hbm, hbm],
        out_specs=(hbm, hbm, vmem, vmem),
        scratch_shapes=[
            pltpu.VMEM((NX_LOC, NY_LOC, WINDOW, NZ), bf16), pltpu.VMEM((NX_LOC, NY_LOC, 96, NZ), bf16),
            pltpu.VMEM((NX_LOC, WINDOW, NY_LOC, NZ), bf16), pltpu.VMEM((NX_LOC, WINDOW, NY_LOC, NZ), bf16),
            pltpu.VMEM((192, 128), bf16), pltpu.VMEM((NY_LOC, 64, NZ), f32),
            pltpu.SemaphoreType.DMA((2,)), pltpu.SemaphoreType.DMA((2,)),
        ],
        compiler_params=pltpu.CompilerParams(vmem_limit_bytes=60 << 20),
        name="algebra_outputs",
    )(small, w_t, aw)


def local(factor, offset, diagonal, actuators, sensors):
    small, w_t, aw = stats(offset, factor, diagonal, actuators, sensors)
    return outputs(small, w_t, aw)


def solution(mesh):
    return jax.shard_map(
        local,
        mesh=mesh,
        in_specs=(P(None, "gx", "gy", None), P(), P("gx", "gy", None), P(None, "gx", "gy", None), P(None, "gx", "gy", None)),
        out_specs=(P(None, "gx", "gy", None), P(None, "gx", "gy", None), P(), P()),
        check_vma=False,
    )
```

```python
import functools
import jax
import jax.numpy as jnp
from jax import lax
from jax.experimental import pallas as pl
from jax.experimental.pallas import tpu as pltpu
from jax.sharding import PartitionSpec as P

WINDOW = 32
KLEIN = 3
SMITH = 4
CONTROLS = 8
NX_LOC, NY_LOC, NZ = 8, 16, 256
CELLS = 256 * 128 * 256
MESH = pl.DeviceIdType.MESH
f32, bf16 = jnp.float32, jnp.bfloat16
HIGHEST = lax.Precision.HIGHEST


def dot(left, right, dims=((1,), (0,))):
    return lax.dot_general(left, right, (dims, ((), ())), precision=HIGHEST, preferred_element_type=f32)


def bdot(left, right, dims=((1,), (0,))):
    return lax.dot_general(left, right, (dims, ((), ())), preferred_element_type=f32)


def dot3(left, right, dims=((1,), (0,))):
    left_hi, left_lo = pieces(left, 2)
    right_hi, right_lo = pieces(right, 2)
    return bdot(left_hi, right_hi, dims) + (bdot(left_hi, right_lo, dims) + bdot(left_lo, right_hi, dims))


def pieces(value, count):
    out = []
    rest = value
    for at in range(count):
        piece = rest.astype(bf16)
        out.append(piece)
        if at < count - 1:
            rest = rest - piece.astype(f32)
    return out


def peer_groups():
    gx = lax.axis_index("gx")
    z = lax.axis_index("gy")
    xy = gx // 2
    core = gx % 2
    x, y = xy // 4, xy % 4
    plane = sorted(((dx, dy) for dx in range(4) for dy in range(4) if dx or dy),
                   key=lambda d: -(min(d[0], 4 - d[0]) + min(d[1], 4 - d[1])))
    return (
        (2, core, [(xy * 2 + (core + 1) % 2, z)]),
        (16, xy, [((((x + dx) % 4) * 4 + (y + dy) % 4) * 2 + core, z) for dx, dy in plane]),
        (8, z, [(gx, (z + dz) % 8) for dz in (4, 3, 5, 2, 6, 1, 7)]),
    )


def tree_sum(parts):
    while len(parts) > 1:
        parts = [parts[i] + parts[i + 1] for i in range(0, len(parts) - 1, 2)] + parts[len(parts) - len(parts) % 2:]
    return parts[0]


class Reduction:
    def __init__(self, bufs, s_sem, r_sem):
        self.bufs, self.s_sem, self.r_sem = bufs, s_sem, r_sem
        self.groups = peer_groups()

    def send(self, at, value):
        n, me, peers = self.groups[at]
        buf = self.bufs[at]
        buf[me] = value
        for peer in peers:
            pltpu.make_async_remote_copy(buf.at[me], buf.at[me], self.s_sem.at[at], self.r_sem.at[at],
                                         device_id=peer, device_id_type=MESH).start()

    def receive(self, at):
        n = self.groups[at][0]
        buf = self.bufs[at]
        span = buf.at[pl.ds(0, n - 1)]
        pltpu.make_async_copy(span, span, self.r_sem.at[at]).wait()
        return tree_sum([buf[j] for j in range(n)])

    def finish(self):
        for at, (n, me, peers) in enumerate(self.groups):
            span = self.bufs[at].at[pl.ds(0, n - 1)]
            pltpu.make_async_copy(span, span, self.s_sem.at[at]).wait()


def fold(rows):
    return jnp.concatenate([rows[8 * q:8 * q + 8] for q in range(4)], axis=1)


def unfold(block):
    return jnp.concatenate([block[:, 32 * q:32 * q + 32] for q in range(4)], axis=0)


def stats_kernel(off_ref, fac_hbm, diag_hbm, act_hbm, sen_hbm, small_ref, w_hbm, aw_hbm,
                 fac_ends, fac_mid, diag_ref, io, wext, xhalo, yhalo, io_t, awbuf, g0, g1, g2, s0, s1, s2,
                 in_sem, hs_sem, hr_sem, gs_sem, gr_sem, ss_sem, sr_sem, out_sem):
    gx = lax.axis_index("gx")
    gz = lax.axis_index("gy")
    last = NX_LOC - 1
    loads = [pltpu.make_async_copy(fac_hbm.at[:, 0], fac_ends.at[0], in_sem.at[0]),
             pltpu.make_async_copy(fac_hbm.at[:, last], fac_ends.at[1], in_sem.at[1]),
             pltpu.make_async_copy(fac_hbm.at[:, pl.ds(1, NX_LOC - 2)], fac_mid, in_sem.at[2]),
             pltpu.make_async_copy(act_hbm, io.at[pl.ds(0, CONTROLS)], in_sem.at[3]),
             pltpu.make_async_copy(sen_hbm, io.at[pl.ds(CONTROLS, CONTROLS)], in_sem.at[4]),
             pltpu.make_async_copy(diag_hbm, diag_ref, in_sem.at[5])]
    for load in loads:
        load.start()
    barrier = pltpu.get_barrier_semaphore()
    right, left = ((gx + 1) % 32, gz), ((gx + 31) % 32, gz)
    up, down = (gx, (gz + 1) % 8), (gx, (gz + 7) % 8)
    count = 0
    for n, me, peers in peer_groups():
        for peer in peers:
            pl.semaphore_signal(barrier, inc=1, device_id=peer, device_id_type=MESH)
            count += 1
    for target in (right, left):
        pl.semaphore_signal(barrier, inc=1, device_id=target, device_id_type=MESH)
        count += 1
    start = off_ref[0]
    inner_y = pl.ds(1, NY_LOC)
    inner_x = pl.ds(1, NX_LOC)
    side_x = jnp.zeros((NY_LOC + 2, WINDOW, NZ), bf16)
    side_y = jnp.zeros((NX_LOC + 2, WINDOW, NZ), bf16)
    wext[0] = side_x
    wext[NX_LOC + 1] = side_x
    wext[:, 0] = side_y
    wext[:, NY_LOC + 1] = side_y

    def turned(plane):
        return jnp.swapaxes(plane.astype(f32), 0, 1).astype(bf16)

    loads[0].wait()
    loads[1].wait()
    wext[1, inner_y] = turned(fac_ends[0, pl.ds(start, WINDOW)])
    wext[NX_LOC, inner_y] = turned(fac_ends[1, pl.ds(start, WINDOW)])
    pl.semaphore_wait(barrier, count)
    moves = (
        (wext.at[NX_LOC, inner_y], xhalo.at[0], right),
        (wext.at[1, inner_y], xhalo.at[1], left),
        (wext.at[inner_x, NY_LOC], yhalo.at[0], up),
        (wext.at[inner_x, 1], yhalo.at[1], down),
    )
    copies = [pltpu.make_async_remote_copy(source, target, hs_sem.at[at], hr_sem.at[at], device_id=who, device_id_type=MESH)
              for at, (source, target, who) in enumerate(moves)]
    copies[0].start()
    copies[1].start()
    loads[2].wait()

    def turn(x, carry):
        wext[x + 2, inner_y] = turned(fac_mid[pl.ds(start, WINDOW), x])
        return carry

    lax.fori_loop(0, NX_LOC - 2, turn, 0)
    copies[2].start()
    copies[3].start()

    def gram_plane(x, total):
        part = jnp.zeros((WINDOW, WINDOW), f32)
        for y in range(NY_LOC):
            rows = wext[x + 1, y + 1]
            part = part + bdot(rows, rows, ((1,), (1,)))
        return total + part

    gram_local = lax.fori_loop(0, NX_LOC, gram_plane, jnp.zeros((WINDOW, WINDOW), f32)) * (1.0 / CELLS)
    gram_sum = Reduction((g0, g1, g2), gs_sem, gr_sem)
    cross_sum = Reduction((s0, s1, s2), ss_sem, sr_sem)
    gram_sum.send(0, fold(gram_local))
    w_write = pltpu.make_async_copy(wext.at[inner_x, inner_y], w_hbm, out_sem.at[0])
    w_write.start()
    for load in loads[3:]:
        load.wait()

    def turn_io(x, carry):
        io_t[x] = turned(io[:, x])
        return carry

    lax.fori_loop(0, NX_LOC, turn_io, 0)
    gram_sum.send(1, gram_sum.receive(0))

    lane = lax.broadcasted_iota(jnp.int32, (WINDOW, NZ), 1)

    def inside_plane(x, total):
        part = jnp.zeros((112, WINDOW), f32)
        for y in range(NY_LOC):
            w16 = wext[x + 1, y + 1]
            w = w16.astype(f32)
            beside = wext[x + 2, y + 1].astype(f32) + wext[x, y + 1].astype(f32)
            beside = beside + wext[x + 1, y + 2].astype(f32) + wext[x + 1, y].astype(f32)
            beside = beside + jnp.where(lane == NZ - 1, 0.0, pltpu.roll(w, NZ - 1, 1))
            beside = beside + jnp.where(lane == 0, 0.0, pltpu.roll(w, 1, 1))
            image = beside - (6.0 + diag_ref[x, y:y + 1, :]) * w
            parts = jnp.concatenate(pieces(image, 3), axis=0)
            awbuf[x, y] = parts
            part = part + bdot(jnp.concatenate([parts, io_t[x, y]], axis=0), w16, ((1,), (1,)))
        return total + part

    total = lax.fori_loop(0, NX_LOC, inside_plane, jnp.zeros((112, WINDOW), f32))
    cross = total[0:32] + (total[32:64] + total[64:96])
    for copy in copies:
        copy.wait()

    for edge, halo in ((gx == 0, xhalo.at[0]), (gx == 31, xhalo.at[1]), (gz == 0, yhalo.at[0]), (gz == 7, yhalo.at[1])):
        @pl.when(edge)
        def _(halo=halo):
            halo[...] = jnp.zeros_like(halo)

    for y in range(NY_LOC):
        cross = cross + bdot(xhalo[0, y], wext[1, y + 1], ((1,), (1,)))
        cross = cross + bdot(xhalo[1, y], wext[NX_LOC, y + 1], ((1,), (1,)))
    for x in range(NX_LOC):
        cross = cross + bdot(yhalo[0, x], wext[x + 1, 1], ((1,), (1,)))
        cross = cross + bdot(yhalo[1, x], wext[x + 1, NY_LOC], ((1,), (1,)))
    io_part = total[96:112]
    io_fold = jnp.concatenate([io_part[4 * q:4 * q + 4] for q in range(4)], axis=1)
    cross_sum.send(0, jnp.concatenate([fold(cross), io_fold], axis=0) * (1.0 / CELLS))

    def add_layer(x, y, halo):
        parts = awbuf[x, y].astype(f32)
        image = parts[0:32] + (parts[32:64] + parts[64:96]) + halo.astype(f32)
        awbuf[x, y] = jnp.concatenate(pieces(image, 3), axis=0)

    for y in range(NY_LOC):
        add_layer(0, y, xhalo[0, y])
        add_layer(last, y, xhalo[1, y])
    for x in range(NX_LOC):
        add_layer(x, 0, yhalo[0, x])
        add_layer(x, NY_LOC - 1, yhalo[1, x])
    cross_sum.send(1, cross_sum.receive(0))
    aw_write = pltpu.make_async_copy(awbuf, aw_hbm, out_sem.at[1])
    aw_write.start()
    gram_sum.send(2, gram_sum.receive(1))
    cross_sum.send(2, cross_sum.receive(1))
    gram = unfold(gram_sum.receive(2))
    ident = eye(WINDOW)
    table = jnp.concatenate([gram, ident, jnp.zeros((WINDOW, 64), f32)], axis=1)
    inverse_first = unit_pivots(sweep(table, WINDOW, False))[:, 32:64]
    gram_second = dot(dot(inverse_first, gram), inverse_first, ((1,), (1,)))
    table = jnp.concatenate([gram_second, ident, jnp.zeros((WINDOW, 64), f32)], axis=1)
    inverse_second = unit_pivots(sweep(table, WINDOW, False))[:, 32:64]
    transform = dot(inverse_second, inverse_first)
    received = cross_sum.receive(2)
    cross = unfold(received[0:8])
    io_rows = jnp.concatenate([received[8:12, 32 * q:32 * q + 32] for q in range(4)], axis=0)
    raw = dot(dot(transform, cross), transform, ((1,), (1,)))
    io_basis = dot(transform, io_rows, ((1,), (1,)))
    small_ref[0:32] = jnp.concatenate([raw, transform, io_basis, jnp.zeros((WINDOW, 48), f32)], axis=1)
    small_ref[32:64] = jnp.concatenate([gram, jnp.zeros((WINDOW, 96), f32)], axis=1)
    gram_sum.finish()
    cross_sum.finish()
    w_write.wait()
    aw_write.wait()


def stats(offset, factor, diagonal, actuators, sensors):
    vmem, anywhere = pl.BlockSpec(memory_space=pltpu.VMEM), pl.BlockSpec(memory_space=pltpu.HBM)
    dma = pltpu.SemaphoreType.DMA
    return pl.pallas_call(
        stats_kernel,
        out_shape=(jax.ShapeDtypeStruct((64, 128), f32),
                   jax.ShapeDtypeStruct((NX_LOC, NY_LOC, WINDOW, NZ), bf16),
                   jax.ShapeDtypeStruct((NX_LOC, NY_LOC, 96, NZ), bf16)),
        in_specs=[pl.BlockSpec(memory_space=pltpu.SMEM), anywhere, anywhere, anywhere, anywhere],
        out_specs=(vmem, anywhere, anywhere),
        scratch_shapes=[
            pltpu.VMEM((2, 64, NY_LOC, NZ), bf16), pltpu.VMEM((64, NX_LOC - 2, NY_LOC, NZ), bf16),
            pltpu.VMEM((NX_LOC, NY_LOC, NZ), f32),
            pltpu.VMEM((2 * CONTROLS, NX_LOC, NY_LOC, NZ), bf16),
            pltpu.VMEM((NX_LOC + 2, NY_LOC + 2, WINDOW, NZ), bf16),
            pltpu.VMEM((2, NY_LOC, WINDOW, NZ), bf16), pltpu.VMEM((2, NX_LOC, WINDOW, NZ), bf16),
            pltpu.VMEM((NX_LOC, NY_LOC, 2 * CONTROLS, NZ), bf16),
            pltpu.VMEM((NX_LOC, NY_LOC, 96, NZ), bf16),
            pltpu.VMEM((2, 8, 128), f32), pltpu.VMEM((16, 8, 128), f32), pltpu.VMEM((8, 8, 128), f32),
            pltpu.VMEM((2, 12, 128), f32), pltpu.VMEM((16, 12, 128), f32), pltpu.VMEM((8, 12, 128), f32),
            dma((6,)), dma((4,)), dma((4,)), dma((3,)), dma((3,)), dma((3,)), dma((3,)), dma((2,)),
        ],
        compiler_params=pltpu.CompilerParams(collective_id=0, has_side_effects=True, vmem_limit_bytes=60 << 20),
        name="stats_all_reduce",
    )(offset, factor, diagonal, actuators, sensors)


def sweep(table, count, upward):
    row_at = lax.broadcasted_iota(jnp.int32, table.shape, 0)
    for start in range(0, count, 8):
        columns = [jnp.broadcast_to(table[:, k:k + 1], table.shape) for k in range(start, start + 8)]
        for at in range(0, 8, 2):
            k = start + at
            col0, col1 = columns[at], columns[at + 1]
            a, b, c, d = col0[k:k + 1], col1[k:k + 1], col0[k + 1:k + 2], col1[k + 1:k + 2]
            inverse = 1.0 / (a * d - b * c)

            def step(value):
                row0, row1 = value[k:k + 1], value[k + 1:k + 2]
                scaled0 = (row0 * d - row1 * b) * inverse
                scaled1 = (row1 * a - row0 * c) * inverse
                other = value - (col0 * scaled0 + col1 * scaled1)
                if upward:
                    return jnp.where(row_at == k, scaled0, jnp.where(row_at == k + 1, scaled1, other))
                inner = row1 - row0 * (c / a)
                return jnp.where(row_at > k + 1, other, jnp.where(row_at == k + 1, inner, value))

            table = step(table)
            for later in range(at + 2, 8):
                columns[later] = step(columns[later])
    return table


def unit_pivots(done):
    row_at = lax.broadcasted_iota(jnp.int32, (WINDOW, WINDOW), 0)
    col_at = lax.broadcasted_iota(jnp.int32, (WINDOW, WINDOW), 1)
    pivots = jnp.sum(jnp.where(row_at == col_at, done[:, :WINDOW], 0.0), axis=1, keepdims=True)
    return done * (1.0 / jnp.sqrt(pivots))


def eye(n):
    return (lax.broadcasted_iota(jnp.int32, (n, n), 0) == lax.broadcasted_iota(jnp.int32, (n, n), 1)).astype(f32)


def small_algebra(small):
    ident = eye(WINDOW)
    raw = small[0:32, 0:32]
    transform = small[0:32, 32:64]
    projected = 0.5 * (raw + raw.T)
    drive = small[0:32, 64:72]
    sense = small[0:32, 72:80]
    gram = small[32:64, 0:32]
    shifted = sweep(jnp.concatenate([ident - projected, ident, jnp.zeros((WINDOW, 64), f32)], axis=1), WINDOW, True)
    inv_n = shifted[:, 32:64]
    drive_t, sense_t = drive.T, sense.T
    hd = dot3(inv_n, drive)
    hd_t = hd.T
    sense_h = dot3(sense_t, inv_n)
    sense_hd = dot3(sense_t, hd)
    chain = None
    for iteration in range(KLEIN):
        if chain is None:
            einv_t = -inv_n
            chain = -sense_h
        else:
            q_t = 2.0 * dot3(dot3(drive_t, chain, ((1,), (1,))), chain)
            hq_t = dot3(q_t, inv_n)
            q_hd = dot3(q_t, hd)
            small = eye(CONTROLS) + dot3(hd_t, q_t, ((1,), (1,)))
            normal = dot3(small, small, ((1,), (1,)))
            table = jnp.concatenate([normal, dot3(small, hq_t), jnp.zeros((CONTROLS, 88), f32)], axis=1)
            solved = sweep(table, CONTROLS, True)[:, CONTROLS:CONTROLS + WINDOW]
            einv_t = dot3(hd, solved) - inv_n
            chain = dot3(jnp.concatenate([sense_hd, q_hd], axis=0), solved) - jnp.concatenate([sense_h, hq_t], axis=0)
        cayley_t = ident + 2.0 * einv_t
        for doubling in range(SMITH):
            chain = jnp.concatenate([chain, dot3(chain, cayley_t)], axis=0)
            if doubling < SMITH - 1:
                cayley_t = dot3(cayley_t, cayley_t)
    riccati = 2.0 * dot3(chain, chain, ((0,), (0,)))
    both = dot(riccati, jnp.concatenate([transform, dot(projected, transform)], axis=1))
    return both[:, :32], both[:, 32:], riccati, gram


def output_kernel(small_ref, w_hbm, aw_hbm, rot_hbm, res_hbm, ric_ref, gram_ref,
                  wbuf, awbuf, rot, res, coef, tmp, in_sem, out_sem):
    loads = [pltpu.make_async_copy(w_hbm, wbuf, in_sem.at[0]), pltpu.make_async_copy(aw_hbm, awbuf, in_sem.at[1])]
    for load in loads:
        load.start()
    rotate, remain, riccati, gram = small_algebra(small_ref[...])
    ric_ref[...] = riccati
    gram_ref[...] = gram
    r0, r1, r2 = pieces(rotate, 3)
    m0, m1, m2 = pieces(-remain, 3)
    zero = jnp.zeros((WINDOW, WINDOW), bf16)
    cat = lambda *blocks: jnp.concatenate(blocks, axis=1)
    coef[...] = jnp.concatenate([
        cat(r0, zero, zero, zero), cat(m0, r0, r0, r0),
        cat(r1, zero, zero, zero), cat(m1, r1, r1, zero),
        cat(r2, zero, zero, zero), cat(m2, r2, zero, zero)], axis=0)
    for load in loads:
        load.wait()

    def plane(x, carry):
        for y in range(NY_LOC):
            data = jnp.concatenate([wbuf[x, y], awbuf[x, y]], axis=0)
            out = bdot(coef[...], data)
            tmp[y] = out[0:64] + (out[64:128] + out[128:192])
        rot[x] = jnp.swapaxes(tmp[:, 0:32, :], 0, 1).astype(bf16)
        res[x] = jnp.swapaxes(tmp[:, 32:64, :], 0, 1).astype(bf16)
        pltpu.make_async_copy(rot.at[x], rot_hbm.at[:, x], out_sem.at[0]).start()
        pltpu.make_async_copy(res.at[x], res_hbm.at[:, x], out_sem.at[1]).start()
        return carry

    lax.fori_loop(0, NX_LOC, plane, 0)
    pltpu.make_async_copy(rot, rot, out_sem.at[0]).wait()
    pltpu.make_async_copy(res, res, out_sem.at[1]).wait()


def outputs(small, w_t, aw):
    field = (WINDOW, NX_LOC, NY_LOC, NZ)
    vmem, hbm = pl.BlockSpec(memory_space=pltpu.VMEM), pl.BlockSpec(memory_space=pltpu.HBM)
    return pl.pallas_call(
        output_kernel,
        out_shape=(jax.ShapeDtypeStruct(field, bf16), jax.ShapeDtypeStruct(field, bf16),
                   jax.ShapeDtypeStruct((WINDOW, WINDOW), f32), jax.ShapeDtypeStruct((WINDOW, WINDOW), f32)),
        in_specs=[vmem, hbm, hbm],
        out_specs=(hbm, hbm, vmem, vmem),
        scratch_shapes=[
            pltpu.VMEM((NX_LOC, NY_LOC, WINDOW, NZ), bf16), pltpu.VMEM((NX_LOC, NY_LOC, 96, NZ), bf16),
            pltpu.VMEM((NX_LOC, WINDOW, NY_LOC, NZ), bf16), pltpu.VMEM((NX_LOC, WINDOW, NY_LOC, NZ), bf16),
            pltpu.VMEM((192, 128), bf16), pltpu.VMEM((NY_LOC, 64, NZ), f32),
            pltpu.SemaphoreType.DMA((2,)), pltpu.SemaphoreType.DMA((2,)),
        ],
        compiler_params=pltpu.CompilerParams(vmem_limit_bytes=60 << 20),
        name="algebra_outputs",
    )(small, w_t, aw)


def local(factor, offset, diagonal, actuators, sensors):
    small, w_t, aw = stats(offset, factor, diagonal, actuators, sensors)
    return outputs(small, w_t, aw)


def solution(mesh):
    return jax.shard_map(
        local,
        mesh=mesh,
        in_specs=(P(None, "gx", "gy", None), P(), P("gx", "gy", None), P(None, "gx", "gy", None), P(None, "gx", "gy", None)),
        out_specs=(P(None, "gx", "gy", None), P(None, "gx", "gy", None), P(), P()),
        check_vma=False,
    )
```

```python
import functools
import jax
import jax.numpy as jnp
from jax import lax
from jax.experimental import pallas as pl
from jax.experimental.pallas import tpu as pltpu
from jax.sharding import PartitionSpec as P

WINDOW = 32
KLEIN = 3
SMITH = 4
CONTROLS = 8
NX_LOC, NY_LOC, NZ = 8, 16, 256
CELLS = 256 * 128 * 256
MESH = pl.DeviceIdType.MESH
f32, bf16 = jnp.float32, jnp.bfloat16
HIGHEST = lax.Precision.HIGHEST


def dot(left, right, dims=((1,), (0,))):
    return lax.dot_general(left, right, (dims, ((), ())), precision=HIGHEST, preferred_element_type=f32)


def bdot(left, right, dims=((1,), (0,))):
    return lax.dot_general(left, right, (dims, ((), ())), preferred_element_type=f32)


def dot3(left, right, dims=((1,), (0,))):
    left_hi, left_lo = pieces(left, 2)
    right_hi, right_lo = pieces(right, 2)
    return bdot(left_hi, right_hi, dims) + (bdot(left_hi, right_lo, dims) + bdot(left_lo, right_hi, dims))


def pieces(value, count):
    out = []
    rest = value
    for at in range(count):
        piece = rest.astype(bf16)
        out.append(piece)
        if at < count - 1:
            rest = rest - piece.astype(f32)
    return out


def peer_groups():
    gx = lax.axis_index("gx")
    z = lax.axis_index("gy")
    xy = gx // 2
    core = gx % 2
    x, y = xy // 4, xy % 4
    plane = sorted(((dx, dy) for dx in range(4) for dy in range(4) if dx or dy),
                   key=lambda d: -(min(d[0], 4 - d[0]) + min(d[1], 4 - d[1])))
    return (
        (2, core, [(xy * 2 + (core + 1) % 2, z)]),
        (16, xy, [((((x + dx) % 4) * 4 + (y + dy) % 4) * 2 + core, z) for dx, dy in plane]),
        (8, z, [(gx, (z + dz) % 8) for dz in (4, 3, 5, 2, 6, 1, 7)]),
    )


def tree_sum(parts):
    while len(parts) > 1:
        parts = [parts[i] + parts[i + 1] for i in range(0, len(parts) - 1, 2)] + parts[len(parts) - len(parts) % 2:]
    return parts[0]


class Reduction:
    def __init__(self, bufs, s_sem, r_sem):
        self.bufs, self.s_sem, self.r_sem = bufs, s_sem, r_sem
        self.groups = peer_groups()

    def send(self, at, value):
        n, me, peers = self.groups[at]
        buf = self.bufs[at]
        buf[me] = value
        for peer in peers:
            pltpu.make_async_remote_copy(buf.at[me], buf.at[me], self.s_sem.at[at], self.r_sem.at[at],
                                         device_id=peer, device_id_type=MESH).start()

    def receive(self, at):
        n = self.groups[at][0]
        buf = self.bufs[at]
        span = buf.at[pl.ds(0, n - 1)]
        pltpu.make_async_copy(span, span, self.r_sem.at[at]).wait()
        return tree_sum([buf[j] for j in range(n)])

    def finish(self):
        for at, (n, me, peers) in enumerate(self.groups):
            span = self.bufs[at].at[pl.ds(0, n - 1)]
            pltpu.make_async_copy(span, span, self.s_sem.at[at]).wait()


def fold(rows):
    return jnp.concatenate([rows[8 * q:8 * q + 8] for q in range(4)], axis=1)


def unfold(block):
    return jnp.concatenate([block[:, 32 * q:32 * q + 32] for q in range(4)], axis=0)


def stats_kernel(off_ref, fac_hbm, diag_hbm, act_hbm, sen_hbm, small_ref, w_hbm, aw_hbm,
                 fac_ends, fac_mid, diag_ref, io, wext, xhalo, yhalo, io_t, awbuf, g0, g1, g2, s0, s1, s2,
                 in_sem, hs_sem, hr_sem, gs_sem, gr_sem, ss_sem, sr_sem, out_sem):
    gx = lax.axis_index("gx")
    gz = lax.axis_index("gy")
    last = NX_LOC - 1
    loads = [pltpu.make_async_copy(fac_hbm.at[:, 0], fac_ends.at[0], in_sem.at[0]),
             pltpu.make_async_copy(fac_hbm.at[:, last], fac_ends.at[1], in_sem.at[1]),
             pltpu.make_async_copy(fac_hbm.at[:, pl.ds(1, NX_LOC - 2)], fac_mid, in_sem.at[2]),
             pltpu.make_async_copy(act_hbm, io.at[pl.ds(0, CONTROLS)], in_sem.at[3]),
             pltpu.make_async_copy(sen_hbm, io.at[pl.ds(CONTROLS, CONTROLS)], in_sem.at[4]),
             pltpu.make_async_copy(diag_hbm, diag_ref, in_sem.at[5])]
    for load in loads:
        load.start()
    barrier = pltpu.get_barrier_semaphore()
    right, left = ((gx + 1) % 32, gz), ((gx + 31) % 32, gz)
    up, down = (gx, (gz + 1) % 8), (gx, (gz + 7) % 8)
    count = 0
    for n, me, peers in peer_groups():
        for peer in peers:
            pl.semaphore_signal(barrier, inc=1, device_id=peer, device_id_type=MESH)
            count += 1
    for target in (right, left):
        pl.semaphore_signal(barrier, inc=1, device_id=target, device_id_type=MESH)
        count += 1
    start = off_ref[0]
    inner_y = pl.ds(1, NY_LOC)
    inner_x = pl.ds(1, NX_LOC)
    side_x = jnp.zeros((NY_LOC + 2, WINDOW, NZ), bf16)
    side_y = jnp.zeros((NX_LOC + 2, WINDOW, NZ), bf16)
    wext[0] = side_x
    wext[NX_LOC + 1] = side_x
    wext[:, 0] = side_y
    wext[:, NY_LOC + 1] = side_y

    def turned(plane):
        return jnp.swapaxes(plane.astype(f32), 0, 1).astype(bf16)

    loads[0].wait()
    loads[1].wait()
    wext[1, inner_y] = turned(fac_ends[0, pl.ds(start, WINDOW)])
    wext[NX_LOC, inner_y] = turned(fac_ends[1, pl.ds(start, WINDOW)])
    pl.semaphore_wait(barrier, count)
    moves = (
        (wext.at[NX_LOC, inner_y], xhalo.at[0], right),
        (wext.at[1, inner_y], xhalo.at[1], left),
        (wext.at[inner_x, NY_LOC], yhalo.at[0], up),
        (wext.at[inner_x, 1], yhalo.at[1], down),
    )
    copies = [pltpu.make_async_remote_copy(source, target, hs_sem.at[at], hr_sem.at[at], device_id=who, device_id_type=MESH)
              for at, (source, target, who) in enumerate(moves)]
    copies[0].start()
    copies[1].start()
    loads[2].wait()

    def turn(x, carry):
        wext[x + 2, inner_y] = turned(fac_mid[pl.ds(start, WINDOW), x])
        return carry

    lax.fori_loop(0, NX_LOC - 2, turn, 0)
    copies[2].start()
    copies[3].start()

    def gram_plane(x, total):
        part = jnp.zeros((WINDOW, WINDOW), f32)
        for y in range(NY_LOC):
            rows = wext[x + 1, y + 1]
            part = part + bdot(rows, rows, ((1,), (1,)))
        return total + part

    gram_local = lax.fori_loop(0, NX_LOC, gram_plane, jnp.zeros((WINDOW, WINDOW), f32)) * (1.0 / CELLS)
    gram_sum = Reduction((g0, g1, g2), gs_sem, gr_sem)
    cross_sum = Reduction((s0, s1, s2), ss_sem, sr_sem)
    gram_sum.send(0, fold(gram_local))
    w_write = pltpu.make_async_copy(wext.at[inner_x, inner_y], w_hbm, out_sem.at[0])
    w_write.start()
    for load in loads[3:]:
        load.wait()

    def turn_io(x, carry):
        io_t[x] = turned(io[:, x])
        return carry

    lax.fori_loop(0, NX_LOC, turn_io, 0)
    gram_sum.send(1, gram_sum.receive(0))

    lane = lax.broadcasted_iota(jnp.int32, (WINDOW, NZ), 1)

    def inside_plane(x, total):
        part = jnp.zeros((112, WINDOW), f32)
        rows = [wext[x + 1, 0].astype(f32), wext[x + 1, 1].astype(f32)]
        for y in range(NY_LOC):
            rows.append(wext[x + 1, y + 2].astype(f32))
            w16 = wext[x + 1, y + 1]
            w = rows[y + 1]
            beside = wext[x + 2, y + 1].astype(f32) + wext[x, y + 1].astype(f32)
            beside = beside + rows[y + 2] + rows[y]
            beside = beside + jnp.where(lane == NZ - 1, 0.0, pltpu.roll(w16, NZ - 1, 1).astype(f32))
            beside = beside + jnp.where(lane == 0, 0.0, pltpu.roll(w16, 1, 1).astype(f32))
            image = beside - (6.0 + diag_ref[x, y:y + 1, :]) * w
            parts = jnp.concatenate(pieces(image, 3), axis=0)
            awbuf[x, y] = parts
            part = part + bdot(jnp.concatenate([parts, io_t[x, y]], axis=0), w16, ((1,), (1,)))
        return total + part

    total = lax.fori_loop(0, NX_LOC, inside_plane, jnp.zeros((112, WINDOW), f32))
    cross = total[0:32] + (total[32:64] + total[64:96])
    for copy in copies:
        copy.wait()

    for edge, halo in ((gx == 0, xhalo.at[0]), (gx == 31, xhalo.at[1]), (gz == 0, yhalo.at[0]), (gz == 7, yhalo.at[1])):
        @pl.when(edge)
        def _(halo=halo):
            halo[...] = jnp.zeros_like(halo)

    for y in range(NY_LOC):
        cross = cross + bdot(xhalo[0, y], wext[1, y + 1], ((1,), (1,)))
        cross = cross + bdot(xhalo[1, y], wext[NX_LOC, y + 1], ((1,), (1,)))
    for x in range(NX_LOC):
        cross = cross + bdot(yhalo[0, x], wext[x + 1, 1], ((1,), (1,)))
        cross = cross + bdot(yhalo[1, x], wext[x + 1, NY_LOC], ((1,), (1,)))
    io_part = total[96:112]
    io_fold = jnp.concatenate([io_part[4 * q:4 * q + 4] for q in range(4)], axis=1)
    cross_sum.send(0, jnp.concatenate([fold(cross), io_fold], axis=0) * (1.0 / CELLS))

    def add_layer(x, y, halo):
        parts = awbuf[x, y].astype(f32)
        image = parts[0:32] + (parts[32:64] + parts[64:96]) + halo.astype(f32)
        awbuf[x, y] = jnp.concatenate(pieces(image, 3), axis=0)

    for y in range(NY_LOC):
        add_layer(0, y, xhalo[0, y])
        add_layer(last, y, xhalo[1, y])
    for x in range(NX_LOC):
        add_layer(x, 0, yhalo[0, x])
        add_layer(x, NY_LOC - 1, yhalo[1, x])
    cross_sum.send(1, cross_sum.receive(0))
    aw_write = pltpu.make_async_copy(awbuf, aw_hbm, out_sem.at[1])
    aw_write.start()
    gram_sum.send(2, gram_sum.receive(1))
    cross_sum.send(2, cross_sum.receive(1))
    gram = unfold(gram_sum.receive(2))
    ident = eye(WINDOW)
    table = jnp.concatenate([gram, ident, jnp.zeros((WINDOW, 64), f32)], axis=1)
    inverse_first = unit_pivots(sweep(table, WINDOW, False))[:, 32:64]
    gram_second = dot(dot(inverse_first, gram), inverse_first, ((1,), (1,)))
    table = jnp.concatenate([gram_second, ident, jnp.zeros((WINDOW, 64), f32)], axis=1)
    inverse_second = unit_pivots(sweep(table, WINDOW, False))[:, 32:64]
    transform = dot(inverse_second, inverse_first)
    received = cross_sum.receive(2)
    cross = unfold(received[0:8])
    io_rows = jnp.concatenate([received[8:12, 32 * q:32 * q + 32] for q in range(4)], axis=0)
    raw = dot(dot(transform, cross), transform, ((1,), (1,)))
    io_basis = dot(transform, io_rows, ((1,), (1,)))
    small_ref[0:32] = jnp.concatenate([raw, transform, io_basis, jnp.zeros((WINDOW, 48), f32)], axis=1)
    small_ref[32:64] = jnp.concatenate([gram, jnp.zeros((WINDOW, 96), f32)], axis=1)
    gram_sum.finish()
    cross_sum.finish()
    w_write.wait()
    aw_write.wait()


def stats(offset, factor, diagonal, actuators, sensors):
    vmem, anywhere = pl.BlockSpec(memory_space=pltpu.VMEM), pl.BlockSpec(memory_space=pltpu.HBM)
    dma = pltpu.SemaphoreType.DMA
    return pl.pallas_call(
        stats_kernel,
        out_shape=(jax.ShapeDtypeStruct((64, 128), f32),
                   jax.ShapeDtypeStruct((NX_LOC, NY_LOC, WINDOW, NZ), bf16),
                   jax.ShapeDtypeStruct((NX_LOC, NY_LOC, 96, NZ), bf16)),
        in_specs=[pl.BlockSpec(memory_space=pltpu.SMEM), anywhere, anywhere, anywhere, anywhere],
        out_specs=(vmem, anywhere, anywhere),
        scratch_shapes=[
            pltpu.VMEM((2, 64, NY_LOC, NZ), bf16), pltpu.VMEM((64, NX_LOC - 2, NY_LOC, NZ), bf16),
            pltpu.VMEM((NX_LOC, NY_LOC, NZ), f32),
            pltpu.VMEM((2 * CONTROLS, NX_LOC, NY_LOC, NZ), bf16),
            pltpu.VMEM((NX_LOC + 2, NY_LOC + 2, WINDOW, NZ), bf16),
            pltpu.VMEM((2, NY_LOC, WINDOW, NZ), bf16), pltpu.VMEM((2, NX_LOC, WINDOW, NZ), bf16),
            pltpu.VMEM((NX_LOC, NY_LOC, 2 * CONTROLS, NZ), bf16),
            pltpu.VMEM((NX_LOC, NY_LOC, 96, NZ), bf16),
            pltpu.VMEM((2, 8, 128), f32), pltpu.VMEM((16, 8, 128), f32), pltpu.VMEM((8, 8, 128), f32),
            pltpu.VMEM((2, 12, 128), f32), pltpu.VMEM((16, 12, 128), f32), pltpu.VMEM((8, 12, 128), f32),
            dma((6,)), dma((4,)), dma((4,)), dma((3,)), dma((3,)), dma((3,)), dma((3,)), dma((2,)),
        ],
        compiler_params=pltpu.CompilerParams(collective_id=0, has_side_effects=True, vmem_limit_bytes=60 << 20),
        name="stats_all_reduce",
    )(offset, factor, diagonal, actuators, sensors)


def sweep(table, count, upward):
    row_at = lax.broadcasted_iota(jnp.int32, table.shape, 0)
    for start in range(0, count, 8):
        columns = [jnp.broadcast_to(table[:, k:k + 1], table.shape) for k in range(start, start + 8)]
        for at in range(0, 8, 2):
            k = start + at
            col0, col1 = columns[at], columns[at + 1]
            a, b, c, d = col0[k:k + 1], col1[k:k + 1], col0[k + 1:k + 2], col1[k + 1:k + 2]
            inverse = 1.0 / (a * d - b * c)

            def step(value):
                row0, row1 = value[k:k + 1], value[k + 1:k + 2]
                scaled0 = (row0 * d - row1 * b) * inverse
                scaled1 = (row1 * a - row0 * c) * inverse
                other = value - (col0 * scaled0 + col1 * scaled1)
                if upward:
                    return jnp.where(row_at == k, scaled0, jnp.where(row_at == k + 1, scaled1, other))
                inner = row1 - row0 * (c / a)
                return jnp.where(row_at > k + 1, other, jnp.where(row_at == k + 1, inner, value))

            table = step(table)
            for later in range(at + 2, 8):
                columns[later] = step(columns[later])
    return table


def unit_pivots(done):
    row_at = lax.broadcasted_iota(jnp.int32, (WINDOW, WINDOW), 0)
    col_at = lax.broadcasted_iota(jnp.int32, (WINDOW, WINDOW), 1)
    pivots = jnp.sum(jnp.where(row_at == col_at, done[:, :WINDOW], 0.0), axis=1, keepdims=True)
    return done * (1.0 / jnp.sqrt(pivots))


def eye(n):
    return (lax.broadcasted_iota(jnp.int32, (n, n), 0) == lax.broadcasted_iota(jnp.int32, (n, n), 1)).astype(f32)


def small_algebra(small):
    ident = eye(WINDOW)
    raw = small[0:32, 0:32]
    transform = small[0:32, 32:64]
    projected = 0.5 * (raw + raw.T)
    drive = small[0:32, 64:72]
    sense = small[0:32, 72:80]
    gram = small[32:64, 0:32]
    shifted = sweep(jnp.concatenate([ident - projected, ident, jnp.zeros((WINDOW, 64), f32)], axis=1), WINDOW, True)
    inv_n = shifted[:, 32:64]
    drive_t, sense_t = drive.T, sense.T
    hd = dot3(inv_n, drive)
    hd_t = hd.T
    sense_h = dot3(sense_t, inv_n)
    sense_hd = dot3(sense_t, hd)
    chain = None
    for iteration in range(KLEIN):
        if chain is None:
            einv_t = -inv_n
            chain = -sense_h
        else:
            q_t = 2.0 * dot3(dot3(drive_t, chain, ((1,), (1,))), chain)
            hq_t = dot3(q_t, inv_n)
            q_hd = dot3(q_t, hd)
            small = eye(CONTROLS) + dot3(hd_t, q_t, ((1,), (1,)))
            normal = dot3(small, small, ((1,), (1,)))
            table = jnp.concatenate([normal, dot3(small, hq_t), jnp.zeros((CONTROLS, 88), f32)], axis=1)
            solved = sweep(table, CONTROLS, True)[:, CONTROLS:CONTROLS + WINDOW]
            einv_t = dot3(hd, solved) - inv_n
            chain = dot3(jnp.concatenate([sense_hd, q_hd], axis=0), solved) - jnp.concatenate([sense_h, hq_t], axis=0)
        cayley_t = ident + 2.0 * einv_t
        for doubling in range(SMITH):
            chain = jnp.concatenate([chain, dot3(chain, cayley_t)], axis=0)
            if doubling < SMITH - 1:
                cayley_t = dot3(cayley_t, cayley_t)
    riccati = 2.0 * dot3(chain, chain, ((0,), (0,)))
    both = dot(riccati, jnp.concatenate([transform, dot(projected, transform)], axis=1))
    return both[:, :32], both[:, 32:], riccati, gram


def output_kernel(small_ref, w_hbm, aw_hbm, rot_hbm, res_hbm, ric_ref, gram_ref,
                  wbuf, awbuf, rot, res, coef, tmp, in_sem, out_sem):
    loads = [pltpu.make_async_copy(w_hbm, wbuf, in_sem.at[0]), pltpu.make_async_copy(aw_hbm, awbuf, in_sem.at[1])]
    for load in loads:
        load.start()
    rotate, remain, riccati, gram = small_algebra(small_ref[...])
    ric_ref[...] = riccati
    gram_ref[...] = gram
    r0, r1, r2 = pieces(rotate, 3)
    m0, m1, m2 = pieces(-remain, 3)
    zero = jnp.zeros((WINDOW, WINDOW), bf16)
    cat = lambda *blocks: jnp.concatenate(blocks, axis=1)
    coef[...] = jnp.concatenate([
        cat(r0, zero, zero, zero, r2, zero), cat(m0, r0, r0, r0, m2, r2),
        cat(r1, zero, zero, zero, zero, zero), cat(m1, r1, r1, zero, zero, zero)], axis=0)
    for load in loads:
        load.wait()

    def plane(x, carry):
        for y in range(NY_LOC):
            w, parts = wbuf[x, y], awbuf[x, y]
            out = bdot(coef[...], jnp.concatenate([w, parts, w, parts[0:32]], axis=0))
            tmp[y] = out[0:64] + out[64:128]
        rot[x] = jnp.swapaxes(tmp[:, 0:32, :], 0, 1).astype(bf16)
        res[x] = jnp.swapaxes(tmp[:, 32:64, :], 0, 1).astype(bf16)
        pltpu.make_async_copy(rot.at[x], rot_hbm.at[:, x], out_sem.at[0]).start()
        pltpu.make_async_copy(res.at[x], res_hbm.at[:, x], out_sem.at[1]).start()
        return carry

    lax.fori_loop(0, NX_LOC, plane, 0)
    pltpu.make_async_copy(rot, rot, out_sem.at[0]).wait()
    pltpu.make_async_copy(res, res, out_sem.at[1]).wait()


def outputs(small, w_t, aw):
    field = (WINDOW, NX_LOC, NY_LOC, NZ)
    vmem, hbm = pl.BlockSpec(memory_space=pltpu.VMEM), pl.BlockSpec(memory_space=pltpu.HBM)
    return pl.pallas_call(
        output_kernel,
        out_shape=(jax.ShapeDtypeStruct(field, bf16), jax.ShapeDtypeStruct(field, bf16),
                   jax.ShapeDtypeStruct((WINDOW, WINDOW), f32), jax.ShapeDtypeStruct((WINDOW, WINDOW), f32)),
        in_specs=[vmem, hbm, hbm],
        out_specs=(hbm, hbm, vmem, vmem),
        scratch_shapes=[
            pltpu.VMEM((NX_LOC, NY_LOC, WINDOW, NZ), bf16), pltpu.VMEM((NX_LOC, NY_LOC, 96, NZ), bf16),
            pltpu.VMEM((NX_LOC, WINDOW, NY_LOC, NZ), bf16), pltpu.VMEM((NX_LOC, WINDOW, NY_LOC, NZ), bf16),
            pltpu.VMEM((128, 192), bf16), pltpu.VMEM((NY_LOC, 64, NZ), f32),
            pltpu.SemaphoreType.DMA((2,)), pltpu.SemaphoreType.DMA((2,)),
        ],
        compiler_params=pltpu.CompilerParams(vmem_limit_bytes=60 << 20),
        name="algebra_outputs",
    )(small, w_t, aw)


def local(factor, offset, diagonal, actuators, sensors):
    small, w_t, aw = stats(offset, factor, diagonal, actuators, sensors)
    return outputs(small, w_t, aw)


def solution(mesh):
    return jax.shard_map(
        local,
        mesh=mesh,
        in_specs=(P(None, "gx", "gy", None), P(), P("gx", "gy", None), P(None, "gx", "gy", None), P(None, "gx", "gy", None)),
        out_specs=(P(None, "gx", "gy", None), P(None, "gx", "gy", None), P(), P()),
        check_vma=False,
    )
```

```python
import functools
import jax
import jax.numpy as jnp
from jax import lax
from jax.experimental import pallas as pl
from jax.experimental.pallas import tpu as pltpu
from jax.sharding import PartitionSpec as P

WINDOW = 32
KLEIN = 3
SMITH = 4
CONTROLS = 8
NX_LOC, NY_LOC, NZ = 8, 16, 256
CELLS = 256 * 128 * 256
MESH = pl.DeviceIdType.MESH
f32, bf16 = jnp.float32, jnp.bfloat16
HIGHEST = lax.Precision.HIGHEST


def dot(left, right, dims=((1,), (0,))):
    return lax.dot_general(left, right, (dims, ((), ())), precision=HIGHEST, preferred_element_type=f32)


def bdot(left, right, dims=((1,), (0,))):
    return lax.dot_general(left, right, (dims, ((), ())), preferred_element_type=f32)


def dot3(left, right, dims=((1,), (0,))):
    left_hi, left_lo = pieces(left, 2)
    right_hi, right_lo = pieces(right, 2)
    return bdot(left_hi, right_hi, dims) + (bdot(left_hi, right_lo, dims) + bdot(left_lo, right_hi, dims))


def pieces(value, count):
    out = []
    rest = value
    for at in range(count):
        piece = rest.astype(bf16)
        out.append(piece)
        if at < count - 1:
            rest = rest - piece.astype(f32)
    return out


def peer_groups():
    gx = lax.axis_index("gx")
    z = lax.axis_index("gy")
    xy = gx // 2
    core = gx % 2
    x, y = xy // 4, xy % 4
    plane = sorted(((dx, dy) for dx in range(4) for dy in range(4) if dx or dy),
                   key=lambda d: -(min(d[0], 4 - d[0]) + min(d[1], 4 - d[1])))
    return (
        (2, core, [(xy * 2 + (core + 1) % 2, z)]),
        (16, xy, [((((x + dx) % 4) * 4 + (y + dy) % 4) * 2 + core, z) for dx, dy in plane]),
        (8, z, [(gx, (z + dz) % 8) for dz in (4, 3, 5, 2, 6, 1, 7)]),
    )


def tree_sum(parts):
    while len(parts) > 1:
        parts = [parts[i] + parts[i + 1] for i in range(0, len(parts) - 1, 2)] + parts[len(parts) - len(parts) % 2:]
    return parts[0]


class Reduction:
    def __init__(self, bufs, s_sem, r_sem):
        self.bufs, self.s_sem, self.r_sem = bufs, s_sem, r_sem
        self.groups = peer_groups()

    def send(self, at, value):
        n, me, peers = self.groups[at]
        buf = self.bufs[at]
        buf[me] = value
        for peer in peers:
            pltpu.make_async_remote_copy(buf.at[me], buf.at[me], self.s_sem.at[at], self.r_sem.at[at],
                                         device_id=peer, device_id_type=MESH).start()

    def receive(self, at):
        n = self.groups[at][0]
        buf = self.bufs[at]
        span = buf.at[pl.ds(0, n - 1)]
        pltpu.make_async_copy(span, span, self.r_sem.at[at]).wait()
        return tree_sum([buf[j] for j in range(n)])

    def finish(self):
        for at, (n, me, peers) in enumerate(self.groups):
            span = self.bufs[at].at[pl.ds(0, n - 1)]
            pltpu.make_async_copy(span, span, self.s_sem.at[at]).wait()


def fold(rows):
    return jnp.concatenate([rows[8 * q:8 * q + 8] for q in range(4)], axis=1)


def unfold(block):
    return jnp.concatenate([block[:, 32 * q:32 * q + 32] for q in range(4)], axis=0)


def stats_kernel(off_ref, fac_hbm, diag_hbm, act_hbm, sen_hbm, small_ref, w_hbm, aw_hbm,
                 fac_ends, fac_mid, diag_ref, io, wext, xhalo, yhalo, io_t, awbuf, g0, g1, g2, s0, s1, s2,
                 in_sem, hs_sem, hr_sem, gs_sem, gr_sem, ss_sem, sr_sem, out_sem):
    gx = lax.axis_index("gx")
    gz = lax.axis_index("gy")
    last = NX_LOC - 1
    loads = [pltpu.make_async_copy(fac_hbm.at[:, 0], fac_ends.at[0], in_sem.at[0]),
             pltpu.make_async_copy(fac_hbm.at[:, last], fac_ends.at[1], in_sem.at[1]),
             pltpu.make_async_copy(fac_hbm.at[:, pl.ds(1, NX_LOC - 2)], fac_mid, in_sem.at[2]),
             pltpu.make_async_copy(act_hbm, io.at[pl.ds(0, CONTROLS)], in_sem.at[3]),
             pltpu.make_async_copy(sen_hbm, io.at[pl.ds(CONTROLS, CONTROLS)], in_sem.at[4]),
             pltpu.make_async_copy(diag_hbm, diag_ref, in_sem.at[5])]
    for load in loads:
        load.start()
    barrier = pltpu.get_barrier_semaphore()
    right, left = ((gx + 1) % 32, gz), ((gx + 31) % 32, gz)
    up, down = (gx, (gz + 1) % 8), (gx, (gz + 7) % 8)
    count = 0
    for n, me, peers in peer_groups():
        for peer in peers:
            pl.semaphore_signal(barrier, inc=1, device_id=peer, device_id_type=MESH)
            count += 1
    for target in (right, left):
        pl.semaphore_signal(barrier, inc=1, device_id=target, device_id_type=MESH)
        count += 1
    start = off_ref[0]
    inner_y = pl.ds(1, NY_LOC)
    inner_x = pl.ds(1, NX_LOC)
    side_x = jnp.zeros((NY_LOC + 2, WINDOW, NZ), bf16)
    side_y = jnp.zeros((NX_LOC + 2, WINDOW, NZ), bf16)
    wext[0] = side_x
    wext[NX_LOC + 1] = side_x
    wext[:, 0] = side_y
    wext[:, NY_LOC + 1] = side_y

    def turned(plane):
        return jnp.swapaxes(plane.astype(f32), 0, 1).astype(bf16)

    loads[0].wait()
    loads[1].wait()
    wext[1, inner_y] = turned(fac_ends[0, pl.ds(start, WINDOW)])
    wext[NX_LOC, inner_y] = turned(fac_ends[1, pl.ds(start, WINDOW)])
    loads[2].wait()

    def turn(x, carry):
        wext[x + 2, inner_y] = turned(fac_mid[pl.ds(start, WINDOW), x])
        return carry

    lax.fori_loop(0, NX_LOC - 2, turn, 0)
    pl.semaphore_wait(barrier, count)
    moves = (
        (wext.at[NX_LOC, inner_y], xhalo.at[0], right),
        (wext.at[1, inner_y], xhalo.at[1], left),
        (wext.at[inner_x, NY_LOC], yhalo.at[0], up),
        (wext.at[inner_x, 1], yhalo.at[1], down),
    )
    copies = [pltpu.make_async_remote_copy(source, target, hs_sem.at[at], hr_sem.at[at], device_id=who, device_id_type=MESH)
              for at, (source, target, who) in enumerate(moves)]
    for copy in copies:
        copy.start()

    def gram_plane(x, total):
        part = jnp.zeros((WINDOW, WINDOW), f32)
        for y in range(NY_LOC):
            rows = wext[x + 1, y + 1]
            part = part + bdot(rows, rows, ((1,), (1,)))
        return total + part

    gram_local = lax.fori_loop(0, NX_LOC, gram_plane, jnp.zeros((WINDOW, WINDOW), f32)) * (1.0 / CELLS)
    gram_sum = Reduction((g0, g1, g2), gs_sem, gr_sem)
    cross_sum = Reduction((s0, s1, s2), ss_sem, sr_sem)
    gram_sum.send(0, fold(gram_local))
    w_write = pltpu.make_async_copy(wext.at[inner_x, inner_y], w_hbm, out_sem.at[0])
    w_write.start()
    for load in loads[3:]:
        load.wait()

    def turn_io(x, carry):
        io_t[x] = turned(io[:, x])
        return carry

    lax.fori_loop(0, NX_LOC, turn_io, 0)
    gram_sum.send(1, gram_sum.receive(0))

    lane = lax.broadcasted_iota(jnp.int32, (WINDOW, NZ), 1)

    def inside_plane(x, total):
        part = jnp.zeros((112, WINDOW), f32)
        rows = [wext[x + 1, 0].astype(f32), wext[x + 1, 1].astype(f32)]
        for y in range(NY_LOC):
            rows.append(wext[x + 1, y + 2].astype(f32))
            w16 = wext[x + 1, y + 1]
            w = rows[y + 1]
            beside = wext[x + 2, y + 1].astype(f32) + wext[x, y + 1].astype(f32)
            beside = beside + rows[y + 2] + rows[y]
            beside = beside + jnp.where(lane == NZ - 1, 0.0, pltpu.roll(w16, NZ - 1, 1).astype(f32))
            beside = beside + jnp.where(lane == 0, 0.0, pltpu.roll(w16, 1, 1).astype(f32))
            image = beside - (6.0 + diag_ref[x, y:y + 1, :]) * w
            parts = jnp.concatenate(pieces(image, 3), axis=0)
            awbuf[x, y] = parts
            part = part + bdot(jnp.concatenate([parts, io_t[x, y]], axis=0), w16, ((1,), (1,)))
        return total + part

    total = lax.fori_loop(0, NX_LOC, inside_plane, jnp.zeros((112, WINDOW), f32))
    cross = total[0:32] + (total[32:64] + total[64:96])
    for copy in copies:
        copy.wait()

    for edge, halo in ((gx == 0, xhalo.at[0]), (gx == 31, xhalo.at[1]), (gz == 0, yhalo.at[0]), (gz == 7, yhalo.at[1])):
        @pl.when(edge)
        def _(halo=halo):
            halo[...] = jnp.zeros_like(halo)

    for y in range(NY_LOC):
        cross = cross + bdot(xhalo[0, y], wext[1, y + 1], ((1,), (1,)))
        cross = cross + bdot(xhalo[1, y], wext[NX_LOC, y + 1], ((1,), (1,)))
    for x in range(NX_LOC):
        cross = cross + bdot(yhalo[0, x], wext[x + 1, 1], ((1,), (1,)))
        cross = cross + bdot(yhalo[1, x], wext[x + 1, NY_LOC], ((1,), (1,)))
    io_part = total[96:112]
    io_fold = jnp.concatenate([io_part[4 * q:4 * q + 4] for q in range(4)], axis=1)
    cross_sum.send(0, jnp.concatenate([fold(cross), io_fold], axis=0) * (1.0 / CELLS))

    def add_layer(x, y, halo):
        parts = awbuf[x, y].astype(f32)
        image = parts[0:32] + (parts[32:64] + parts[64:96]) + halo.astype(f32)
        awbuf[x, y] = jnp.concatenate(pieces(image, 3), axis=0)

    for y in range(NY_LOC):
        add_layer(0, y, xhalo[0, y])
        add_layer(last, y, xhalo[1, y])
    for x in range(NX_LOC):
        add_layer(x, 0, yhalo[0, x])
        add_layer(x, NY_LOC - 1, yhalo[1, x])
    cross_sum.send(1, cross_sum.receive(0))
    aw_write = pltpu.make_async_copy(awbuf, aw_hbm, out_sem.at[1])
    aw_write.start()
    gram_sum.send(2, gram_sum.receive(1))
    cross_sum.send(2, cross_sum.receive(1))
    gram = unfold(gram_sum.receive(2))
    ident = eye(WINDOW)
    table = jnp.concatenate([gram, ident, jnp.zeros((WINDOW, 64), f32)], axis=1)
    inverse_first = unit_pivots(sweep(table, WINDOW, False))[:, 32:64]
    gram_second = dot(dot(inverse_first, gram), inverse_first, ((1,), (1,)))
    table = jnp.concatenate([gram_second, ident, jnp.zeros((WINDOW, 64), f32)], axis=1)
    inverse_second = unit_pivots(sweep(table, WINDOW, False))[:, 32:64]
    transform = dot(inverse_second, inverse_first)
    received = cross_sum.receive(2)
    cross = unfold(received[0:8])
    io_rows = jnp.concatenate([received[8:12, 32 * q:32 * q + 32] for q in range(4)], axis=0)
    raw = dot(dot(transform, cross), transform, ((1,), (1,)))
    io_basis = dot(transform, io_rows, ((1,), (1,)))
    small_ref[0:32] = jnp.concatenate([raw, transform, io_basis, jnp.zeros((WINDOW, 48), f32)], axis=1)
    small_ref[32:64] = jnp.concatenate([gram, jnp.zeros((WINDOW, 96), f32)], axis=1)
    gram_sum.finish()
    cross_sum.finish()
    w_write.wait()
    aw_write.wait()


def stats(offset, factor, diagonal, actuators, sensors):
    vmem, anywhere = pl.BlockSpec(memory_space=pltpu.VMEM), pl.BlockSpec(memory_space=pltpu.HBM)
    dma = pltpu.SemaphoreType.DMA
    return pl.pallas_call(
        stats_kernel,
        out_shape=(jax.ShapeDtypeStruct((64, 128), f32),
                   jax.ShapeDtypeStruct((NX_LOC, NY_LOC, WINDOW, NZ), bf16),
                   jax.ShapeDtypeStruct((NX_LOC, NY_LOC, 96, NZ), bf16)),
        in_specs=[pl.BlockSpec(memory_space=pltpu.SMEM), anywhere, anywhere, anywhere, anywhere],
        out_specs=(vmem, anywhere, anywhere),
        scratch_shapes=[
            pltpu.VMEM((2, 64, NY_LOC, NZ), bf16), pltpu.VMEM((64, NX_LOC - 2, NY_LOC, NZ), bf16),
            pltpu.VMEM((NX_LOC, NY_LOC, NZ), f32),
            pltpu.VMEM((2 * CONTROLS, NX_LOC, NY_LOC, NZ), bf16),
            pltpu.VMEM((NX_LOC + 2, NY_LOC + 2, WINDOW, NZ), bf16),
            pltpu.VMEM((2, NY_LOC, WINDOW, NZ), bf16), pltpu.VMEM((2, NX_LOC, WINDOW, NZ), bf16),
            pltpu.VMEM((NX_LOC, NY_LOC, 2 * CONTROLS, NZ), bf16),
            pltpu.VMEM((NX_LOC, NY_LOC, 96, NZ), bf16),
            pltpu.VMEM((2, 8, 128), f32), pltpu.VMEM((16, 8, 128), f32), pltpu.VMEM((8, 8, 128), f32),
            pltpu.VMEM((2, 12, 128), f32), pltpu.VMEM((16, 12, 128), f32), pltpu.VMEM((8, 12, 128), f32),
            dma((6,)), dma((4,)), dma((4,)), dma((3,)), dma((3,)), dma((3,)), dma((3,)), dma((2,)),
        ],
        compiler_params=pltpu.CompilerParams(collective_id=0, has_side_effects=True, vmem_limit_bytes=60 << 20),
        name="stats_all_reduce",
    )(offset, factor, diagonal, actuators, sensors)


def sweep(table, count, upward):
    row_at = lax.broadcasted_iota(jnp.int32, table.shape, 0)
    for start in range(0, count, 8):
        columns = [jnp.broadcast_to(table[:, k:k + 1], table.shape) for k in range(start, start + 8)]
        for at in range(0, 8, 2):
            k = start + at
            col0, col1 = columns[at], columns[at + 1]
            a, b, c, d = col0[k:k + 1], col1[k:k + 1], col0[k + 1:k + 2], col1[k + 1:k + 2]
            inverse = 1.0 / (a * d - b * c)

            def step(value):
                row0, row1 = value[k:k + 1], value[k + 1:k + 2]
                scaled0 = (row0 * d - row1 * b) * inverse
                scaled1 = (row1 * a - row0 * c) * inverse
                other = value - (col0 * scaled0 + col1 * scaled1)
                if upward:
                    return jnp.where(row_at == k, scaled0, jnp.where(row_at == k + 1, scaled1, other))
                inner = row1 - row0 * (c / a)
                return jnp.where(row_at > k + 1, other, jnp.where(row_at == k + 1, inner, value))

            table = step(table)
            for later in range(at + 2, 8):
                columns[later] = step(columns[later])
    return table


def unit_pivots(done):
    row_at = lax.broadcasted_iota(jnp.int32, (WINDOW, WINDOW), 0)
    col_at = lax.broadcasted_iota(jnp.int32, (WINDOW, WINDOW), 1)
    pivots = jnp.sum(jnp.where(row_at == col_at, done[:, :WINDOW], 0.0), axis=1, keepdims=True)
    return done * (1.0 / jnp.sqrt(pivots))


def eye(n):
    return (lax.broadcasted_iota(jnp.int32, (n, n), 0) == lax.broadcasted_iota(jnp.int32, (n, n), 1)).astype(f32)


def small_algebra(small):
    ident = eye(WINDOW)
    raw = small[0:32, 0:32]
    transform = small[0:32, 32:64]
    projected = 0.5 * (raw + raw.T)
    drive = small[0:32, 64:72]
    sense = small[0:32, 72:80]
    gram = small[32:64, 0:32]
    shifted = sweep(jnp.concatenate([ident - projected, ident, jnp.zeros((WINDOW, 64), f32)], axis=1), WINDOW, True)
    inv_n = shifted[:, 32:64]
    drive_t, sense_t = drive.T, sense.T
    hd = dot3(inv_n, drive)
    hd_t = hd.T
    sense_h = dot3(sense_t, inv_n)
    sense_hd = dot3(sense_t, hd)
    chain = None
    for iteration in range(KLEIN):
        if chain is None:
            einv_t = -inv_n
            chain = -sense_h
        else:
            q_t = 2.0 * dot3(dot3(drive_t, chain, ((1,), (1,))), chain)
            hq_t = dot3(q_t, inv_n)
            q_hd = dot3(q_t, hd)
            small = eye(CONTROLS) + dot3(hd_t, q_t, ((1,), (1,)))
            normal = dot3(small, small, ((1,), (1,)))
            table = jnp.concatenate([normal, dot3(small, hq_t), jnp.zeros((CONTROLS, 88), f32)], axis=1)
            solved = sweep(table, CONTROLS, True)[:, CONTROLS:CONTROLS + WINDOW]
            einv_t = dot3(hd, solved) - inv_n
            chain = dot3(jnp.concatenate([sense_hd, q_hd], axis=0), solved) - jnp.concatenate([sense_h, hq_t], axis=0)
        cayley_t = ident + 2.0 * einv_t
        for doubling in range(SMITH):
            chain = jnp.concatenate([chain, dot3(chain, cayley_t)], axis=0)
            if doubling < SMITH - 1:
                cayley_t = dot3(cayley_t, cayley_t)
    halves = [chain[:128].T, chain[128:].T]
    riccati = 2.0 * (dot3(halves[0], halves[0], ((1,), (1,))) + dot3(halves[1], halves[1], ((1,), (1,))))
    both = dot(riccati, jnp.concatenate([transform, dot(projected, transform)], axis=1))
    return both[:, :32], both[:, 32:], riccati, gram


def output_kernel(small_ref, w_hbm, aw_hbm, rot_hbm, res_hbm, ric_ref, gram_ref,
                  wbuf, awbuf, rot, res, coef, tmp, in_sem, out_sem):
    loads = [pltpu.make_async_copy(w_hbm, wbuf, in_sem.at[0]), pltpu.make_async_copy(aw_hbm, awbuf, in_sem.at[1])]
    for load in loads:
        load.start()
    rotate, remain, riccati, gram = small_algebra(small_ref[...])
    ric_ref[...] = riccati
    gram_ref[...] = gram
    r0, r1, r2 = pieces(rotate, 3)
    m0, m1, m2 = pieces(-remain, 3)
    zero = jnp.zeros((WINDOW, WINDOW), bf16)
    cat = lambda *blocks: jnp.concatenate(blocks, axis=1)
    coef[...] = jnp.concatenate([
        cat(r0, zero, zero, zero, r2, zero), cat(m0, r0, r0, r0, m2, r2),
        cat(r1, zero, zero, zero, zero, zero), cat(m1, r1, r1, zero, zero, zero)], axis=0)
    for load in loads:
        load.wait()

    def plane(x, carry):
        for y in range(NY_LOC):
            w, parts = wbuf[x, y], awbuf[x, y]
            out = bdot(coef[...], jnp.concatenate([w, parts, w, parts[0:32]], axis=0))
            tmp[y] = out[0:64] + out[64:128]
        rot[x] = jnp.swapaxes(tmp[:, 0:32, :], 0, 1).astype(bf16)
        res[x] = jnp.swapaxes(tmp[:, 32:64, :], 0, 1).astype(bf16)
        pltpu.make_async_copy(rot.at[x], rot_hbm.at[:, x], out_sem.at[0]).start()
        pltpu.make_async_copy(res.at[x], res_hbm.at[:, x], out_sem.at[1]).start()
        return carry

    lax.fori_loop(0, NX_LOC, plane, 0)
    pltpu.make_async_copy(rot, rot, out_sem.at[0]).wait()
    pltpu.make_async_copy(res, res, out_sem.at[1]).wait()


def outputs(small, w_t, aw):
    field = (WINDOW, NX_LOC, NY_LOC, NZ)
    vmem, hbm = pl.BlockSpec(memory_space=pltpu.VMEM), pl.BlockSpec(memory_space=pltpu.HBM)
    return pl.pallas_call(
        output_kernel,
        out_shape=(jax.ShapeDtypeStruct(field, bf16), jax.ShapeDtypeStruct(field, bf16),
                   jax.ShapeDtypeStruct((WINDOW, WINDOW), f32), jax.ShapeDtypeStruct((WINDOW, WINDOW), f32)),
        in_specs=[vmem, hbm, hbm],
        out_specs=(hbm, hbm, vmem, vmem),
        scratch_shapes=[
            pltpu.VMEM((NX_LOC, NY_LOC, WINDOW, NZ), bf16), pltpu.VMEM((NX_LOC, NY_LOC, 96, NZ), bf16),
            pltpu.VMEM((NX_LOC, WINDOW, NY_LOC, NZ), bf16), pltpu.VMEM((NX_LOC, WINDOW, NY_LOC, NZ), bf16),
            pltpu.VMEM((128, 192), bf16), pltpu.VMEM((NY_LOC, 64, NZ), f32),
            pltpu.SemaphoreType.DMA((2,)), pltpu.SemaphoreType.DMA((2,)),
        ],
        compiler_params=pltpu.CompilerParams(vmem_limit_bytes=60 << 20),
        name="algebra_outputs",
    )(small, w_t, aw)


def local(factor, offset, diagonal, actuators, sensors):
    small, w_t, aw = stats(offset, factor, diagonal, actuators, sensors)
    return outputs(small, w_t, aw)


def solution(mesh):
    return jax.shard_map(
        local,
        mesh=mesh,
        in_specs=(P(None, "gx", "gy", None), P(), P("gx", "gy", None), P(None, "gx", "gy", None), P(None, "gx", "gy", None)),
        out_specs=(P(None, "gx", "gy", None), P(None, "gx", "gy", None), P(), P()),
        check_vma=False,
    )
```

```python
import functools
import jax
import jax.numpy as jnp
from jax import lax
from jax.experimental import pallas as pl
from jax.experimental.pallas import tpu as pltpu
from jax.sharding import PartitionSpec as P

WINDOW = 32
KLEIN = 3
SMITH = 4
CONTROLS = 8
NX_LOC, NY_LOC, NZ = 8, 16, 256
CELLS = 256 * 128 * 256
MESH = pl.DeviceIdType.MESH
f32, bf16 = jnp.float32, jnp.bfloat16
HIGHEST = lax.Precision.HIGHEST


def dot(left, right, dims=((1,), (0,))):
    return lax.dot_general(left, right, (dims, ((), ())), precision=HIGHEST, preferred_element_type=f32)


def bdot(left, right, dims=((1,), (0,))):
    return lax.dot_general(left, right, (dims, ((), ())), preferred_element_type=f32)


def dot3(left, right, dims=((1,), (0,))):
    left_hi, left_lo = pieces(left, 2)
    right_hi, right_lo = pieces(right, 2)
    return bdot(left_hi, right_hi, dims) + (bdot(left_hi, right_lo, dims) + bdot(left_lo, right_hi, dims))


def pieces(value, count):
    out = []
    rest = value
    for at in range(count):
        piece = rest.astype(bf16)
        out.append(piece)
        if at < count - 1:
            rest = rest - piece.astype(f32)
    return out


def peer_groups():
    gx = lax.axis_index("gx")
    z = lax.axis_index("gy")
    xy = gx // 2
    core = gx % 2
    x, y = xy // 4, xy % 4
    plane = sorted(((dx, dy) for dx in range(4) for dy in range(4) if dx or dy),
                   key=lambda d: -(min(d[0], 4 - d[0]) + min(d[1], 4 - d[1])))
    return (
        (2, core, [(xy * 2 + (core + 1) % 2, z)]),
        (16, xy, [((((x + dx) % 4) * 4 + (y + dy) % 4) * 2 + core, z) for dx, dy in plane]),
        (8, z, [(gx, (z + dz) % 8) for dz in (4, 3, 5, 2, 6, 1, 7)]),
    )


def tree_sum(parts):
    while len(parts) > 1:
        parts = [parts[i] + parts[i + 1] for i in range(0, len(parts) - 1, 2)] + parts[len(parts) - len(parts) % 2:]
    return parts[0]


class Reduction:
    def __init__(self, bufs, s_sem, r_sem):
        self.bufs, self.s_sem, self.r_sem = bufs, s_sem, r_sem
        self.groups = peer_groups()

    def send(self, at, value):
        n, me, peers = self.groups[at]
        buf = self.bufs[at]
        buf[me] = value
        for peer in peers:
            pltpu.make_async_remote_copy(buf.at[me], buf.at[me], self.s_sem.at[at], self.r_sem.at[at],
                                         device_id=peer, device_id_type=MESH).start()

    def receive(self, at):
        n = self.groups[at][0]
        buf = self.bufs[at]
        span = buf.at[pl.ds(0, n - 1)]
        pltpu.make_async_copy(span, span, self.r_sem.at[at]).wait()
        return tree_sum([buf[j] for j in range(n)])

    def finish(self):
        for at, (n, me, peers) in enumerate(self.groups):
            span = self.bufs[at].at[pl.ds(0, n - 1)]
            pltpu.make_async_copy(span, span, self.s_sem.at[at]).wait()


def fold(rows):
    return jnp.concatenate([rows[8 * q:8 * q + 8] for q in range(4)], axis=1)


def unfold(block):
    return jnp.concatenate([block[:, 32 * q:32 * q + 32] for q in range(4)], axis=0)


def stats_kernel(off_ref, fac_hbm, diag_hbm, act_hbm, sen_hbm, small_ref, w_hbm, aw_hbm,
                 fac_ends, fac_mid, diag_ref, io, wext, xhalo, yhalo, io_t, awbuf, g0, g1, g2, s0, s1, s2,
                 in_sem, hs_sem, hr_sem, gs_sem, gr_sem, ss_sem, sr_sem, out_sem):
    gx = lax.axis_index("gx")
    gz = lax.axis_index("gy")
    last = NX_LOC - 1
    loads = [pltpu.make_async_copy(fac_hbm.at[:, 0], fac_ends.at[0], in_sem.at[0]),
             pltpu.make_async_copy(fac_hbm.at[:, last], fac_ends.at[1], in_sem.at[1]),
             pltpu.make_async_copy(fac_hbm.at[:, pl.ds(1, NX_LOC - 2)], fac_mid, in_sem.at[2]),
             pltpu.make_async_copy(act_hbm, io.at[pl.ds(0, CONTROLS)], in_sem.at[3]),
             pltpu.make_async_copy(sen_hbm, io.at[pl.ds(CONTROLS, CONTROLS)], in_sem.at[4]),
             pltpu.make_async_copy(diag_hbm, diag_ref, in_sem.at[5])]
    for load in loads:
        load.start()
    barrier = pltpu.get_barrier_semaphore()
    right, left = ((gx + 1) % 32, gz), ((gx + 31) % 32, gz)
    up, down = (gx, (gz + 1) % 8), (gx, (gz + 7) % 8)
    count = 0
    for n, me, peers in peer_groups():
        for peer in peers:
            pl.semaphore_signal(barrier, inc=1, device_id=peer, device_id_type=MESH)
            count += 1
    for target in (right, left):
        pl.semaphore_signal(barrier, inc=1, device_id=target, device_id_type=MESH)
        count += 1
    start = off_ref[0]
    inner_y = pl.ds(1, NY_LOC)
    inner_x = pl.ds(1, NX_LOC)
    side_x = jnp.zeros((NY_LOC + 2, WINDOW, NZ), bf16)
    side_y = jnp.zeros((NX_LOC + 2, WINDOW, NZ), bf16)
    wext[0] = side_x
    wext[NX_LOC + 1] = side_x
    wext[:, 0] = side_y
    wext[:, NY_LOC + 1] = side_y

    def turned(plane):
        return jnp.swapaxes(plane, 0, 1)

    loads[0].wait()
    loads[1].wait()
    wext[1, inner_y] = turned(fac_ends[0, pl.ds(start, WINDOW)])
    wext[NX_LOC, inner_y] = turned(fac_ends[1, pl.ds(start, WINDOW)])
    loads[2].wait()

    def turn(x, carry):
        wext[x + 2, inner_y] = turned(fac_mid[pl.ds(start, WINDOW), x])
        return carry

    lax.fori_loop(0, NX_LOC - 2, turn, 0)
    pl.semaphore_wait(barrier, count)
    moves = (
        (wext.at[NX_LOC, inner_y], xhalo.at[0], right),
        (wext.at[1, inner_y], xhalo.at[1], left),
        (wext.at[inner_x, NY_LOC], yhalo.at[0], up),
        (wext.at[inner_x, 1], yhalo.at[1], down),
    )
    copies = [pltpu.make_async_remote_copy(source, target, hs_sem.at[at], hr_sem.at[at], device_id=who, device_id_type=MESH)
              for at, (source, target, who) in enumerate(moves)]
    for copy in copies:
        copy.start()

    def gram_plane(x, total):
        part = jnp.zeros((WINDOW, WINDOW), f32)
        for y in range(NY_LOC):
            rows = wext[x + 1, y + 1]
            part = part + bdot(rows, rows, ((1,), (1,)))
        return total + part

    gram_local = lax.fori_loop(0, NX_LOC, gram_plane, jnp.zeros((WINDOW, WINDOW), f32)) * (1.0 / CELLS)
    gram_sum = Reduction((g0, g1, g2), gs_sem, gr_sem)
    cross_sum = Reduction((s0, s1, s2), ss_sem, sr_sem)
    gram_sum.send(0, fold(gram_local))
    w_write = pltpu.make_async_copy(wext.at[inner_x, inner_y], w_hbm, out_sem.at[0])
    w_write.start()
    for load in loads[3:]:
        load.wait()

    def turn_io(x, carry):
        io_t[x] = turned(io[:, x])
        return carry

    lax.fori_loop(0, NX_LOC, turn_io, 0)
    gram_sum.send(1, gram_sum.receive(0))

    lane = lax.broadcasted_iota(jnp.int32, (WINDOW, NZ), 1)

    def inside_plane(x, total):
        part = jnp.zeros((112, WINDOW), f32)
        rows = [wext[x + 1, 0].astype(f32), wext[x + 1, 1].astype(f32)]
        for y in range(NY_LOC):
            rows.append(wext[x + 1, y + 2].astype(f32))
            w16 = wext[x + 1, y + 1]
            w = rows[y + 1]
            beside = wext[x + 2, y + 1].astype(f32) + wext[x, y + 1].astype(f32)
            beside = beside + rows[y + 2] + rows[y]
            beside = beside + jnp.where(lane == NZ - 1, 0.0, pltpu.roll(w16, NZ - 1, 1).astype(f32))
            beside = beside + jnp.where(lane == 0, 0.0, pltpu.roll(w16, 1, 1).astype(f32))
            image = beside - (6.0 + diag_ref[x, y:y + 1, :]) * w
            parts = jnp.concatenate(pieces(image, 3), axis=0)
            awbuf[x, y] = parts
            part = part + bdot(jnp.concatenate([parts, io_t[x, y]], axis=0), w16, ((1,), (1,)))
        return total + part

    total = lax.fori_loop(0, NX_LOC, inside_plane, jnp.zeros((112, WINDOW), f32))
    cross = total[0:32] + (total[32:64] + total[64:96])
    for copy in copies:
        copy.wait()

    for edge, halo in ((gx == 0, xhalo.at[0]), (gx == 31, xhalo.at[1]), (gz == 0, yhalo.at[0]), (gz == 7, yhalo.at[1])):
        @pl.when(edge)
        def _(halo=halo):
            halo[...] = jnp.zeros_like(halo)

    for y in range(NY_LOC):
        cross = cross + bdot(xhalo[0, y], wext[1, y + 1], ((1,), (1,)))
        cross = cross + bdot(xhalo[1, y], wext[NX_LOC, y + 1], ((1,), (1,)))
    for x in range(NX_LOC):
        cross = cross + bdot(yhalo[0, x], wext[x + 1, 1], ((1,), (1,)))
        cross = cross + bdot(yhalo[1, x], wext[x + 1, NY_LOC], ((1,), (1,)))
    io_part = total[96:112]
    io_fold = jnp.concatenate([io_part[4 * q:4 * q + 4] for q in range(4)], axis=1)
    cross_sum.send(0, jnp.concatenate([fold(cross), io_fold], axis=0) * (1.0 / CELLS))

    cross_sum.send(1, cross_sum.receive(0))
    gram_sum.send(2, gram_sum.receive(1))
    def add_layer(x, y, halo):
        parts = awbuf[x, y].astype(f32)
        image = parts[0:32] + (parts[32:64] + parts[64:96]) + halo.astype(f32)
        awbuf[x, y] = jnp.concatenate(pieces(image, 3), axis=0)

    for y in range(NY_LOC):
        add_layer(0, y, xhalo[0, y])
        add_layer(last, y, xhalo[1, y])
    for x in range(NX_LOC):
        add_layer(x, 0, yhalo[0, x])
        add_layer(x, NY_LOC - 1, yhalo[1, x])
    aw_write = pltpu.make_async_copy(awbuf, aw_hbm, out_sem.at[1])
    aw_write.start()
    cross_sum.send(2, cross_sum.receive(1))
    gram = unfold(gram_sum.receive(2))
    ident = eye(WINDOW)
    table = jnp.concatenate([gram, ident, jnp.zeros((WINDOW, 64), f32)], axis=1)
    inverse_first = unit_pivots(sweep(table, WINDOW, False))[:, 32:64]
    gram_second = dot(dot(inverse_first, gram), inverse_first, ((1,), (1,)))
    table = jnp.concatenate([gram_second, ident, jnp.zeros((WINDOW, 64), f32)], axis=1)
    inverse_second = unit_pivots(sweep(table, WINDOW, False))[:, 32:64]
    transform = dot(inverse_second, inverse_first)
    received = cross_sum.receive(2)
    cross = unfold(received[0:8])
    io_rows = jnp.concatenate([received[8:12, 32 * q:32 * q + 32] for q in range(4)], axis=0)
    raw = dot(dot(transform, cross), transform, ((1,), (1,)))
    io_basis = dot(transform, io_rows, ((1,), (1,)))
    small_ref[0:32] = jnp.concatenate([raw, transform, io_basis, jnp.zeros((WINDOW, 48), f32)], axis=1)
    small_ref[32:64] = jnp.concatenate([gram, jnp.zeros((WINDOW, 96), f32)], axis=1)
    gram_sum.finish()
    cross_sum.finish()
    w_write.wait()
    aw_write.wait()


def stats(offset, factor, diagonal, actuators, sensors):
    vmem, anywhere = pl.BlockSpec(memory_space=pltpu.VMEM), pl.BlockSpec(memory_space=pltpu.HBM)
    dma = pltpu.SemaphoreType.DMA
    return pl.pallas_call(
        stats_kernel,
        out_shape=(jax.ShapeDtypeStruct((64, 128), f32),
                   jax.ShapeDtypeStruct((NX_LOC, NY_LOC, WINDOW, NZ), bf16),
                   jax.ShapeDtypeStruct((NX_LOC, NY_LOC, 96, NZ), bf16)),
        in_specs=[pl.BlockSpec(memory_space=pltpu.SMEM), anywhere, anywhere, anywhere, anywhere],
        out_specs=(vmem, anywhere, anywhere),
        scratch_shapes=[
            pltpu.VMEM((2, 64, NY_LOC, NZ), bf16), pltpu.VMEM((64, NX_LOC - 2, NY_LOC, NZ), bf16),
            pltpu.VMEM((NX_LOC, NY_LOC, NZ), f32),
            pltpu.VMEM((2 * CONTROLS, NX_LOC, NY_LOC, NZ), bf16),
            pltpu.VMEM((NX_LOC + 2, NY_LOC + 2, WINDOW, NZ), bf16),
            pltpu.VMEM((2, NY_LOC, WINDOW, NZ), bf16), pltpu.VMEM((2, NX_LOC, WINDOW, NZ), bf16),
            pltpu.VMEM((NX_LOC, NY_LOC, 2 * CONTROLS, NZ), bf16),
            pltpu.VMEM((NX_LOC, NY_LOC, 96, NZ), bf16),
            pltpu.VMEM((2, 8, 128), f32), pltpu.VMEM((16, 8, 128), f32), pltpu.VMEM((8, 8, 128), f32),
            pltpu.VMEM((2, 12, 128), f32), pltpu.VMEM((16, 12, 128), f32), pltpu.VMEM((8, 12, 128), f32),
            dma((6,)), dma((4,)), dma((4,)), dma((3,)), dma((3,)), dma((3,)), dma((3,)), dma((2,)),
        ],
        compiler_params=pltpu.CompilerParams(collective_id=0, has_side_effects=True, vmem_limit_bytes=60 << 20),
        name="stats_all_reduce",
    )(offset, factor, diagonal, actuators, sensors)


def sweep(table, count, upward):
    row_at = lax.broadcasted_iota(jnp.int32, table.shape, 0)
    for start in range(0, count, 8):
        columns = [jnp.broadcast_to(table[:, k:k + 1], table.shape) for k in range(start, start + 8)]
        for at in range(0, 8, 2):
            k = start + at
            col0, col1 = columns[at], columns[at + 1]
            a, b, c, d = col0[k:k + 1], col1[k:k + 1], col0[k + 1:k + 2], col1[k + 1:k + 2]
            inverse = 1.0 / (a * d - b * c)

            def step(value):
                row0, row1 = value[k:k + 1], value[k + 1:k + 2]
                scaled0 = (row0 * d - row1 * b) * inverse
                scaled1 = (row1 * a - row0 * c) * inverse
                other = value - (col0 * scaled0 + col1 * scaled1)
                if upward:
                    return jnp.where(row_at == k, scaled0, jnp.where(row_at == k + 1, scaled1, other))
                inner = row1 - row0 * (c / a)
                return jnp.where(row_at > k + 1, other, jnp.where(row_at == k + 1, inner, value))

            table = step(table)
            for later in range(at + 2, 8):
                columns[later] = step(columns[later])
    return table


def unit_pivots(done):
    row_at = lax.broadcasted_iota(jnp.int32, (WINDOW, WINDOW), 0)
    col_at = lax.broadcasted_iota(jnp.int32, (WINDOW, WINDOW), 1)
    pivots = jnp.sum(jnp.where(row_at == col_at, done[:, :WINDOW], 0.0), axis=1, keepdims=True)
    return done * (1.0 / jnp.sqrt(pivots))


def eye(n):
    return (lax.broadcasted_iota(jnp.int32, (n, n), 0) == lax.broadcasted_iota(jnp.int32, (n, n), 1)).astype(f32)


def small_algebra(small):
    ident = eye(WINDOW)
    raw = small[0:32, 0:32]
    transform = small[0:32, 32:64]
    projected = 0.5 * (raw + raw.T)
    drive = small[0:32, 64:72]
    sense = small[0:32, 72:80]
    gram = small[32:64, 0:32]
    shifted = sweep(jnp.concatenate([ident - projected, ident, jnp.zeros((WINDOW, 64), f32)], axis=1), WINDOW, True)
    inv_n = shifted[:, 32:64]
    drive_t, sense_t = drive.T, sense.T
    hd = dot3(inv_n, drive)
    hd_t = hd.T
    sense_h = dot3(sense_t, inv_n)
    sense_hd = dot3(sense_t, hd)
    chain = None
    for iteration in range(KLEIN):
        if chain is None:
            einv_t = -inv_n
            chain = -sense_h
        else:
            q_t = 2.0 * dot3(dot3(drive_t, chain, ((1,), (1,))), chain)
            hq_t = dot3(q_t, inv_n)
            q_hd = dot3(q_t, hd)
            small = eye(CONTROLS) + dot3(hd_t, q_t, ((1,), (1,)))
            normal = dot3(small, small, ((1,), (1,)))
            table = jnp.concatenate([normal, dot3(small, hq_t), jnp.zeros((CONTROLS, 88), f32)], axis=1)
            solved = sweep(table, CONTROLS, True)[:, CONTROLS:CONTROLS + WINDOW]
            einv_t = dot3(hd, solved) - inv_n
            chain = dot3(jnp.concatenate([sense_hd, q_hd], axis=0), solved) - jnp.concatenate([sense_h, hq_t], axis=0)
        cayley_t = ident + 2.0 * einv_t
        for doubling in range(SMITH):
            chain = jnp.concatenate([chain, dot3(chain, cayley_t)], axis=0)
            if doubling < SMITH - 1:
                cayley_t = dot3(cayley_t, cayley_t)
    halves = [chain[:128].T, chain[128:].T]
    riccati = 2.0 * (dot3(halves[0], halves[0], ((1,), (1,))) + dot3(halves[1], halves[1], ((1,), (1,))))
    both = dot(riccati, jnp.concatenate([transform, dot(projected, transform)], axis=1))
    return both[:, :32], both[:, 32:], riccati, gram


def output_kernel(small_ref, w_hbm, aw_hbm, rot_hbm, res_hbm, ric_ref, gram_ref,
                  wbuf, awbuf, rot, res, coef, tmp, in_sem, out_sem):
    loads = [pltpu.make_async_copy(w_hbm, wbuf, in_sem.at[0]), pltpu.make_async_copy(aw_hbm, awbuf, in_sem.at[1])]
    for load in loads:
        load.start()
    rotate, remain, riccati, gram = small_algebra(small_ref[...])
    ric_ref[...] = riccati
    gram_ref[...] = gram
    r0, r1, r2 = pieces(rotate, 3)
    m0, m1, m2 = pieces(-remain, 3)
    zero = jnp.zeros((WINDOW, WINDOW), bf16)
    cat = lambda *blocks: jnp.concatenate(blocks, axis=1)
    coef[...] = jnp.concatenate([
        cat(r0, zero, zero, zero, r2, zero), cat(m0, r0, r0, r0, m2, r2),
        cat(r1, zero, zero, zero, zero, zero), cat(m1, r1, r1, zero, zero, zero)], axis=0)
    for load in loads:
        load.wait()

    def plane(x, carry):
        for y in range(NY_LOC):
            w, parts = wbuf[x, y], awbuf[x, y]
            out = bdot(coef[...], jnp.concatenate([w, parts, w, parts[0:32]], axis=0))
            tmp[y] = (out[0:64] + out[64:128]).astype(bf16)
        rot[x] = jnp.swapaxes(tmp[:, 0:32, :], 0, 1)
        res[x] = jnp.swapaxes(tmp[:, 32:64, :], 0, 1)
        pltpu.make_async_copy(rot.at[x], rot_hbm.at[:, x], out_sem.at[0]).start()
        pltpu.make_async_copy(res.at[x], res_hbm.at[:, x], out_sem.at[1]).start()
        return carry

    lax.fori_loop(0, NX_LOC, plane, 0)
    pltpu.make_async_copy(rot, rot, out_sem.at[0]).wait()
    pltpu.make_async_copy(res, res, out_sem.at[1]).wait()


def outputs(small, w_t, aw):
    field = (WINDOW, NX_LOC, NY_LOC, NZ)
    vmem, hbm = pl.BlockSpec(memory_space=pltpu.VMEM), pl.BlockSpec(memory_space=pltpu.HBM)
    return pl.pallas_call(
        output_kernel,
        out_shape=(jax.ShapeDtypeStruct(field, bf16), jax.ShapeDtypeStruct(field, bf16),
                   jax.ShapeDtypeStruct((WINDOW, WINDOW), f32), jax.ShapeDtypeStruct((WINDOW, WINDOW), f32)),
        in_specs=[vmem, hbm, hbm],
        out_specs=(hbm, hbm, vmem, vmem),
        scratch_shapes=[
            pltpu.VMEM((NX_LOC, NY_LOC, WINDOW, NZ), bf16), pltpu.VMEM((NX_LOC, NY_LOC, 96, NZ), bf16),
            pltpu.VMEM((NX_LOC, WINDOW, NY_LOC, NZ), bf16), pltpu.VMEM((NX_LOC, WINDOW, NY_LOC, NZ), bf16),
            pltpu.VMEM((128, 192), bf16), pltpu.VMEM((NY_LOC, 64, NZ), bf16),
            pltpu.SemaphoreType.DMA((2,)), pltpu.SemaphoreType.DMA((2,)),
        ],
        compiler_params=pltpu.CompilerParams(vmem_limit_bytes=60 << 20),
        name="algebra_outputs",
    )(small, w_t, aw)


def local(factor, offset, diagonal, actuators, sensors):
    small, w_t, aw = stats(offset, factor, diagonal, actuators, sensors)
    return outputs(small, w_t, aw)


def solution(mesh):
    return jax.shard_map(
        local,
        mesh=mesh,
        in_specs=(P(None, "gx", "gy", None), P(), P("gx", "gy", None), P(None, "gx", "gy", None), P(None, "gx", "gy", None)),
        out_specs=(P(None, "gx", "gy", None), P(None, "gx", "gy", None), P(), P()),
        check_vma=False,
    )
```

```python
import functools
import jax
import jax.numpy as jnp
from jax import lax
from jax.experimental import pallas as pl
from jax.experimental.pallas import tpu as pltpu
from jax.sharding import PartitionSpec as P

WINDOW = 32
KLEIN = 3
SMITH = 4
CONTROLS = 8
NX_LOC, NY_LOC, NZ = 8, 16, 256
CELLS = 256 * 128 * 256
MESH = pl.DeviceIdType.MESH
f32, bf16 = jnp.float32, jnp.bfloat16
HIGHEST = lax.Precision.HIGHEST


def dot(left, right, dims=((1,), (0,))):
    return lax.dot_general(left, right, (dims, ((), ())), precision=HIGHEST, preferred_element_type=f32)


def bdot(left, right, dims=((1,), (0,))):
    return lax.dot_general(left, right, (dims, ((), ())), preferred_element_type=f32)


def dot3(left, right, dims=((1,), (0,))):
    left_hi, left_lo = pieces(left, 2)
    right_hi, right_lo = pieces(right, 2)
    return bdot(left_hi, right_hi, dims) + (bdot(left_hi, right_lo, dims) + bdot(left_lo, right_hi, dims))


def pieces(value, count):
    out = []
    rest = value
    for at in range(count):
        piece = rest.astype(bf16)
        out.append(piece)
        if at < count - 1:
            rest = rest - piece.astype(f32)
    return out


def peer_groups():
    gx = lax.axis_index("gx")
    z = lax.axis_index("gy")
    xy = gx // 2
    core = gx % 2
    x, y = xy // 4, xy % 4
    plane = sorted(((dx, dy) for dx in range(4) for dy in range(4) if dx or dy),
                   key=lambda d: -(min(d[0], 4 - d[0]) + min(d[1], 4 - d[1])))
    return (
        (2, core, [(xy * 2 + (core + 1) % 2, z)]),
        (16, xy, [((((x + dx) % 4) * 4 + (y + dy) % 4) * 2 + core, z) for dx, dy in plane]),
        (8, z, [(gx, (z + dz) % 8) for dz in (4, 3, 5, 2, 6, 1, 7)]),
    )


def tree_sum(parts):
    while len(parts) > 1:
        parts = [parts[i] + parts[i + 1] for i in range(0, len(parts) - 1, 2)] + parts[len(parts) - len(parts) % 2:]
    return parts[0]


class Reduction:
    def __init__(self, bufs, s_sem, r_sem):
        self.bufs, self.s_sem, self.r_sem = bufs, s_sem, r_sem
        self.groups = peer_groups()

    def send(self, at, value):
        n, me, peers = self.groups[at]
        buf = self.bufs[at]
        buf[me] = value
        for peer in peers:
            pltpu.make_async_remote_copy(buf.at[me], buf.at[me], self.s_sem.at[at], self.r_sem.at[at],
                                         device_id=peer, device_id_type=MESH).start()

    def receive(self, at):
        n = self.groups[at][0]
        buf = self.bufs[at]
        span = buf.at[pl.ds(0, n - 1)]
        pltpu.make_async_copy(span, span, self.r_sem.at[at]).wait()
        return tree_sum([buf[j] for j in range(n)])

    def finish(self):
        for at, (n, me, peers) in enumerate(self.groups):
            span = self.bufs[at].at[pl.ds(0, n - 1)]
            pltpu.make_async_copy(span, span, self.s_sem.at[at]).wait()


def fold(rows):
    return jnp.concatenate([rows[8 * q:8 * q + 8] for q in range(4)], axis=1)


def unfold(block):
    return jnp.concatenate([block[:, 32 * q:32 * q + 32] for q in range(4)], axis=0)


def stats_kernel(off_ref, fac_hbm, diag_hbm, act_hbm, sen_hbm, small_ref, w_hbm, aw_hbm,
                 fac, diag_ref, io, wext, xhalo, yhalo, io_t, awbuf, g0, g1, g2, s0, s1, s2,
                 in_sem, hs_sem, hr_sem, gs_sem, gr_sem, ss_sem, sr_sem, out_sem):
    gx = lax.axis_index("gx")
    gz = lax.axis_index("gy")
    last = NX_LOC - 1
    third = 24
    loads = [pltpu.make_async_copy(fac_hbm.at[pl.ds(0, third)], fac.at[pl.ds(0, third)], in_sem.at[0]),
             pltpu.make_async_copy(fac_hbm.at[pl.ds(third, third)], fac.at[pl.ds(third, third)], in_sem.at[1]),
             pltpu.make_async_copy(fac_hbm.at[pl.ds(2 * third, 64 - 2 * third)], fac.at[pl.ds(2 * third, 64 - 2 * third)], in_sem.at[2]),
             pltpu.make_async_copy(act_hbm, io.at[pl.ds(0, CONTROLS)], in_sem.at[3]),
             pltpu.make_async_copy(sen_hbm, io.at[pl.ds(CONTROLS, CONTROLS)], in_sem.at[4]),
             pltpu.make_async_copy(diag_hbm, diag_ref, in_sem.at[5])]
    for load in loads:
        load.start()
    barrier = pltpu.get_barrier_semaphore()
    right, left = ((gx + 1) % 32, gz), ((gx + 31) % 32, gz)
    up, down = (gx, (gz + 1) % 8), (gx, (gz + 7) % 8)
    count = 0
    for n, me, peers in peer_groups():
        for peer in peers:
            pl.semaphore_signal(barrier, inc=1, device_id=peer, device_id_type=MESH)
            count += 1
    for target in (right, left):
        pl.semaphore_signal(barrier, inc=1, device_id=target, device_id_type=MESH)
        count += 1
    start = off_ref[0]
    inner_y = pl.ds(1, NY_LOC)
    inner_x = pl.ds(1, NX_LOC)
    side_x = jnp.zeros((NY_LOC + 2, WINDOW, NZ), bf16)
    side_y = jnp.zeros((NX_LOC + 2, WINDOW, NZ), bf16)
    wext[0] = side_x
    wext[NX_LOC + 1] = side_x
    wext[:, 0] = side_y
    wext[:, NY_LOC + 1] = side_y

    def turned(plane):
        return jnp.swapaxes(plane, 0, 1)

    for load in loads[:3]:
        load.wait()

    def turn(x, carry):
        wext[x + 1, inner_y] = turned(fac[pl.ds(start, WINDOW), x])
        return carry

    lax.fori_loop(0, NX_LOC, turn, 0)
    pl.semaphore_wait(barrier, count)
    moves = (
        (wext.at[NX_LOC, inner_y], xhalo.at[0], right),
        (wext.at[1, inner_y], xhalo.at[1], left),
        (wext.at[inner_x, NY_LOC], yhalo.at[0], up),
        (wext.at[inner_x, 1], yhalo.at[1], down),
    )
    copies = [pltpu.make_async_remote_copy(source, target, hs_sem.at[at], hr_sem.at[at], device_id=who, device_id_type=MESH)
              for at, (source, target, who) in enumerate(moves)]
    for copy in copies:
        copy.start()

    def gram_plane(x, total):
        part = jnp.zeros((WINDOW, WINDOW), f32)
        for y in range(NY_LOC):
            rows = wext[x + 1, y + 1]
            part = part + bdot(rows, rows, ((1,), (1,)))
        return total + part

    gram_local = lax.fori_loop(0, NX_LOC, gram_plane, jnp.zeros((WINDOW, WINDOW), f32)) * (1.0 / CELLS)
    gram_sum = Reduction((g0, g1, g2), gs_sem, gr_sem)
    cross_sum = Reduction((s0, s1, s2), ss_sem, sr_sem)
    gram_sum.send(0, fold(gram_local))
    w_write = pltpu.make_async_copy(wext.at[inner_x, inner_y], w_hbm, out_sem.at[0])
    w_write.start()
    for load in loads[3:]:
        load.wait()

    def turn_io(x, carry):
        io_t[x] = turned(io[:, x])
        return carry

    lax.fori_loop(0, NX_LOC, turn_io, 0)
    gram_sum.send(1, gram_sum.receive(0))

    lane = lax.broadcasted_iota(jnp.int32, (WINDOW, NZ), 1)

    def inside_plane(x, total):
        part = jnp.zeros((112, WINDOW), f32)
        rows = [wext[x + 1, 0].astype(f32), wext[x + 1, 1].astype(f32)]
        for y in range(NY_LOC):
            rows.append(wext[x + 1, y + 2].astype(f32))
            w16 = wext[x + 1, y + 1]
            w = rows[y + 1]
            beside = wext[x + 2, y + 1].astype(f32) + wext[x, y + 1].astype(f32)
            beside = beside + rows[y + 2] + rows[y]
            beside = beside + jnp.where(lane == NZ - 1, 0.0, pltpu.roll(w16, NZ - 1, 1).astype(f32))
            beside = beside + jnp.where(lane == 0, 0.0, pltpu.roll(w16, 1, 1).astype(f32))
            image = beside - (6.0 + diag_ref[x, y:y + 1, :]) * w
            parts = jnp.concatenate(pieces(image, 3), axis=0)
            awbuf[x, y] = parts
            part = part + bdot(jnp.concatenate([parts, io_t[x, y]], axis=0), w16, ((1,), (1,)))
        return total + part

    total = lax.fori_loop(0, NX_LOC, inside_plane, jnp.zeros((112, WINDOW), f32))
    cross = total[0:32] + (total[32:64] + total[64:96])
    for copy in copies:
        copy.wait()

    for edge, halo in ((gx == 0, xhalo.at[0]), (gx == 31, xhalo.at[1]), (gz == 0, yhalo.at[0]), (gz == 7, yhalo.at[1])):
        @pl.when(edge)
        def _(halo=halo):
            halo[...] = jnp.zeros_like(halo)

    for y in range(NY_LOC):
        cross = cross + bdot(xhalo[0, y], wext[1, y + 1], ((1,), (1,)))
        cross = cross + bdot(xhalo[1, y], wext[NX_LOC, y + 1], ((1,), (1,)))
    for x in range(NX_LOC):
        cross = cross + bdot(yhalo[0, x], wext[x + 1, 1], ((1,), (1,)))
        cross = cross + bdot(yhalo[1, x], wext[x + 1, NY_LOC], ((1,), (1,)))
    io_part = total[96:112]
    io_fold = jnp.concatenate([io_part[4 * q:4 * q + 4] for q in range(4)], axis=1)
    cross_sum.send(0, jnp.concatenate([fold(cross), io_fold], axis=0) * (1.0 / CELLS))

    cross_sum.send(1, cross_sum.receive(0))
    gram_sum.send(2, gram_sum.receive(1))
    def add_layer(x, y, halo):
        parts = awbuf[x, y].astype(f32)
        image = parts[0:32] + (parts[32:64] + parts[64:96]) + halo.astype(f32)
        awbuf[x, y] = jnp.concatenate(pieces(image, 3), axis=0)

    for y in range(NY_LOC):
        add_layer(0, y, xhalo[0, y])
        add_layer(last, y, xhalo[1, y])
    for x in range(NX_LOC):
        add_layer(x, 0, yhalo[0, x])
        add_layer(x, NY_LOC - 1, yhalo[1, x])
    aw_write = pltpu.make_async_copy(awbuf, aw_hbm, out_sem.at[1])
    aw_write.start()
    cross_sum.send(2, cross_sum.receive(1))
    gram = unfold(gram_sum.receive(2))
    ident = eye(WINDOW)
    table = jnp.concatenate([gram, ident, jnp.zeros((WINDOW, 64), f32)], axis=1)
    inverse_first = unit_pivots(sweep(table, WINDOW, False))[:, 32:64]
    gram_second = dot(dot(inverse_first, gram), inverse_first, ((1,), (1,)))
    table = jnp.concatenate([gram_second, ident, jnp.zeros((WINDOW, 64), f32)], axis=1)
    inverse_second = unit_pivots(sweep(table, WINDOW, False))[:, 32:64]
    transform = dot(inverse_second, inverse_first)
    received = cross_sum.receive(2)
    cross = unfold(received[0:8])
    io_rows = jnp.concatenate([received[8:12, 32 * q:32 * q + 32] for q in range(4)], axis=0)
    raw = dot(dot(transform, cross), transform, ((1,), (1,)))
    io_basis = dot(transform, io_rows, ((1,), (1,)))
    small_ref[0:32] = jnp.concatenate([raw, transform, io_basis, jnp.zeros((WINDOW, 48), f32)], axis=1)
    small_ref[32:64] = jnp.concatenate([gram, jnp.zeros((WINDOW, 96), f32)], axis=1)
    gram_sum.finish()
    cross_sum.finish()
    w_write.wait()
    aw_write.wait()


def stats(offset, factor, diagonal, actuators, sensors):
    vmem, anywhere = pl.BlockSpec(memory_space=pltpu.VMEM), pl.BlockSpec(memory_space=pltpu.HBM)
    dma = pltpu.SemaphoreType.DMA
    return pl.pallas_call(
        stats_kernel,
        out_shape=(jax.ShapeDtypeStruct((64, 128), f32),
                   jax.ShapeDtypeStruct((NX_LOC, NY_LOC, WINDOW, NZ), bf16),
                   jax.ShapeDtypeStruct((NX_LOC, NY_LOC, 96, NZ), bf16)),
        in_specs=[pl.BlockSpec(memory_space=pltpu.SMEM), anywhere, anywhere, anywhere, anywhere],
        out_specs=(vmem, anywhere, anywhere),
        scratch_shapes=[
            pltpu.VMEM((64, NX_LOC, NY_LOC, NZ), bf16),
            pltpu.VMEM((NX_LOC, NY_LOC, NZ), f32),
            pltpu.VMEM((2 * CONTROLS, NX_LOC, NY_LOC, NZ), bf16),
            pltpu.VMEM((NX_LOC + 2, NY_LOC + 2, WINDOW, NZ), bf16),
            pltpu.VMEM((2, NY_LOC, WINDOW, NZ), bf16), pltpu.VMEM((2, NX_LOC, WINDOW, NZ), bf16),
            pltpu.VMEM((NX_LOC, NY_LOC, 2 * CONTROLS, NZ), bf16),
            pltpu.VMEM((NX_LOC, NY_LOC, 96, NZ), bf16),
            pltpu.VMEM((2, 8, 128), f32), pltpu.VMEM((16, 8, 128), f32), pltpu.VMEM((8, 8, 128), f32),
            pltpu.VMEM((2, 12, 128), f32), pltpu.VMEM((16, 12, 128), f32), pltpu.VMEM((8, 12, 128), f32),
            dma((6,)), dma((4,)), dma((4,)), dma((3,)), dma((3,)), dma((3,)), dma((3,)), dma((2,)),
        ],
        compiler_params=pltpu.CompilerParams(collective_id=0, has_side_effects=True, vmem_limit_bytes=60 << 20),
        name="stats_all_reduce",
    )(offset, factor, diagonal, actuators, sensors)


def sweep(table, count, upward):
    row_at = lax.broadcasted_iota(jnp.int32, table.shape, 0)
    for start in range(0, count, 8):
        columns = [jnp.broadcast_to(table[:, k:k + 1], table.shape) for k in range(start, start + 8)]
        for at in range(0, 8, 2):
            k = start + at
            col0, col1 = columns[at], columns[at + 1]
            a, b, c, d = col0[k:k + 1], col1[k:k + 1], col0[k + 1:k + 2], col1[k + 1:k + 2]
            inverse = 1.0 / (a * d - b * c)

            def step(value):
                row0, row1 = value[k:k + 1], value[k + 1:k + 2]
                scaled0 = (row0 * d - row1 * b) * inverse
                scaled1 = (row1 * a - row0 * c) * inverse
                other = value - (col0 * scaled0 + col1 * scaled1)
                if upward:
                    return jnp.where(row_at == k, scaled0, jnp.where(row_at == k + 1, scaled1, other))
                inner = row1 - row0 * (c / a)
                return jnp.where(row_at > k + 1, other, jnp.where(row_at == k + 1, inner, value))

            table = step(table)
            for later in range(at + 2, 8):
                columns[later] = step(columns[later])
    return table


def unit_pivots(done):
    row_at = lax.broadcasted_iota(jnp.int32, (WINDOW, WINDOW), 0)
    col_at = lax.broadcasted_iota(jnp.int32, (WINDOW, WINDOW), 1)
    pivots = jnp.sum(jnp.where(row_at == col_at, done[:, :WINDOW], 0.0), axis=1, keepdims=True)
    return done * (1.0 / jnp.sqrt(pivots))


def eye(n):
    return (lax.broadcasted_iota(jnp.int32, (n, n), 0) == lax.broadcasted_iota(jnp.int32, (n, n), 1)).astype(f32)


def small_algebra(small):
    ident = eye(WINDOW)
    raw = small[0:32, 0:32]
    transform = small[0:32, 32:64]
    projected = 0.5 * (raw + raw.T)
    drive = small[0:32, 64:72]
    sense = small[0:32, 72:80]
    gram = small[32:64, 0:32]
    shifted = sweep(jnp.concatenate([ident - projected, ident, jnp.zeros((WINDOW, 64), f32)], axis=1), WINDOW, True)
    inv_n = shifted[:, 32:64]
    drive_t, sense_t = drive.T, sense.T
    hd = dot3(inv_n, drive)
    hd_t = hd.T
    sense_h = dot3(sense_t, inv_n)
    sense_hd = dot3(sense_t, hd)
    chain = None
    for iteration in range(KLEIN):
        if chain is None:
            einv_t = -inv_n
            chain = -sense_h
        else:
            q_t = 2.0 * dot3(dot3(drive_t, chain, ((1,), (1,))), chain)
            hq_t = dot3(q_t, inv_n)
            q_hd = dot3(q_t, hd)
            small = eye(CONTROLS) + dot3(hd_t, q_t, ((1,), (1,)))
            normal = dot3(small, small, ((1,), (1,)))
            table = jnp.concatenate([normal, dot3(small, hq_t), jnp.zeros((CONTROLS, 88), f32)], axis=1)
            solved = sweep(table, CONTROLS, True)[:, CONTROLS:CONTROLS + WINDOW]
            einv_t = dot3(hd, solved) - inv_n
            chain = dot3(jnp.concatenate([sense_hd, q_hd], axis=0), solved) - jnp.concatenate([sense_h, hq_t], axis=0)
        cayley_t = ident + 2.0 * einv_t
        for doubling in range(SMITH):
            chain = jnp.concatenate([chain, dot3(chain, cayley_t)], axis=0)
            if doubling < SMITH - 1:
                cayley_t = dot3(cayley_t, cayley_t)
    halves = [chain[:128].T, chain[128:].T]
    riccati = 2.0 * (dot3(halves[0], halves[0], ((1,), (1,))) + dot3(halves[1], halves[1], ((1,), (1,))))
    both = dot(riccati, jnp.concatenate([transform, dot(projected, transform)], axis=1))
    return both[:, :32], both[:, 32:], riccati, gram


def output_kernel(small_ref, w_hbm, aw_hbm, rot_hbm, res_hbm, ric_ref, gram_ref,
                  wbuf, awbuf, rot, res, coef, tmp, in_sem, out_sem):
    loads = [pltpu.make_async_copy(w_hbm, wbuf, in_sem.at[0]), pltpu.make_async_copy(aw_hbm, awbuf, in_sem.at[1])]
    for load in loads:
        load.start()
    rotate, remain, riccati, gram = small_algebra(small_ref[...])
    ric_ref[...] = riccati
    gram_ref[...] = gram
    r0, r1, r2 = pieces(rotate, 3)
    m0, m1, m2 = pieces(-remain, 3)
    zero = jnp.zeros((WINDOW, WINDOW), bf16)
    cat = lambda *blocks: jnp.concatenate(blocks, axis=1)
    coef[...] = jnp.concatenate([
        cat(r0, zero, zero, zero, r2, zero), cat(m0, r0, r0, r0, m2, r2),
        cat(r1, zero, zero, zero, zero, zero), cat(m1, r1, r1, zero, zero, zero)], axis=0)
    for load in loads:
        load.wait()

    def plane(x, carry):
        for y in range(NY_LOC):
            w, parts = wbuf[x, y], awbuf[x, y]
            out = bdot(coef[...], jnp.concatenate([w, parts, w, parts[0:32]], axis=0))
            tmp[y] = (out[0:64] + out[64:128]).astype(bf16)
        rot[x] = jnp.swapaxes(tmp[:, 0:32, :], 0, 1)
        res[x] = jnp.swapaxes(tmp[:, 32:64, :], 0, 1)
        pltpu.make_async_copy(rot.at[x], rot_hbm.at[:, x], out_sem.at[0]).start()
        pltpu.make_async_copy(res.at[x], res_hbm.at[:, x], out_sem.at[1]).start()
        return carry

    lax.fori_loop(0, NX_LOC, plane, 0)
    pltpu.make_async_copy(rot, rot, out_sem.at[0]).wait()
    pltpu.make_async_copy(res, res, out_sem.at[1]).wait()


def outputs(small, w_t, aw):
    field = (WINDOW, NX_LOC, NY_LOC, NZ)
    vmem, hbm = pl.BlockSpec(memory_space=pltpu.VMEM), pl.BlockSpec(memory_space=pltpu.HBM)
    return pl.pallas_call(
        output_kernel,
        out_shape=(jax.ShapeDtypeStruct(field, bf16), jax.ShapeDtypeStruct(field, bf16),
                   jax.ShapeDtypeStruct((WINDOW, WINDOW), f32), jax.ShapeDtypeStruct((WINDOW, WINDOW), f32)),
        in_specs=[vmem, hbm, hbm],
        out_specs=(hbm, hbm, vmem, vmem),
        scratch_shapes=[
            pltpu.VMEM((NX_LOC, NY_LOC, WINDOW, NZ), bf16), pltpu.VMEM((NX_LOC, NY_LOC, 96, NZ), bf16),
            pltpu.VMEM((NX_LOC, WINDOW, NY_LOC, NZ), bf16), pltpu.VMEM((NX_LOC, WINDOW, NY_LOC, NZ), bf16),
            pltpu.VMEM((128, 192), bf16), pltpu.VMEM((NY_LOC, 64, NZ), bf16),
            pltpu.SemaphoreType.DMA((2,)), pltpu.SemaphoreType.DMA((2,)),
        ],
        compiler_params=pltpu.CompilerParams(vmem_limit_bytes=60 << 20),
        name="algebra_outputs",
    )(small, w_t, aw)


def local(factor, offset, diagonal, actuators, sensors):
    small, w_t, aw = stats(offset, factor, diagonal, actuators, sensors)
    return outputs(small, w_t, aw)


def solution(mesh):
    return jax.shard_map(
        local,
        mesh=mesh,
        in_specs=(P(None, "gx", "gy", None), P(), P("gx", "gy", None), P(None, "gx", "gy", None), P(None, "gx", "gy", None)),
        out_specs=(P(None, "gx", "gy", None), P(None, "gx", "gy", None), P(), P()),
        check_vma=False,
    )
```

```python
import functools
import jax
import jax.numpy as jnp
from jax import lax
from jax.experimental import pallas as pl
from jax.experimental.pallas import tpu as pltpu
from jax.sharding import PartitionSpec as P

WINDOW = 32
KLEIN = 3
SMITH = 4
CONTROLS = 8
NX_LOC, NY_LOC, NZ = 8, 16, 256
CELLS = 256 * 128 * 256
MESH = pl.DeviceIdType.MESH
f32, bf16 = jnp.float32, jnp.bfloat16
HIGHEST = lax.Precision.HIGHEST


def dot(left, right, dims=((1,), (0,))):
    return lax.dot_general(left, right, (dims, ((), ())), precision=HIGHEST, preferred_element_type=f32)


def bdot(left, right, dims=((1,), (0,))):
    return lax.dot_general(left, right, (dims, ((), ())), preferred_element_type=f32)


def dot3(left, right, dims=((1,), (0,))):
    left_hi, left_lo = pieces(left, 2)
    right_hi, right_lo = pieces(right, 2)
    return bdot(left_hi, right_hi, dims) + (bdot(left_hi, right_lo, dims) + bdot(left_lo, right_hi, dims))


def pieces(value, count):
    out = []
    rest = value
    for at in range(count):
        piece = rest.astype(bf16)
        out.append(piece)
        if at < count - 1:
            rest = rest - piece.astype(f32)
    return out


def peer_groups():
    gx = lax.axis_index("gx")
    z = lax.axis_index("gy")
    xy = gx // 2
    core = gx % 2
    x, y = xy // 4, xy % 4
    plane = sorted(((dx, dy) for dx in range(4) for dy in range(4) if dx or dy),
                   key=lambda d: -(min(d[0], 4 - d[0]) + min(d[1], 4 - d[1])))
    return (
        (2, core, [(xy * 2 + (core + 1) % 2, z)]),
        (16, xy, [((((x + dx) % 4) * 4 + (y + dy) % 4) * 2 + core, z) for dx, dy in plane]),
        (8, z, [(gx, (z + dz) % 8) for dz in (4, 3, 5, 2, 6, 1, 7)]),
    )


def tree_sum(parts):
    while len(parts) > 1:
        parts = [parts[i] + parts[i + 1] for i in range(0, len(parts) - 1, 2)] + parts[len(parts) - len(parts) % 2:]
    return parts[0]


class Reduction:
    def __init__(self, bufs, s_sem, r_sem):
        self.bufs, self.s_sem, self.r_sem = bufs, s_sem, r_sem
        self.groups = peer_groups()

    def send(self, at, value):
        n, me, peers = self.groups[at]
        buf = self.bufs[at]
        buf[me] = value
        for peer in peers:
            pltpu.make_async_remote_copy(buf.at[me], buf.at[me], self.s_sem.at[at], self.r_sem.at[at],
                                         device_id=peer, device_id_type=MESH).start()

    def receive(self, at):
        n = self.groups[at][0]
        buf = self.bufs[at]
        span = buf.at[pl.ds(0, n - 1)]
        pltpu.make_async_copy(span, span, self.r_sem.at[at]).wait()
        return tree_sum([buf[j] for j in range(n)])

    def finish(self):
        for at, (n, me, peers) in enumerate(self.groups):
            span = self.bufs[at].at[pl.ds(0, n - 1)]
            pltpu.make_async_copy(span, span, self.s_sem.at[at]).wait()


def fold(rows):
    return jnp.concatenate([rows[8 * q:8 * q + 8] for q in range(4)], axis=1)


def unfold(block):
    return jnp.concatenate([block[:, 32 * q:32 * q + 32] for q in range(4)], axis=0)


def stats_kernel(off_ref, fac_hbm, diag_hbm, act_hbm, sen_hbm, small_ref, w_hbm, aw_hbm,
                 fac_ends, fac_mid, diag_ref, io, wext, xhalo, yhalo, io_t, awbuf, g0, g1, g2, s0, s1, s2,
                 in_sem, hs_sem, hr_sem, gs_sem, gr_sem, ss_sem, sr_sem, out_sem):
    gx = lax.axis_index("gx")
    gz = lax.axis_index("gy")
    last = NX_LOC - 1
    loads = [pltpu.make_async_copy(fac_hbm.at[:, 0], fac_ends.at[0], in_sem.at[0]),
             pltpu.make_async_copy(fac_hbm.at[:, last], fac_ends.at[1], in_sem.at[1]),
             pltpu.make_async_copy(fac_hbm.at[:, pl.ds(1, NX_LOC - 2)], fac_mid, in_sem.at[2]),
             pltpu.make_async_copy(act_hbm, io.at[pl.ds(0, CONTROLS)], in_sem.at[3]),
             pltpu.make_async_copy(sen_hbm, io.at[pl.ds(CONTROLS, CONTROLS)], in_sem.at[4]),
             pltpu.make_async_copy(diag_hbm, diag_ref, in_sem.at[5])]
    barrier = pltpu.get_barrier_semaphore()
    right, left = ((gx + 1) % 32, gz), ((gx + 31) % 32, gz)
    up, down = (gx, (gz + 1) % 8), (gx, (gz + 7) % 8)
    count = 0
    for n, me, peers in peer_groups():
        for peer in peers:
            pl.semaphore_signal(barrier, inc=1, device_id=peer, device_id_type=MESH)
            count += 1
    for target in (right, left):
        pl.semaphore_signal(barrier, inc=1, device_id=target, device_id_type=MESH)
        count += 1
    for load in loads:
        load.start()
    start = off_ref[0]
    inner_y = pl.ds(1, NY_LOC)
    inner_x = pl.ds(1, NX_LOC)
    side_x = jnp.zeros((NY_LOC + 2, WINDOW, NZ), bf16)
    side_y = jnp.zeros((NX_LOC + 2, WINDOW, NZ), bf16)
    wext[0] = side_x
    wext[NX_LOC + 1] = side_x
    wext[:, 0] = side_y
    wext[:, NY_LOC + 1] = side_y

    def turned(plane):
        return jnp.swapaxes(plane, 0, 1)

    loads[0].wait()
    loads[1].wait()
    wext[1, inner_y] = turned(fac_ends[0, pl.ds(start, WINDOW)])
    wext[NX_LOC, inner_y] = turned(fac_ends[1, pl.ds(start, WINDOW)])
    loads[2].wait()

    def turn(x, carry):
        wext[x + 2, inner_y] = turned(fac_mid[pl.ds(start, WINDOW), x])
        return carry

    lax.fori_loop(0, NX_LOC - 2, turn, 0)
    pl.semaphore_wait(barrier, count)
    moves = (
        (wext.at[NX_LOC, inner_y], xhalo.at[0], right),
        (wext.at[1, inner_y], xhalo.at[1], left),
        (wext.at[inner_x, NY_LOC], yhalo.at[0], up),
        (wext.at[inner_x, 1], yhalo.at[1], down),
    )
    copies = [pltpu.make_async_remote_copy(source, target, hs_sem.at[at], hr_sem.at[at], device_id=who, device_id_type=MESH)
              for at, (source, target, who) in enumerate(moves)]
    for copy in copies:
        copy.start()

    def gram_plane(x, total):
        part = jnp.zeros((WINDOW, WINDOW), f32)
        for y in range(NY_LOC):
            rows = wext[x + 1, y + 1]
            part = part + bdot(rows, rows, ((1,), (1,)))
        return total + part

    gram_local = lax.fori_loop(0, NX_LOC, gram_plane, jnp.zeros((WINDOW, WINDOW), f32)) * (1.0 / CELLS)
    gram_sum = Reduction((g0, g1, g2), gs_sem, gr_sem)
    cross_sum = Reduction((s0, s1, s2), ss_sem, sr_sem)
    gram_sum.send(0, fold(gram_local))
    w_write = pltpu.make_async_copy(wext.at[inner_x, inner_y], w_hbm, out_sem.at[0])
    w_write.start()
    for load in loads[3:]:
        load.wait()

    def turn_io(x, carry):
        io_t[x] = turned(io[:, x])
        return carry

    lax.fori_loop(0, NX_LOC, turn_io, 0)
    gram_sum.send(1, gram_sum.receive(0))

    lane = lax.broadcasted_iota(jnp.int32, (WINDOW, NZ), 1)

    def inside_plane(x, total):
        part = jnp.zeros((112, WINDOW), f32)
        rows = [wext[x + 1, 0].astype(f32), wext[x + 1, 1].astype(f32)]
        for y in range(NY_LOC):
            rows.append(wext[x + 1, y + 2].astype(f32))
            w16 = wext[x + 1, y + 1]
            w = rows[y + 1]
            beside = wext[x + 2, y + 1].astype(f32) + wext[x, y + 1].astype(f32)
            beside = beside + rows[y + 2] + rows[y]
            beside = beside + jnp.where(lane == NZ - 1, 0.0, pltpu.roll(w16, NZ - 1, 1).astype(f32))
            beside = beside + jnp.where(lane == 0, 0.0, pltpu.roll(w16, 1, 1).astype(f32))
            image = beside - (6.0 + diag_ref[x, y:y + 1, :]) * w
            parts = jnp.concatenate(pieces(image, 3), axis=0)
            awbuf[x, y] = parts
            part = part + bdot(jnp.concatenate([parts, io_t[x, y]], axis=0), w16, ((1,), (1,)))
        return total + part

    total = lax.fori_loop(0, NX_LOC, inside_plane, jnp.zeros((112, WINDOW), f32))
    cross = total[0:32] + (total[32:64] + total[64:96])
    for copy in copies:
        copy.wait()

    for edge, halo in ((gx == 0, xhalo.at[0]), (gx == 31, xhalo.at[1]), (gz == 0, yhalo.at[0]), (gz == 7, yhalo.at[1])):
        @pl.when(edge)
        def _(halo=halo):
            halo[...] = jnp.zeros_like(halo)

    for y in range(NY_LOC):
        cross = cross + bdot(xhalo[0, y], wext[1, y + 1], ((1,), (1,)))
        cross = cross + bdot(xhalo[1, y], wext[NX_LOC, y + 1], ((1,), (1,)))
    for x in range(NX_LOC):
        cross = cross + bdot(yhalo[0, x], wext[x + 1, 1], ((1,), (1,)))
        cross = cross + bdot(yhalo[1, x], wext[x + 1, NY_LOC], ((1,), (1,)))
    io_part = total[96:112]
    io_fold = jnp.concatenate([io_part[4 * q:4 * q + 4] for q in range(4)], axis=1)
    cross_sum.send(0, jnp.concatenate([fold(cross), io_fold], axis=0) * (1.0 / CELLS))

    cross_sum.send(1, cross_sum.receive(0))
    gram_sum.send(2, gram_sum.receive(1))
    def add_layer(x, y, halo):
        parts = awbuf[x, y].astype(f32)
        image = parts[0:32] + (parts[32:64] + parts[64:96]) + halo.astype(f32)
        awbuf[x, y] = jnp.concatenate(pieces(image, 3), axis=0)

    for y in range(NY_LOC):
        add_layer(0, y, xhalo[0, y])
        add_layer(last, y, xhalo[1, y])
    for x in range(NX_LOC):
        add_layer(x, 0, yhalo[0, x])
        add_layer(x, NY_LOC - 1, yhalo[1, x])
    aw_write = pltpu.make_async_copy(awbuf, aw_hbm, out_sem.at[1])
    aw_write.start()
    cross_sum.send(2, cross_sum.receive(1))
    gram = unfold(gram_sum.receive(2))
    ident = eye(WINDOW)
    table = jnp.concatenate([gram, ident, jnp.zeros((WINDOW, 64), f32)], axis=1)
    inverse_first = unit_pivots(sweep(table, WINDOW, False))[:, 32:64]
    gram_second = dot(dot(inverse_first, gram), inverse_first, ((1,), (1,)))
    table = jnp.concatenate([gram_second, ident, jnp.zeros((WINDOW, 64), f32)], axis=1)
    inverse_second = unit_pivots(sweep(table, WINDOW, False))[:, 32:64]
    transform = dot(inverse_second, inverse_first)
    received = cross_sum.receive(2)
    cross = unfold(received[0:8])
    io_rows = jnp.concatenate([received[8:12, 32 * q:32 * q + 32] for q in range(4)], axis=0)
    raw = dot(dot(transform, cross), transform, ((1,), (1,)))
    io_basis = dot(transform, io_rows, ((1,), (1,)))
    small_ref[0:32] = jnp.concatenate([raw, transform, io_basis, jnp.zeros((WINDOW, 48), f32)], axis=1)
    small_ref[32:64] = jnp.concatenate([gram, jnp.zeros((WINDOW, 96), f32)], axis=1)
    gram_sum.finish()
    cross_sum.finish()
    w_write.wait()
    aw_write.wait()


def stats(offset, factor, diagonal, actuators, sensors):
    vmem, anywhere = pl.BlockSpec(memory_space=pltpu.VMEM), pl.BlockSpec(memory_space=pltpu.HBM)
    dma = pltpu.SemaphoreType.DMA
    return pl.pallas_call(
        stats_kernel,
        out_shape=(jax.ShapeDtypeStruct((64, 128), f32),
                   jax.ShapeDtypeStruct((NX_LOC, NY_LOC, WINDOW, NZ), bf16),
                   jax.ShapeDtypeStruct((NX_LOC, NY_LOC, 96, NZ), bf16)),
        in_specs=[pl.BlockSpec(memory_space=pltpu.SMEM), anywhere, anywhere, anywhere, anywhere],
        out_specs=(vmem, anywhere, anywhere),
        scratch_shapes=[
            pltpu.VMEM((2, 64, NY_LOC, NZ), bf16), pltpu.VMEM((64, NX_LOC - 2, NY_LOC, NZ), bf16),
            pltpu.VMEM((NX_LOC, NY_LOC, NZ), f32),
            pltpu.VMEM((2 * CONTROLS, NX_LOC, NY_LOC, NZ), bf16),
            pltpu.VMEM((NX_LOC + 2, NY_LOC + 2, WINDOW, NZ), bf16),
            pltpu.VMEM((2, NY_LOC, WINDOW, NZ), bf16), pltpu.VMEM((2, NX_LOC, WINDOW, NZ), bf16),
            pltpu.VMEM((NX_LOC, NY_LOC, 2 * CONTROLS, NZ), bf16),
            pltpu.VMEM((NX_LOC, NY_LOC, 96, NZ), bf16),
            pltpu.VMEM((2, 8, 128), f32), pltpu.VMEM((16, 8, 128), f32), pltpu.VMEM((8, 8, 128), f32),
            pltpu.VMEM((2, 12, 128), f32), pltpu.VMEM((16, 12, 128), f32), pltpu.VMEM((8, 12, 128), f32),
            dma((6,)), dma((4,)), dma((4,)), dma((3,)), dma((3,)), dma((3,)), dma((3,)), dma((2,)),
        ],
        compiler_params=pltpu.CompilerParams(collective_id=0, has_side_effects=True, vmem_limit_bytes=60 << 20),
        name="stats_all_reduce",
    )(offset, factor, diagonal, actuators, sensors)


def sweep(table, count, upward):
    row_at = lax.broadcasted_iota(jnp.int32, table.shape, 0)
    for start in range(0, count, 8):
        columns = [jnp.broadcast_to(table[:, k:k + 1], table.shape) for k in range(start, start + 8)]
        for at in range(0, 8, 2):
            k = start + at
            col0, col1 = columns[at], columns[at + 1]
            a, b, c, d = col0[k:k + 1], col1[k:k + 1], col0[k + 1:k + 2], col1[k + 1:k + 2]
            inverse = 1.0 / (a * d - b * c)

            def step(value):
                row0, row1 = value[k:k + 1], value[k + 1:k + 2]
                scaled0 = (row0 * d - row1 * b) * inverse
                scaled1 = (row1 * a - row0 * c) * inverse
                other = value - (col0 * scaled0 + col1 * scaled1)
                if upward:
                    return jnp.where(row_at == k, scaled0, jnp.where(row_at == k + 1, scaled1, other))
                inner = row1 - row0 * (c / a)
                return jnp.where(row_at > k + 1, other, jnp.where(row_at == k + 1, inner, value))

            table = step(table)
            for later in range(at + 2, 8):
                columns[later] = step(columns[later])
    return table


def unit_pivots(done):
    row_at = lax.broadcasted_iota(jnp.int32, (WINDOW, WINDOW), 0)
    col_at = lax.broadcasted_iota(jnp.int32, (WINDOW, WINDOW), 1)
    pivots = jnp.sum(jnp.where(row_at == col_at, done[:, :WINDOW], 0.0), axis=1, keepdims=True)
    return done * (1.0 / jnp.sqrt(pivots))


def eye(n):
    return (lax.broadcasted_iota(jnp.int32, (n, n), 0) == lax.broadcasted_iota(jnp.int32, (n, n), 1)).astype(f32)


def small_algebra(small):
    ident = eye(WINDOW)
    raw = small[0:32, 0:32]
    transform = small[0:32, 32:64]
    projected = 0.5 * (raw + raw.T)
    drive = small[0:32, 64:72]
    sense = small[0:32, 72:80]
    gram = small[32:64, 0:32]
    shifted = sweep(jnp.concatenate([ident - projected, ident, jnp.zeros((WINDOW, 64), f32)], axis=1), WINDOW, True)
    inv_n = shifted[:, 32:64]
    drive_t, sense_t = drive.T, sense.T
    hd = dot3(inv_n, drive)
    hd_t = hd.T
    sense_h = dot3(sense_t, inv_n)
    sense_hd = dot3(sense_t, hd)
    chain = None
    for iteration in range(KLEIN):
        if chain is None:
            einv_t = -inv_n
            chain = -sense_h
        else:
            q_t = 2.0 * dot3(dot3(drive_t, chain, ((1,), (1,))), chain)
            hq_t = dot3(q_t, inv_n)
            q_hd = dot3(q_t, hd)
            small = eye(CONTROLS) + dot3(hd_t, q_t, ((1,), (1,)))
            normal = dot3(small, small, ((1,), (1,)))
            table = jnp.concatenate([normal, dot3(small, hq_t), jnp.zeros((CONTROLS, 88), f32)], axis=1)
            solved = sweep(table, CONTROLS, True)[:, CONTROLS:CONTROLS + WINDOW]
            einv_t = dot3(hd, solved) - inv_n
            chain = dot3(jnp.concatenate([sense_hd, q_hd], axis=0), solved) - jnp.concatenate([sense_h, hq_t], axis=0)
        cayley_t = ident + 2.0 * einv_t
        for doubling in range(SMITH):
            chain = jnp.concatenate([chain, dot3(chain, cayley_t)], axis=0)
            if doubling < SMITH - 1:
                cayley_t = dot3(cayley_t, cayley_t)
    halves = [chain[:128].T, chain[128:].T]
    riccati = 2.0 * (dot3(halves[0], halves[0], ((1,), (1,))) + dot3(halves[1], halves[1], ((1,), (1,))))
    both = dot(riccati, jnp.concatenate([transform, dot(projected, transform)], axis=1))
    return both[:, :32], both[:, 32:], riccati, gram


def output_kernel(small_ref, w_hbm, aw_hbm, rot_hbm, res_hbm, ric_ref, gram_ref,
                  wbuf, awbuf, rot, res, coef, tmp, in_sem, out_sem):
    loads = [pltpu.make_async_copy(w_hbm, wbuf, in_sem.at[0]), pltpu.make_async_copy(aw_hbm, awbuf, in_sem.at[1])]
    for load in loads:
        load.start()
    rotate, remain, riccati, gram = small_algebra(small_ref[...])
    ric_ref[...] = riccati
    gram_ref[...] = gram
    r0, r1, r2 = pieces(rotate, 3)
    m0, m1, m2 = pieces(-remain, 3)
    zero = jnp.zeros((WINDOW, WINDOW), bf16)
    cat = lambda *blocks: jnp.concatenate(blocks, axis=1)
    coef[...] = jnp.concatenate([
        cat(r0, zero, zero, zero, r2, zero), cat(m0, r0, r0, r0, m2, r2),
        cat(r1, zero, zero, zero, zero, zero), cat(m1, r1, r1, zero, zero, zero)], axis=0)
    for load in loads:
        load.wait()

    def plane(x, carry):
        for y in range(NY_LOC):
            w, parts = wbuf[x, y], awbuf[x, y]
            out = bdot(coef[...], jnp.concatenate([w, parts, w, parts[0:32]], axis=0))
            tmp[y] = (out[0:64] + out[64:128]).astype(bf16)
        rot[x] = jnp.swapaxes(tmp[:, 0:32, :], 0, 1)
        res[x] = jnp.swapaxes(tmp[:, 32:64, :], 0, 1)
        pltpu.make_async_copy(rot.at[x], rot_hbm.at[:, x], out_sem.at[0]).start()
        pltpu.make_async_copy(res.at[x], res_hbm.at[:, x], out_sem.at[1]).start()
        return carry

    lax.fori_loop(0, NX_LOC, plane, 0)
    pltpu.make_async_copy(rot, rot, out_sem.at[0]).wait()
    pltpu.make_async_copy(res, res, out_sem.at[1]).wait()


def outputs(small, w_t, aw):
    field = (WINDOW, NX_LOC, NY_LOC, NZ)
    vmem, hbm = pl.BlockSpec(memory_space=pltpu.VMEM), pl.BlockSpec(memory_space=pltpu.HBM)
    return pl.pallas_call(
        output_kernel,
        out_shape=(jax.ShapeDtypeStruct(field, bf16), jax.ShapeDtypeStruct(field, bf16),
                   jax.ShapeDtypeStruct((WINDOW, WINDOW), f32), jax.ShapeDtypeStruct((WINDOW, WINDOW), f32)),
        in_specs=[vmem, hbm, hbm],
        out_specs=(hbm, hbm, vmem, vmem),
        scratch_shapes=[
            pltpu.VMEM((NX_LOC, NY_LOC, WINDOW, NZ), bf16), pltpu.VMEM((NX_LOC, NY_LOC, 96, NZ), bf16),
            pltpu.VMEM((NX_LOC, WINDOW, NY_LOC, NZ), bf16), pltpu.VMEM((NX_LOC, WINDOW, NY_LOC, NZ), bf16),
            pltpu.VMEM((128, 192), bf16), pltpu.VMEM((NY_LOC, 64, NZ), bf16),
            pltpu.SemaphoreType.DMA((2,)), pltpu.SemaphoreType.DMA((2,)),
        ],
        compiler_params=pltpu.CompilerParams(vmem_limit_bytes=60 << 20),
        name="algebra_outputs",
    )(small, w_t, aw)


def local(factor, offset, diagonal, actuators, sensors):
    small, w_t, aw = stats(offset, factor, diagonal, actuators, sensors)
    return outputs(small, w_t, aw)


def solution(mesh):
    return jax.shard_map(
        local,
        mesh=mesh,
        in_specs=(P(None, "gx", "gy", None), P(), P("gx", "gy", None), P(None, "gx", "gy", None), P(None, "gx", "gy", None)),
        out_specs=(P(None, "gx", "gy", None), P(None, "gx", "gy", None), P(), P()),
        check_vma=False,
    )
```
